32 devices in a mesh: seq: 8 (over z, x), panel: 4 (over y, core).
Axes of the slice: x: 2, y: 2, z: 4, core: 2. Of those that a mesh axis runs over, the one named last changes fastest.
Arguments:
- tokens: bfloat16 [512, 8192], P(('seq', 'panel')), may hold values from -6 to 6
- gate_weight: bfloat16 [2048, 8192], P(('seq', 'panel')), may hold values from -0.0625 to 0.0625
- up_weight: bfloat16 [2048, 8192], P(('seq', 'panel')), may hold values from -0.0625 to 0.0625
- gate_mask: int32 [32, 128], P(('seq', 'panel')), may hold values from 0 to 1, as said below
- up_mask: int32 [32, 128], P(('seq', 'panel')), may hold values from 0 to 1, as said below
Outputs:
- hidden: bfloat16 [512, 2048], P(('seq', 'panel'))
The draws below stay inside these ranges and needn't reach their ends.
Inputs may be any that keep to these rules, and one draw needn't show every extreme that they name: Every block row of gate_mask keeps between 32 and 96 of its 128 blocks; some block row keeps exactly 96. Every block row of up_mask keeps between 32 and 96 of its 128 blocks; some block row keeps exactly 96.
All inputs are finite; a program needn't handle non-finite values.
Results may differ from the reference program's by a relative error of at most 0.0012.
Values may be sent and summed in bfloat16 or wider, within the bound.
A program may use at most 128 MiB of HBM per device.

```python
import jax
import jax.numpy as jnp
from jax import lax

D = 8192
BLOCK = 64
FF = 2048
TOKENS = 512


def keep_blocks(key, row_blocks, col_blocks):
    key_count, key_top, key_rank = jax.random.split(key, 3)
    lowest = row_blocks // 4
    highest = 3 * row_blocks // 4
    counts = jax.random.randint(key_count, (col_blocks,), lowest, highest + 1)
    chosen = jax.random.randint(key_top, (), 0, col_blocks)
    counts = jnp.where(jnp.arange(col_blocks) == chosen, highest, counts)
    scores = jax.random.randint(key_rank, (row_blocks, col_blocks), 0, 1 << 20) * row_blocks + jnp.arange(row_blocks)[:, None]
    order = jnp.argsort(scores, axis=0, stable=True)
    ranks = jnp.argsort(order, axis=0, stable=True)
    return jnp.transpose((ranks < counts[None, :]).astype(jnp.int32))


def draw_gate_mask(key, part):
    return keep_blocks(jax.random.fold_in(key, 11), D // BLOCK, FF // BLOCK)


def draw_up_mask(key, part):
    return keep_blocks(jax.random.fold_in(key, 23), D // BLOCK, FF // BLOCK)


def block_scale(stream_key, shape, cuts, least, high):
    factor_of = 1.0
    for dim, shards_of in cuts:
        draws = jax.random.uniform(jax.random.fold_in(jax.random.fold_in(stream_key, 6), dim), (shards_of,), jnp.float32, least / len(cuts), high / len(cuts))
        factor_of = factor_of * jnp.repeat(jnp.exp(draws), shape[dim] // shards_of).reshape((-1,) + (1,) * (len(shape) - 1 - dim))
    return factor_of


def scatter_about(key, extent, deviation, limit, pieces=(), held_as=jnp.bfloat16):
    gain = block_scale(key, extent, pieces, -0.22, 0.18) if pieces else 1.0
    entries = jax.random.normal(key, extent, jnp.float32) * deviation * gain
    return jnp.minimum(jnp.maximum(entries, -limit), limit).astype(held_as)


def setup_inputs(seed: int = 0) -> dict:
    key_list = jax.random.split(jax.random.key(seed), 6)
    return {
        "tokens": scatter_about(key_list[0], (TOKENS, D), 1.0, 6.0, ((0, 32),)),
        "gate_weight": scatter_about(key_list[1], (FF, D), D ** -0.5, 0.0625, ((0, 32),)),
        "up_weight": scatter_about(key_list[2], (FF, D), D ** -0.5, 0.0625, ((0, 32),)),
        "gate_mask": draw_gate_mask(jax.random.fold_in(key_list[5], 71), 0),
        "up_mask": draw_up_mask(jax.random.fold_in(key_list[5], 71), 0),
    }


def expand_mask(mask, weight):
    block_rows = weight.shape[0] // mask.shape[0]
    block_cols = weight.shape[1] // mask.shape[1]
    full_mask = jnp.repeat(jnp.repeat(mask.astype(jnp.bfloat16), block_rows, axis=0), block_cols, axis=1)
    return weight * full_mask


def project(tokens, weight):
    return lax.dot_general(tokens, weight, (((1,), (1,)), ((), ())), preferred_element_type=jnp.float32)


def reference(tokens, gate_weight, up_weight, gate_mask, up_mask):
    gate = project(tokens, expand_mask(gate_mask, gate_weight))
    up_values = project(tokens, expand_mask(up_mask, up_weight))
    return (jax.nn.silu(gate) * up_values).astype(jnp.bfloat16)
```

```python
import functools

import jax
import jax.numpy as jnp
from jax import lax
from jax.experimental import pallas as pl
from jax.experimental.pallas import tpu as pltpu
from jax.sharding import PartitionSpec as P

MESH = pl.DeviceIdType.MESH
RIDING = 14
NZ = 4
L, LC, X, X2, Y, Y2, DA, DC, R, R2 = range(10)
NKINDS = 10


def passed_along(block, axis, distance):
    devices = range(lax.axis_size(axis))
    route = [((i - distance) % len(devices), i) for i in devices]
    return lax.ppermute(block, axis, route)


def masked_weight(weight, mask):
    row_blocks, col_blocks = mask.shape
    shaped = weight.reshape(
        row_blocks, weight.shape[0] // row_blocks, col_blocks, weight.shape[1] // col_blocks
    )
    return (shaped * mask.astype(jnp.bfloat16)[:, None, :, None]).reshape(weight.shape)


def project(token_rows, weight):
    return lax.dot_general(
        token_rows, weight, (((1,), (1,)), ((), ())), preferred_element_type=jnp.float32
    )


def gated_block(token_rows, gate_part, up_part):
    gate = project(token_rows, gate_part)
    up_values = project(token_rows, up_part)
    return (jax.nn.silu(gate) * up_values).astype(jnp.bfloat16)


def collect_panels(stacked):
    panel_count = lax.axis_size("panel")
    collected = [(stacked, 0)]
    moving = stacked
    for distance in range(1, panel_count):
        moving = passed_along(moving, "panel", 1)
        collected.append((moving, distance))
    return collected


def general_shards(tokens, gate_weight, up_weight, gate_mask, up_mask):
    panel_count = lax.axis_size("panel")
    my_panel = lax.axis_index("panel")
    width_rows = gate_weight.shape[0]
    stacked = jnp.stack([masked_weight(gate_weight, gate_mask), masked_weight(up_weight, up_mask)])
    collected = collect_panels(stacked)
    gathered = lax.all_gather(tokens, "seq", axis=0, tiled=True)
    tile = jnp.zeros((gathered.shape[0], panel_count * width_rows), jnp.bfloat16)
    for pair, distance in collected:
        source = (my_panel - distance) % panel_count
        result = gated_block(gathered, pair[0], pair[1])
        tile = lax.dynamic_update_slice_in_dim(tile, result, source * width_rows, 1)
    return lax.all_to_all(tile, "seq", split_axis=0, concat_axis=1, tiled=True)


def kernel(
    tok, gw, uw, gm, um, out,
    held, w, masks, wide, hid,
    recv_sem, send_sem, part_send, part_recv, local_sem, out_send, out_recv, out_local,
):
    rows, width = tok.shape
    wrows = gw.shape[0]
    seq, panel = lax.axis_index("seq"), lax.axis_index("panel")
    z, x = seq // 2, seq % 2
    y, core = panel // 2, panel % 2
    def block_of(bz, bx, by):
        return (bz * 2 + bx) * 2 + by

    def device(bz, bx, by):
        return (bz * 2 + bx, by * 2 + core)

    me = block_of(z, x, y)
    xdev, ydev = device(z, 1 - x, y), device(z, x, 1 - y)
    updev, downdev = device(z + 1, x, y), device(z - 1, x, y)
    partner = (seq, y * 2 + 1 - core)

    barrier = pltpu.get_barrier_semaphore()
    for dev in (xdev, ydev, partner):
        pl.semaphore_signal(barrier, inc=1, device_id=dev, device_id_type=MESH)

    @pl.when(z < NZ - 1)
    def _():
        pl.semaphore_signal(barrier, inc=1, device_id=updev, device_id_type=MESH)

    @pl.when(z > 0)
    def _():
        pl.semaphore_signal(barrier, inc=1, device_id=downdev, device_id_type=MESH)

    rows_of = lambda b: pl.ds(pl.multiple_of(b * rows, rows), rows)
    own = pl.ds(pl.multiple_of(core * wrows, wrows), wrows)
    own_up = pl.ds(pl.multiple_of((2 + core) * wrows, wrows), wrows)
    locals_ = [
        pltpu.make_async_copy(gw, w.at[own], local_sem.at[0]),
        pltpu.make_async_copy(uw, w.at[own_up], local_sem.at[1]),
        pltpu.make_async_copy(gm, masks.at[core], local_sem.at[2]),
        pltpu.make_async_copy(um, masks.at[2 + core], local_sem.at[3]),
        pltpu.make_async_copy(tok, held.at[rows_of(me)], local_sem.at[4]),
    ]
    for copy in locals_:
        copy.start()

    links = (z > 0).astype(jnp.int32) + (z < NZ - 1).astype(jnp.int32)
    pl.semaphore_wait(barrier, 3 + links)

    unit = width // 64
    first = (64 - RIDING) // 2
    ALL, C, A, B = (0, 64), (0, first), (first, 64 - RIDING), (64 - RIDING, 64)
    AB = (first, 64)
    RIDES = (((64 - RIDING, 64 - RIDING // 2), R), ((64 - RIDING // 2, 64), R2))
    sends = []

    def when(cond):
        return pl.when(cond) if cond is not None else (lambda f: f())

    def cols(part):
        return pl.ds(part[0] * unit, (part[1] - part[0]) * unit)

    def plane_rows(oz):
        return pl.ds(pl.multiple_of(oz * 4 * rows, 4 * rows), 4 * rows)

    def copy_piece(src, at, part, dev, kind, oz, cond):
        span = cols(part)
        copy = pltpu.make_async_remote_copy(
            src_ref=src.at[:, span] if src is tok else src.at[at, span], dst_ref=held.at[at, span],
            send_sem=send_sem.at[len(sends)], recv_sem=recv_sem.at[kind, oz],
            device_id=dev, device_id_type=MESH,
        )
        sends.append((copy, cond))
        when(cond)(copy.start)

    def send(origin, part, dev, kind, oz, cond=None):
        copy_piece(held, rows_of(origin), part, dev, kind, oz, cond)

    def await_rows(at, part, kind, oz):
        ref = held.at[at, cols(part)]
        pltpu.make_async_copy(ref, ref, recv_sem.at[kind, oz]).wait()

    def await_piece(origin, part, kind, oz):
        await_rows(rows_of(origin), part, kind, oz)

    has_up, has_down = z < NZ - 1, z > 0
    at_end = jnp.logical_or(z == 0, z == NZ - 1)
    bx, by, bd = block_of(z, 1 - x, y), block_of(z, x, 1 - y), block_of(z, 1 - x, 1 - y)

    def begin():
        mine = rows_of(me)
        for part, kind in ((A, L), (C, LC)):
            copy_piece(tok, mine, part, updev, kind, z, has_up)
            copy_piece(tok, mine, part, downdev, kind, z, has_down)
        copy_piece(tok, mine, AB, xdev, X, z, None)
        copy_piece(tok, mine, C, ydev, Y, z, None)
        copy_piece(tok, mine, C, xdev, X2, z, None)
        copy_piece(tok, mine, AB, ydev, Y2, z, None)

    def plane():
        await_piece(by, C, Y, z)
        send(by, C, xdev, DC, z)
        await_piece(bx, AB, X, z)
        send(bx, AB, ydev, DA, z)

    def ride_own():
        await_piece(by, AB, Y2, z)
        await_piece(bd, AB, DA, z)
        for part, kind in RIDES:
            copy_piece(held, plane_rows(z), part, updev, kind, z, has_up)
            copy_piece(held, plane_rows(z), part, downdev, kind, z, has_down)

    def sides(d):
        for up in (True, False):
            oz = z - d if up else z + d
            here = oz >= 0 if up else oz <= NZ - 1
            onward = jnp.logical_and(here, has_up if up else has_down)
            yield oz, here, (updev if up else downdev), (onward if d < NZ - 1 else False)

    def line(d):
        for oz, here, dev, onward in sides(d):
            b = block_of(oz, x, y)
            when(here)(functools.partial(await_piece, b, A, L, oz))
            if onward is not False:
                send(b, A, dev, L, oz, onward)
            send(b, A, xdev, X, oz, here)
            when(here)(functools.partial(await_piece, b, C, LC, oz))
            if onward is not False:
                send(b, C, dev, LC, oz, onward)
            send(b, C, ydev, Y, oz, here)
            send(b, C, xdev, X2, oz, here)
            send(b, A, ydev, Y2, oz, here)

    def cross(d):
        for oz, here, dev, onward in sides(d):
            ox, oy = block_of(oz, 1 - x, y), block_of(oz, x, 1 - y)
            when(here)(functools.partial(await_piece, ox, A, X, oz))
            send(ox, A, ydev, DA, oz, here)
            when(here)(functools.partial(await_piece, oy, C, Y, oz))
            send(oy, C, xdev, DC, oz, here)

    def ride(d):
        for oz, here, dev, onward in sides(d):
            for part, kind in RIDES:
                when(here)(functools.partial(await_rows, plane_rows(oz), part, kind, oz))
                if onward is not False:
                    copy_piece(held, plane_rows(oz), part, dev, kind, oz, onward)

    half = 2 * wrows
    mine_out = pl.ds(pl.multiple_of(me * half, half), half)

    def result_copy(oz, k):
        tx, ty = (x + k // 2) % 2, (y + k % 2) % 2
        return pltpu.make_async_remote_copy(
            src_ref=hid.at[rows_of(block_of(oz, tx, ty))], dst_ref=out.at[:, mine_out],
            send_sem=out_send.at[oz, k], recv_sem=out_recv.at[z, k],
            device_id=device(oz, tx, ty), device_id_type=MESH,
        )

    def multiply(oz):
        both = lax.dot_general(
            held[plane_rows(oz), :], w[...], (((1,), (1,)), ((), ())), preferred_element_type=jnp.float32
        )
        gate = both[:, :half]
        hid[plane_rows(oz), :] = (gate / (1.0 + jnp.exp(-gate)) * both[:, half:]).astype(jnp.bfloat16)

    def own_plane():
        await_piece(bx, C, X2, z)
        await_piece(bd, C, DC, z)
        multiply(z)
        for k in (3, 2, 1):
            result_copy(z, k).start()

    def other_planes(d, cond=None):
        for oz, here, _, _ in sides(d):
            def finish(oz=oz):
                diagonal = block_of(oz, 1 - x, 1 - y)
                await_piece(block_of(oz, 1 - x, y), C, X2, oz)
                await_piece(block_of(oz, x, 1 - y), A, Y2, oz)
                await_piece(diagonal, A, DA, oz)
                await_piece(diagonal, C, DC, oz)
                multiply(oz)
                for k in (3, 2, 1, 0):
                    result_copy(oz, k).start()
            when(here if cond is None else jnp.logical_and(here, cond))(finish)

    def weights():
        copies = []
        for i, (src, dst) in enumerate((
            (gw, w.at[own]), (uw, w.at[own_up]), (gm, masks.at[core]), (um, masks.at[2 + core]),
        )):
            copies.append(pltpu.make_async_remote_copy(
                src_ref=src, dst_ref=dst, send_sem=part_send.at[i], recv_sem=part_recv.at[i],
                device_id=partner, device_id_type=MESH,
            ))
        for copy in copies:
            copy.start()
        return copies

    def prune(copies):
        for copy in copies:
            copy.wait()
        for copy in locals_:
            copy.wait()
        step = 512
        block = width // masks.shape[2]
        row = lax.broadcasted_iota(jnp.int32, (8, masks.shape[2]), 0)
        table = jnp.zeros((8, masks.shape[2]), jnp.float32)
        for r in range(4):
            table = jnp.where(row == r, masks[r].astype(jnp.float32), table)
        table = table.astype(jnp.bfloat16)

        @pl.loop(0, width // step)
        def _(i):
            start = pl.multiple_of(i * step, step)
            where_ = lax.broadcasted_iota(jnp.int32, (masks.shape[2], step), 0)
            col = lax.broadcasted_iota(jnp.int32, (masks.shape[2], step), 1) + start
            first = where_ * block
            inside = jnp.logical_and(col >= first, col < first + block)
            select = jnp.where(inside, 1.0, 0.0).astype(jnp.bfloat16)
            wide[...] = jnp.dot(table, select, preferred_element_type=jnp.float32)
            for r in range(4):
                at = (pl.ds(r * wrows, wrows), pl.ds(start, step))
                keep = jnp.broadcast_to(wide[r:r + 1, :], (wrows, step))
                w[at] = (w[at].astype(jnp.float32) * keep).astype(jnp.bfloat16)

    begin()
    swaps = weights()
    plane()
    line(1)
    prune(swaps)
    line(2)
    ride_own()
    cross(1)
    line(3)
    own_plane()
    ride(1)
    cross(2)
    other_planes(1, at_end)
    ride(2)
    other_planes(1, jnp.logical_not(at_end))
    cross(3)
    other_planes(2)
    ride(3)
    other_planes(3)

    keep_own = pltpu.make_async_copy(hid.at[rows_of(me)], out.at[:, mine_out], out_local)
    keep_own.start()
    for copy, cond in sends:
        when(cond)(copy.wait_send)
    for oz in range(NZ):
        for k in range(4):
            def settle(oz=oz, k=k):
                sent = hid.at[rows_of(block_of(oz, (x + k // 2) % 2, (y + k % 2) % 2))]
                pltpu.make_async_copy(sent, sent, out_send.at[oz, k]).wait()
                source = block_of(oz, (x + k // 2) % 2, (y + k % 2) % 2)
                ref = out.at[:, pl.ds(pl.multiple_of(source * half, half), half)]
                pltpu.make_async_copy(ref, ref, out_recv.at[oz, k]).wait()
            when(z != oz if k == 0 else None)(settle)
    keep_own.wait()


NSENDS = 68


def shards(tokens, gate_weight, up_weight, gate_mask, up_mask):
    rows, width = tokens.shape
    wrows = gate_weight.shape[0]
    blocks = lax.axis_size("seq") * lax.axis_size("panel") // 2
    hidden = lax.axis_size("seq") * lax.axis_size("panel") * wrows
    dma = pltpu.SemaphoreType.DMA
    return pl.pallas_call(
        kernel,
        out_shape=pltpu.VMEM((rows, hidden), jnp.bfloat16),
        in_specs=[pl.BlockSpec(memory_space=pl.ANY)] * 5,
        out_specs=pl.BlockSpec(memory_space=pltpu.VMEM),
        scratch_shapes=[
            pltpu.VMEM((blocks * rows, width), jnp.bfloat16),
            pltpu.VMEM((4 * wrows, width), jnp.bfloat16),
            pltpu.VMEM((4, 1, gate_mask.shape[1]), jnp.int32),
            pltpu.VMEM((8, 512), jnp.float32),
            pltpu.VMEM((blocks * rows, 2 * wrows), jnp.bfloat16),
            dma((NKINDS, NZ)),
            dma((NSENDS,)),
            dma((4,)), dma((4,)), dma((5,)),
            dma((NZ, 4)), dma((NZ, 4)), dma,
        ],
        compiler_params=pltpu.CompilerParams(collective_id=0, has_side_effects=True),
    )(tokens, gate_weight, up_weight, gate_mask, up_mask)


def solution(mesh):
    spec = P(("seq", "panel"), None)
    fits = mesh.shape["seq"] == 2 * NZ and mesh.shape["panel"] == 4
    body = shards if fits else general_shards
    return jax.shard_map(
        body, mesh=mesh, in_specs=(spec,) * 5, out_specs=spec, check_vma=False
    )
```

```python
import functools

import jax
import jax.numpy as jnp
from jax import lax
from jax.experimental import pallas as pl
from jax.experimental.pallas import tpu as pltpu
from jax.sharding import PartitionSpec as P

MESH = pl.DeviceIdType.MESH
NZ = 4
PRUNES = 16
PIECES = ((0, 13), (13, 12), (25, 13), (38, 12), (50, 4), (54, 3), (57, 4), (61, 3))
ORDERS = ((
    (0, 0, 0, 5, 0, 0, 1), (0, 0, 0, 4, 0, 0, 1), (0, 0, 0, 6, 0, 0, 1), (0, 0, 0, 0, 0, 0, 1), (0, 1, 0, 6, 0, 0, 2),
    (0, 1, 0, 3, 0, 0, 2), (0, 1, 0, 5, 0, 0, 2), (0, 1, 0, 2, 0, 0, 2), (0, 2, 0, 0, 0, 0, 0), (0, 2, 0, 1, 0, 0, 0),
    (0, 0, 0, 1, 0, 0, 1), (0, 2, 0, 2, 0, 0, 0), (0, 1, 0, 7, 0, 0, 2), (0, 1, 0, 1, 0, 0, 2), (0, 0, 0, 7, 0, 0, 1),
    (0, 2, 0, 3, 0, 0, 0), (0, 0, 0, 3, 0, 0, 1), (1, 0, 5, 1), (0, 1, 0, 5, 1, 0, 3), (1, 0, 6, 2),
    (0, 1, 0, 0, 0, 0, 2), (1, 0, 4, 1), (0, 0, 0, 6, 2, 0, 3), (1, 0, 6, 1), (0, 0, 0, 2, 0, 0, 1), (1, 1, 0, 0),
    (1, 0, 3, 2), (1, 0, 5, 2), (0, 1, 0, 4, 1, 0, 3), (0, 1, 0, 4, 0, 0, 2), (1, 0, 0, 1), (0, 0, 0, 3, 2, 0, 3),
    (1, 1, 1, 0), (3, 0), (0, 1, 0, 0, 1, 0, 3), (3, 1), (1, 0, 2, 2), (3, 2), (1, 0, 7, 2), (1, 0, 1, 1),
    (0, 0, 0, 7, 2, 0, 3), (1, 1, 2, 0), (3, 3), (1, 0, 7, 1), (0, 0, 0, 2, 2, 0, 3), (0, 1, 0, 1, 1, 0, 3), (3, 4),
    (3, 5), (1, 0, 1, 2), (3, 6), (1, 0, 5, 3), (0, 2, 0, 5, 4, 0, 4), (1, 1, 3, 0), (1, 0, 3, 1),
    (0, 0, 1, 3, 0, 1, 1), (0, 1, 1, 2, 0, 1, 2), (3, 7), (1, 0, 6, 3), (0, 2, 0, 6, 4, 0, 4), (3, 8), (3, 9),
    (1, 0, 0, 2), (1, 2, 0, 0), (3, 10), (0, 0, 2, 0, 0, 2, 1), (0, 1, 1, 3, 0, 1, 2), (1, 0, 4, 3), (1, 0, 2, 1),
    (3, 11), (1, 0, 4, 2), (0, 2, 0, 4, 4, 0, 4), (3, 12), (1, 2, 1, 0), (3, 13), (0, 0, 2, 1, 0, 2, 1),
    (0, 1, 2, 1, 0, 2, 2), (1, 0, 3, 3), (3, 14), (1, 0, 7, 3), (0, 2, 0, 7, 4, 0, 4), (3, 15), (1, 0, 0, 3),
    (2, 0, 5), (1, 2, 2, 0), (0, 0, 2, 2, 0, 2, 1), (0, 1, 2, 2, 0, 2, 2), (2, 0, 6), (2, 0, 4), (1, 0, 2, 3),
    (1, 0, 1, 3), (2, 0, 3), (1, 2, 3, 0), (2, 0, 7), (0, 0, 2, 3, 0, 2, 1), (0, 1, 2, 3, 0, 2, 2), (2, 0, 0),
    (2, 0, 2), (1, 1, 3, 1), (1, 1, 2, 2), (2, 0, 1), (1, 1, 5, 4), (2, 1, 5), (0, 0, 1, 1, 0, 1, 1),
    (0, 1, 2, 0, 0, 2, 2), (1, 2, 0, 1), (1, 1, 3, 2), (1, 3, 0, 0), (0, 0, 3, 0, 0, 3, 1), (0, 1, 2, 0, 1, 2, 3),
    (1, 2, 1, 1), (1, 2, 1, 2), (1, 3, 1, 0), (0, 0, 3, 1, 0, 3, 1), (0, 1, 2, 1, 1, 2, 3), (1, 2, 2, 1),
    (1, 2, 2, 2), (1, 3, 2, 0), (0, 0, 2, 2, 2, 2, 3), (0, 1, 3, 2, 0, 3, 2), (1, 2, 3, 1), (1, 2, 3, 2),
    (1, 3, 3, 0), (0, 0, 2, 3, 2, 2, 3), (0, 1, 3, 3, 0, 3, 2), (1, 1, 1, 1), (1, 2, 0, 2), (1, 2, 5, 4), (2, 2, 5),
    (0, 0, 3, 3, 0, 3, 1), (0, 1, 1, 1, 1, 1, 3), (1, 3, 0, 1), (1, 2, 0, 3), (2, 2, 0), (1, 2, 7, 4), (2, 2, 7),
    (0, 0, 3, 2, 0, 3, 1), (0, 1, 3, 0, 1, 3, 3), (1, 3, 1, 1), (1, 2, 1, 3), (2, 2, 1), (0, 0, 1, 0, 0, 1, 1),
    (1, 2, 4, 4), (2, 2, 4), (0, 1, 3, 1, 1, 3, 3), (1, 2, 2, 3), (2, 2, 2), (1, 3, 2, 2), (0, 0, 3, 2, 2, 3, 3),
    (0, 1, 3, 0, 0, 3, 2), (1, 2, 6, 4), (2, 2, 6), (1, 2, 3, 3), (1, 3, 3, 2), (2, 2, 3), (0, 0, 3, 3, 2, 3, 3),
    (0, 1, 3, 1, 0, 3, 2), (1, 3, 5, 4), (2, 3, 5), (1, 3, 3, 1), (1, 1, 1, 3), (0, 0, 1, 2, 2, 1, 3),
    (0, 1, 1, 0, 0, 1, 2), (1, 3, 2, 1), (1, 3, 6, 4), (1, 3, 0, 3), (2, 3, 6), (0, 0, 1, 3, 2, 1, 3),
    (0, 1, 1, 1, 0, 1, 2), (1, 1, 0, 1), (1, 3, 7, 4), (1, 3, 1, 3), (2, 3, 7), (0, 0, 1, 2, 0, 1, 1),
    (0, 1, 1, 0, 1, 1, 3), (1, 3, 2, 3), (1, 3, 0, 2), (2, 3, 0), (2, 3, 2), (1, 3, 4, 4), (2, 3, 4), (1, 3, 3, 3),
    (1, 3, 1, 2), (2, 3, 1), (2, 3, 3), (1, 1, 4, 4), (2, 1, 4), (1, 1, 2, 3), (1, 1, 0, 2), (1, 1, 7, 4), (2, 1, 7),
    (1, 1, 3, 3), (1, 1, 1, 2), (2, 1, 1), (2, 1, 3), (1, 1, 6, 4), (2, 1, 6), (1, 1, 2, 1), (1, 1, 0, 3), (2, 1, 0),
    (2, 1, 2),
), (
    (0, 0, 1, 5, 0, 1, 1), (0, 0, 1, 6, 0, 1, 1), (0, 0, 1, 1, 0, 1, 1), (0, 0, 1, 4, 0, 1, 1), (0, 1, 1, 4, 0, 1, 2),
    (0, 1, 1, 7, 0, 1, 2), (0, 1, 1, 6, 0, 1, 2), (0, 1, 1, 3, 0, 1, 2), (0, 2, 1, 0, 0, 1, 0), (0, 2, 1, 1, 0, 1, 0),
    (0, 3, 1, 0, 0, 2, 0), (0, 3, 1, 1, 0, 2, 0), (0, 0, 1, 0, 0, 1, 1), (0, 1, 1, 2, 0, 1, 2), (0, 2, 1, 2, 0, 1, 0),
    (0, 3, 1, 2, 0, 2, 0), (0, 0, 1, 7, 0, 1, 1), (0, 1, 1, 1, 0, 1, 2), (0, 2, 1, 3, 0, 1, 0), (0, 3, 1, 3, 0, 2, 0),
    (0, 0, 1, 3, 0, 1, 1), (1, 1, 5, 1), (1, 1, 4, 2), (0, 1, 1, 5, 1, 1, 3), (1, 1, 6, 1), (1, 1, 7, 2),
    (0, 1, 1, 5, 0, 1, 2), (0, 0, 1, 7, 2, 1, 3), (0, 1, 1, 0, 0, 1, 2), (0, 0, 1, 2, 0, 1, 1), (1, 1, 6, 2),
    (1, 0, 0, 0), (1, 2, 0, 0), (0, 3, 0, 0, 0, 3, 0), (0, 2, 2, 0, 0, 2, 0), (1, 1, 1, 1), (1, 1, 4, 1),
    (1, 1, 3, 2), (0, 1, 1, 1, 1, 1, 3), (0, 0, 1, 3, 2, 1, 3), (1, 0, 1, 0), (1, 2, 1, 0), (0, 3, 0, 1, 0, 3, 0),
    (0, 2, 2, 1, 0, 2, 0), (3, 0), (3, 1), (3, 2), (0, 1, 1, 4, 1, 1, 3), (0, 0, 1, 6, 2, 1, 3), (1, 1, 0, 1),
    (1, 1, 2, 2), (1, 0, 2, 0), (1, 2, 2, 0), (0, 3, 0, 2, 0, 3, 0), (0, 2, 2, 2, 0, 2, 0), (3, 3), (1, 1, 7, 1),
    (0, 1, 1, 0, 1, 1, 3), (0, 0, 1, 2, 2, 1, 3), (3, 4), (3, 5), (1, 1, 1, 2), (3, 6), (1, 0, 3, 0), (1, 2, 3, 0),
    (0, 3, 0, 3, 0, 3, 0), (0, 2, 2, 3, 0, 2, 0), (1, 1, 5, 3), (1, 1, 3, 1), (0, 1, 2, 3, 0, 2, 2),
    (0, 0, 2, 0, 0, 2, 1), (3, 7), (1, 1, 5, 2), (1, 1, 7, 3), (0, 2, 1, 5, 4, 1, 4), (0, 3, 1, 5, 4, 2, 4), (3, 8),
    (3, 9), (1, 3, 0, 0), (3, 10), (0, 1, 2, 2, 0, 2, 2), (0, 0, 2, 1, 0, 2, 1), (1, 1, 0, 2), (1, 1, 2, 1), (3, 11),
    (0, 2, 3, 0, 0, 3, 0), (0, 3, 1, 7, 4, 2, 4), (3, 12), (1, 3, 1, 0), (3, 13), (0, 1, 2, 1, 0, 2, 2),
    (0, 0, 3, 1, 0, 3, 1), (1, 1, 1, 3), (1, 1, 3, 3), (3, 14), (0, 2, 3, 1, 0, 3, 0), (1, 1, 4, 3),
    (0, 3, 1, 4, 4, 2, 4), (1, 1, 6, 3), (3, 15), (1, 0, 5, 4), (2, 1, 5), (1, 3, 2, 0), (0, 1, 2, 0, 0, 2, 2),
    (0, 0, 2, 2, 0, 2, 1), (2, 1, 7), (0, 2, 3, 2, 0, 3, 0), (2, 1, 1), (1, 1, 0, 3), (1, 1, 2, 3),
    (0, 3, 1, 6, 4, 2, 4), (2, 1, 3), (1, 3, 3, 0), (2, 1, 4), (1, 0, 6, 4), (0, 1, 3, 3, 0, 3, 2),
    (0, 0, 2, 3, 0, 2, 1), (2, 1, 6), (0, 2, 3, 3, 0, 3, 0), (2, 0, 5), (1, 2, 3, 2), (1, 2, 0, 1), (2, 1, 0),
    (1, 2, 5, 4), (0, 3, 0, 5, 4, 3, 4), (2, 1, 2), (0, 1, 2, 0, 1, 2, 3), (0, 0, 2, 3, 2, 2, 3), (2, 0, 6),
    (1, 0, 4, 4), (0, 2, 2, 5, 4, 2, 4), (1, 2, 2, 2), (1, 2, 1, 1), (2, 2, 5), (1, 2, 7, 4), (2, 0, 4),
    (0, 3, 0, 6, 4, 3, 4), (0, 0, 2, 2, 2, 2, 3), (0, 1, 2, 1, 1, 2, 3), (2, 2, 7), (1, 0, 7, 4),
    (0, 2, 2, 7, 4, 2, 4), (2, 0, 7), (1, 2, 1, 2), (1, 3, 1, 1), (0, 0, 3, 0, 0, 3, 1), (0, 1, 3, 2, 0, 3, 2),
    (1, 2, 4, 4), (2, 2, 4), (0, 3, 0, 7, 4, 3, 4), (0, 2, 2, 4, 4, 2, 4), (1, 2, 0, 2), (1, 2, 2, 1),
    (0, 0, 3, 2, 0, 3, 1), (0, 1, 3, 1, 1, 3, 3), (0, 3, 0, 4, 4, 3, 4), (1, 2, 6, 4), (2, 2, 6), (1, 3, 3, 2),
    (1, 2, 3, 1), (0, 2, 2, 6, 4, 2, 4), (0, 1, 3, 1, 0, 3, 2), (0, 0, 3, 3, 2, 3, 3), (1, 3, 5, 4), (2, 3, 5),
    (1, 2, 3, 3), (1, 2, 0, 3), (2, 2, 3), (2, 2, 0), (0, 2, 3, 5, 4, 3, 4), (0, 1, 3, 0, 0, 3, 2),
    (0, 0, 3, 3, 0, 3, 1), (1, 2, 2, 3), (1, 2, 1, 3), (2, 2, 1), (1, 3, 6, 4), (2, 2, 2), (0, 2, 3, 6, 4, 3, 4),
    (2, 3, 6), (0, 1, 0, 3, 0, 0, 2), (0, 0, 0, 3, 0, 0, 1), (1, 3, 0, 1), (1, 3, 2, 2), (1, 3, 7, 4), (2, 3, 7),
    (0, 1, 3, 0, 1, 3, 3), (0, 0, 3, 2, 2, 3, 3), (0, 2, 3, 7, 4, 3, 4), (1, 3, 1, 3), (1, 3, 2, 1), (1, 3, 4, 4),
    (2, 3, 4), (0, 1, 0, 2, 0, 0, 2), (0, 0, 0, 0, 0, 0, 1), (0, 2, 3, 4, 4, 3, 4), (1, 3, 1, 2), (2, 3, 1),
    (1, 3, 3, 3), (0, 1, 0, 0, 0, 0, 2), (0, 0, 0, 1, 0, 0, 1), (0, 2, 1, 4, 4, 1, 4), (1, 3, 0, 2), (1, 3, 3, 1),
    (2, 3, 3), (0, 0, 0, 2, 0, 0, 1), (0, 1, 0, 1, 0, 0, 2), (1, 0, 3, 2), (1, 0, 3, 1), (0, 2, 1, 7, 4, 1, 4),
    (0, 0, 0, 3, 2, 0, 3), (1, 3, 0, 3), (1, 3, 2, 3), (2, 3, 0), (0, 2, 1, 6, 4, 1, 4), (2, 3, 2), (1, 0, 2, 2),
    (1, 0, 0, 1), (0, 0, 0, 2, 2, 0, 3), (0, 1, 0, 0, 1, 0, 3), (1, 0, 1, 1), (0, 1, 0, 1, 1, 0, 3), (1, 0, 0, 2),
    (1, 0, 2, 1), (1, 0, 1, 2), (1, 0, 3, 3), (2, 0, 3), (1, 0, 0, 3), (2, 0, 0), (1, 0, 2, 3), (1, 0, 1, 3),
    (2, 0, 1), (2, 0, 2),
))
GROUPS = ((0, 0, 0, 0, 0, 0, 0, 0, 0, 0, 0, 0, 0, 0, 0, 0, 0, 0, 0, 0, 0, 0, 0, 0, 0, 0, 0, 0, 0, 0, 0, 0, 0, 0, 0, 0, 0, 0, 0, 0, 0, 0, 0, 0, 0, 0, 0, 0, 0, 0, 0, 0, 0, 0, 0, 0, 0, 0, 0, 0, 0, 0, 0, 0, 0, 0, 0, 1), (0, 0, 0, 0, 0, 0, 0, 0, 0, 0, 0, 0, 0, 0, 0, 0, 0, 0, 0, 0, 0, 0, 0, 0, 0, 0, 0, 0, 0, 0, 0, 0, 0, 0, 0, 0, 0, 0, 0, 0, 0, 0, 0, 0, 0, 0, 0, 0, 0, 0, 0, 0, 0, 0, 0, 0, 0, 0, 0, 0, 0, 0, 0, 0, 0, 0, 0, 0, 0, 0, 0, 0, 0, 0, 0, 0, 0, 0, 0, 1, 1, 1, 1, 1, 1, 1, 1, 1, 1, 1, 1, 1, 1, 1, 1, 1, 1, 1, 1, 1))
SHAPES = (((15, 49), (13, 1)), ((16, 56), (12, 23)))
ARRIVALS = tuple(tuple(op[1:] for op in order if op[0] == 1) for order in ORDERS)


def passed_along(block, axis, distance):
    devices = range(lax.axis_size(axis))
    route = [((i - distance) % len(devices), i) for i in devices]
    return lax.ppermute(block, axis, route)


def masked_weight(weight, mask):
    row_blocks, col_blocks = mask.shape
    shaped = weight.reshape(
        row_blocks, weight.shape[0] // row_blocks, col_blocks, weight.shape[1] // col_blocks
    )
    return (shaped * mask.astype(jnp.bfloat16)[:, None, :, None]).reshape(weight.shape)


def project(token_rows, weight):
    return lax.dot_general(
        token_rows, weight, (((1,), (1,)), ((), ())), preferred_element_type=jnp.float32
    )


def gated_block(token_rows, gate_part, up_part):
    gate = project(token_rows, gate_part)
    up_values = project(token_rows, up_part)
    return (jax.nn.silu(gate) * up_values).astype(jnp.bfloat16)


def collect_panels(stacked):
    panel_count = lax.axis_size("panel")
    collected = [(stacked, 0)]
    moving = stacked
    for distance in range(1, panel_count):
        moving = passed_along(moving, "panel", 1)
        collected.append((moving, distance))
    return collected


def general_shards(tokens, gate_weight, up_weight, gate_mask, up_mask):
    panel_count = lax.axis_size("panel")
    my_panel = lax.axis_index("panel")
    width_rows = gate_weight.shape[0]
    stacked = jnp.stack([masked_weight(gate_weight, gate_mask), masked_weight(up_weight, up_mask)])
    collected = collect_panels(stacked)
    gathered = lax.all_gather(tokens, "seq", axis=0, tiled=True)
    tile = jnp.zeros((gathered.shape[0], panel_count * width_rows), jnp.bfloat16)
    for pair, distance in collected:
        source = (my_panel - distance) % panel_count
        result = gated_block(gathered, pair[0], pair[1])
        tile = lax.dynamic_update_slice_in_dim(tile, result, source * width_rows, 1)
    return lax.all_to_all(tile, "seq", split_axis=0, concat_axis=1, tiled=True)


def kernel(
    tok, gw, uw, gm, um, out,
    held, w, masks, wide, hid,
    total, recv_sem, send_sem, part_send, part_recv, local_sem, out_send, out_recv, out_local,
):
    rows, width = tok.shape
    wrows = gw.shape[0]
    seq, panel = lax.axis_index("seq"), lax.axis_index("panel")
    z, x = seq // 2, seq % 2
    y, core = panel // 2, panel % 2

    def device(bz, bx, by):
        return (bz * 2 + bx, by * 2 + core)

    low = z < NZ // 2
    toward = jnp.where(low, 1, -1)
    at_end = jnp.logical_or(z == 0, z == NZ - 1)

    def plane_z(p):
        return jnp.where(low, p, NZ - 1 - p)

    xdev, ydev = device(z, 1 - x, y), device(z, x, 1 - y)
    inward, outward = device(z + toward, x, y), device(z - toward, x, y)
    partner = (seq, y * 2 + 1 - core)

    barrier = pltpu.get_barrier_semaphore()
    for dev in (xdev, ydev, partner, inward):
        pl.semaphore_signal(barrier, inc=1, device_id=dev, device_id_type=MESH)

    @pl.when(jnp.logical_not(at_end))
    def _():
        pl.semaphore_signal(barrier, inc=1, device_id=outward, device_id_type=MESH)

    def slot(p, b):
        return pl.ds((p * 4 + b) * rows, rows) if b < 4 else pl.ds(p * 4 * rows, 4 * rows)

    own = pl.ds(pl.multiple_of(core * wrows, wrows), wrows)
    own_up = pl.ds(pl.multiple_of((2 + core) * wrows, wrows), wrows)
    weight_parts = (
        (gw, w.at[own]), (uw, w.at[own_up]), (gm, masks.at[core]), (um, masks.at[2 + core]),
    )
    for i, (src, dst) in enumerate(weight_parts):
        pltpu.make_async_copy(src, dst, local_sem.at[i // 2]).start()
    keep_tokens = [
        pltpu.make_async_copy(tok, held.at[slot(q, 0)], local_sem.at[2]) for q in range(2)
    ]
    when_q = (at_end, jnp.logical_not(at_end))
    for q in range(2):
        pl.when(when_q[q])(keep_tokens[q].start)
    pl.semaphore_wait(barrier, jnp.where(at_end, 4, 5))

    unit = width // 64

    def cols(k):
        return pl.ds(PIECES[k][0] * unit, PIECES[k][1] * unit)

    half = 2 * wrows

    def out_cols(bz, bx, by):
        block = (bz * 2 + bx) * 2 + by
        return pl.ds(pl.multiple_of(block * half, half), half)

    def relative(b):
        return (x + b % 2) % 2, (y + b // 2) % 2

    swaps = [
        pltpu.make_async_remote_copy(
            src_ref=src, dst_ref=dst, send_sem=part_send.at[i // 2], recv_sem=part_recv.at[i // 2],
            device_id=partner, device_id_type=MESH,
        )
        for i, (src, dst) in enumerate(weight_parts)
    ]

    def prune(i, state):
        if i == 0:
            for j, ref in enumerate((w.at[pl.ds(0, half)], masks.at[pl.ds(0, 2)])):
                for sem in (local_sem, part_send, part_recv):
                    pltpu.make_async_copy(ref, ref, sem.at[j]).wait()
            row = lax.broadcasted_iota(jnp.int32, (8, masks.shape[2]), 0)
            table = jnp.zeros((8, masks.shape[2]), jnp.float32)
            for r in range(4):
                table = jnp.where(row == r, masks[r].astype(jnp.float32), table)
            state["table"] = table.astype(jnp.bfloat16)
        step = width // PRUNES
        block = width // masks.shape[2]
        start = i * step
        where_ = lax.broadcasted_iota(jnp.int32, (masks.shape[2], step), 0)
        col = lax.broadcasted_iota(jnp.int32, (masks.shape[2], step), 1) + start
        first = where_ * block
        inside = jnp.logical_and(col >= first, col < first + block)
        select = jnp.where(inside, 1.0, 0.0).astype(jnp.bfloat16)
        wide[...] = jnp.dot(state["table"], select, preferred_element_type=jnp.float32)
        for r in range(4):
            at = (pl.ds(r * wrows, wrows), pl.ds(start, step))
            keep = jnp.broadcast_to(wide[r:r + 1, :], (wrows, step))
            w[at] = (w[at].astype(jnp.float32) * keep).astype(jnp.bfloat16)

    def program(q, table):
        links = (xdev, ydev, inward if q == 0 else outward, inward)
        sends, state, results = [], {}, []

        def own_tokens():
            if "kept" not in state:
                state["kept"] = True
                keep_tokens[q].wait()

        def finish(p, both):
            gate = both[:, :half]
            hid[slot(p, 4), :] = (gate / (1.0 + jnp.exp(-gate)) * both[:, half:]).astype(jnp.bfloat16)
            for b in (3, 2, 1, 0):
                if (p, b) == (q, 0):
                    state["kept_out"] = pltpu.make_async_copy(
                        hid.at[slot(p, 0)], out.at[:, out_cols(z, x, y)], out_local
                    )
                    state["kept_out"].start()
                    continue
                tx, ty = relative(b)
                pltpu.make_async_remote_copy(
                    src_ref=hid.at[slot(p, b)], dst_ref=out.at[:, out_cols(z, x, y)],
                    send_sem=out_send, recv_sem=out_recv,
                    device_id=device(plane_z(p), tx, ty), device_id_type=MESH,
                ).start()

        def multiply(p, k):
            if p == q:
                own_tokens()
            at = slot(p, 4)
            both = lax.dot_general(
                held[at, cols(k)], w[:, cols(k)], (((1,), (1,)), ((), ())), preferred_element_type=jnp.float32
            )
            done = state.get(p, 0)
            if done:
                both = both + total[at, :]
            state[p] = done + 1
            if done + 1 < len(PIECES):
                total[at, :] = both
            else:
                finish(p, both)

        for copy in swaps:
            copy.start()
        for op in table:
            if op[0] == 0:
                _, link, p, k, src, p2, dst = op
                q2 = 1 - q if link == 2 else q
                if src == 4 and p == q:
                    own_tokens()
                source = tok.at[:, cols(k)] if src == 0 and p == q else held.at[slot(p, src), cols(k)]
                copy = pltpu.make_async_remote_copy(
                    src_ref=source, dst_ref=held.at[slot(p2, dst), cols(k)],
                    send_sem=send_sem.at[GROUPS[q][len(sends)]], recv_sem=recv_sem.at[ARRIVALS[q2].index((p2, k, dst))],
                    device_id=links[link], device_id_type=MESH,
                )
                copy.start()
                sends.append(copy)
            elif op[0] == 1:
                _, p, k, b = op
                ref = held.at[slot(p, b), cols(k)]
                pltpu.make_async_copy(ref, ref, recv_sem.at[ARRIVALS[q].index((p, k, b))]).wait()
            elif op[0] == 2:
                multiply(op[1], op[2])
            else:
                prune(op[1], state)
        for group, (high, wide_) in enumerate(SHAPES[q]):
            ref = held.at[pl.ds(0, high * rows), pl.ds(0, wide_ * unit)]
            pltpu.make_async_copy(ref, ref, send_sem.at[group]).wait()
        others = 4 * NZ - 1
        ref = hid.at[pl.ds(0, others * rows)]
        pltpu.make_async_copy(ref, ref, out_send).wait()
        state["kept_out"].wait()
        ref = out.at[:, pl.ds(0, others * half)]
        pltpu.make_async_copy(ref, ref, out_recv).wait()

    for q in range(2):
        pl.when(when_q[q])(functools.partial(program, q, ORDERS[q]))


def shards(tokens, gate_weight, up_weight, gate_mask, up_mask):
    rows, width = tokens.shape
    wrows = gate_weight.shape[0]
    blocks = lax.axis_size("seq") * lax.axis_size("panel") // 2
    hidden = lax.axis_size("seq") * lax.axis_size("panel") * wrows
    dma = pltpu.SemaphoreType.DMA
    return pl.pallas_call(
        kernel,
        out_shape=pltpu.VMEM((rows, hidden), jnp.bfloat16),
        in_specs=[pl.BlockSpec(memory_space=pl.ANY)] * 5,
        out_specs=pl.BlockSpec(memory_space=pltpu.VMEM),
        scratch_shapes=[
            pltpu.VMEM((blocks * rows, width), jnp.bfloat16),
            pltpu.VMEM((4 * wrows, width), jnp.bfloat16),
            pltpu.VMEM((4, 1, gate_mask.shape[1]), jnp.int32),
            pltpu.VMEM((8, width // PRUNES), jnp.float32),
            pltpu.VMEM((blocks * rows, 2 * wrows), jnp.bfloat16),
            pltpu.VMEM((blocks * rows, 4 * wrows), jnp.float32),
            dma((max(map(len, ARRIVALS)),)), dma((max(map(len, SHAPES)),)),
            dma((2,)), dma((2,)), dma((3,)), dma, dma, dma,
        ],
        compiler_params=pltpu.CompilerParams(collective_id=0, has_side_effects=True),
    )(tokens, gate_weight, up_weight, gate_mask, up_mask)


def solution(mesh):
    spec = P(("seq", "panel"), None)
    fits = mesh.shape["seq"] == 2 * NZ and mesh.shape["panel"] == 4
    body = shards if fits else general_shards
    return jax.shard_map(
        body, mesh=mesh, in_specs=(spec,) * 5, out_specs=spec, check_vma=False
    )
```

```python
import functools

import jax
import jax.numpy as jnp
from jax import lax
from jax.experimental import pallas as pl
from jax.experimental.pallas import tpu as pltpu
from jax.sharding import PartitionSpec as P

MESH = pl.DeviceIdType.MESH
NZ = 4
PRUNES = 16
PIECES = ((0, 13, 1), (13, 12, 1), (25, 13, 0), (38, 12, 0), (50, 4, 1), (54, 3, 1), (57, 4, 0), (61, 3, 0))
ORDERS = ((
    (0, 0, 0, 3, 0, 0, 1), (0, 0, 0, 6, 0, 0, 1), (0, 0, 0, 0, 0, 0, 1), (0, 1, 0, 7, 0, 0, 3), (0, 1, 0, 1, 0, 0, 3),
    (0, 1, 0, 3, 0, 0, 3), (0, 2, 0, 0, 0, 0, 0), (0, 2, 0, 1, 0, 0, 0), (0, 2, 0, 2, 0, 0, 0), (0, 1, 0, 4, 0, 0, 3),
    (0, 0, 0, 7, 0, 0, 1), (4, 0), (0, 1, 0, 2, 0, 0, 3), (0, 0, 0, 5, 0, 0, 1), (0, 0, 0, 4, 0, 0, 1),
    (0, 2, 0, 3, 0, 0, 0), (0, 0, 0, 1, 0, 0, 1), (0, 1, 0, 6, 0, 0, 3), (1, 0, 7, 3), (0, 1, 0, 0, 0, 0, 3),
    (0, 0, 0, 7, 3, 0, 2), (0, 0, 0, 2, 0, 0, 1), (1, 1, 0, 0), (0, 1, 1, 0, 0, 1, 3), (0, 0, 1, 0, 0, 1, 1),
    (1, 1, 1, 0), (1, 0, 3, 3), (3, 0), (1, 0, 0, 1), (3, 1), (0, 1, 0, 5, 0, 0, 3), (0, 1, 0, 0, 1, 0, 2), (3, 2),
    (1, 0, 5, 1), (0, 0, 0, 3, 3, 0, 2), (1, 1, 3, 0), (3, 3), (1, 0, 4, 1), (3, 4), (1, 0, 2, 3), (3, 5),
    (0, 1, 0, 5, 1, 0, 2), (1, 0, 6, 3), (0, 0, 0, 2, 3, 0, 2), (3, 6), (0, 1, 0, 4, 1, 0, 2), (1, 1, 2, 0),
    (1, 0, 1, 1), (3, 7), (0, 1, 0, 1, 1, 0, 2), (1, 0, 7, 5), (0, 2, 0, 7, 4, 0, 4), (3, 8), (3, 9),
    (0, 0, 0, 6, 3, 0, 2), (1, 2, 0, 0), (3, 10), (0, 1, 2, 0, 0, 2, 3), (0, 0, 2, 0, 0, 2, 1), (3, 11), (3, 12),
    (1, 2, 1, 0), (3, 13), (0, 1, 2, 1, 0, 2, 3), (0, 0, 2, 1, 0, 2, 1), (1, 1, 0, 1), (3, 14), (3, 15), (2, 0, 7),
    (1, 2, 2, 0), (1, 0, 0, 5), (2, 0, 0), (0, 1, 2, 2, 0, 2, 3), (0, 0, 2, 2, 0, 2, 1), (1, 0, 3, 5), (1, 0, 5, 5),
    (0, 2, 0, 5, 4, 0, 4), (2, 0, 3), (1, 0, 4, 5), (0, 2, 0, 4, 4, 0, 4), (2, 0, 5), (1, 2, 3, 0), (2, 0, 4),
    (0, 1, 2, 3, 0, 2, 3), (0, 0, 2, 3, 0, 2, 1), (1, 0, 2, 5), (2, 0, 2), (1, 0, 1, 5), (1, 0, 6, 5),
    (0, 2, 0, 6, 4, 0, 4), (2, 0, 1), (1, 1, 7, 4), (2, 0, 6), (2, 1, 7), (0, 1, 1, 2, 0, 1, 3),
    (0, 0, 1, 1, 0, 1, 1), (1, 2, 0, 1), (1, 3, 0, 0), (0, 0, 3, 0, 0, 3, 1), (0, 1, 2, 0, 1, 2, 2), (1, 2, 1, 1),
    (1, 3, 1, 0), (0, 0, 3, 1, 0, 3, 1), (0, 1, 2, 1, 1, 2, 2), (1, 2, 2, 3), (1, 3, 2, 0), (0, 0, 2, 2, 3, 2, 2),
    (0, 1, 3, 2, 0, 3, 3), (1, 2, 3, 3), (1, 3, 3, 0), (0, 0, 2, 3, 3, 2, 2), (0, 1, 3, 3, 0, 3, 3), (1, 1, 1, 1),
    (1, 1, 2, 3), (1, 2, 7, 4), (2, 2, 7), (0, 0, 3, 2, 0, 3, 1), (0, 1, 3, 1, 0, 3, 3), (1, 3, 0, 1), (1, 2, 0, 5),
    (2, 2, 0), (1, 2, 4, 4), (2, 2, 4), (0, 0, 3, 3, 0, 3, 1), (0, 1, 3, 0, 1, 3, 2), (1, 3, 1, 1), (1, 2, 1, 5),
    (2, 2, 1), (1, 2, 5, 4), (2, 2, 5), (0, 0, 1, 3, 0, 1, 1), (0, 1, 3, 1, 1, 3, 2), (1, 2, 2, 5), (2, 2, 2),
    (1, 3, 2, 3), (1, 3, 7, 4), (2, 3, 7), (0, 0, 3, 2, 3, 3, 2), (0, 1, 3, 0, 0, 3, 3), (1, 2, 3, 5), (2, 2, 3),
    (1, 3, 3, 3), (0, 0, 3, 3, 3, 3, 2), (0, 1, 1, 3, 0, 1, 3), (1, 2, 6, 4), (2, 2, 6), (0, 0, 1, 2, 3, 1, 2),
    (0, 1, 1, 1, 1, 1, 2), (1, 3, 5, 4), (2, 3, 5), (0, 0, 1, 2, 0, 1, 1), (0, 1, 1, 0, 1, 1, 2), (1, 3, 4, 4),
    (2, 3, 4), (1, 3, 1, 5), (2, 3, 1), (0, 1, 1, 1, 0, 1, 3), (1, 3, 2, 5), (2, 3, 2), (1, 3, 0, 5), (2, 3, 0),
    (1, 3, 6, 4), (2, 3, 6), (1, 3, 3, 5), (2, 3, 3), (1, 1, 3, 3), (0, 0, 1, 3, 3, 1, 2), (1, 1, 4, 4), (2, 1, 4),
    (1, 1, 5, 4), (2, 1, 5), (1, 1, 2, 5), (1, 1, 0, 5), (2, 1, 0), (2, 1, 2), (1, 1, 6, 4), (2, 1, 6), (1, 1, 1, 5),
    (1, 1, 3, 5), (2, 1, 1), (2, 1, 3),
), (
    (0, 0, 1, 7, 0, 1, 1), (0, 0, 1, 1, 0, 1, 1), (0, 0, 1, 2, 0, 1, 1), (0, 1, 1, 4, 0, 1, 3), (0, 1, 1, 7, 0, 1, 3),
    (0, 1, 1, 2, 0, 1, 3), (0, 2, 1, 0, 0, 1, 0), (0, 2, 1, 1, 0, 1, 0), (0, 3, 1, 0, 0, 2, 0), (0, 3, 1, 1, 0, 2, 0),
    (0, 1, 1, 3, 0, 1, 3), (0, 2, 1, 3, 0, 1, 0), (0, 3, 1, 2, 0, 2, 0), (0, 0, 1, 4, 0, 1, 1), (4, 0),
    (0, 1, 1, 6, 0, 1, 3), (0, 0, 1, 5, 0, 1, 1), (0, 0, 1, 0, 0, 1, 1), (0, 1, 1, 0, 0, 1, 3), (0, 2, 1, 2, 0, 1, 0),
    (0, 3, 1, 3, 0, 2, 0), (0, 0, 1, 6, 0, 1, 1), (0, 1, 1, 1, 0, 1, 3), (1, 1, 7, 3), (0, 0, 1, 7, 3, 1, 2),
    (0, 0, 1, 3, 0, 1, 1), (1, 0, 0, 0), (1, 2, 0, 0), (0, 3, 0, 0, 0, 3, 0), (0, 2, 2, 0, 0, 2, 0), (1, 1, 1, 1),
    (0, 1, 1, 1, 1, 1, 2), (1, 1, 2, 3), (0, 0, 0, 0, 0, 0, 1), (1, 0, 1, 0), (1, 2, 1, 0), (0, 3, 0, 1, 0, 3, 0),
    (0, 2, 2, 1, 0, 2, 0), (3, 0), (0, 1, 1, 5, 0, 1, 3), (3, 1), (1, 1, 3, 3), (1, 1, 4, 1), (0, 1, 1, 4, 1, 1, 2),
    (3, 2), (1, 1, 5, 1), (1, 1, 6, 3), (0, 0, 1, 3, 3, 1, 2), (0, 1, 1, 5, 1, 1, 2), (1, 0, 2, 0), (1, 2, 2, 0),
    (0, 3, 0, 2, 0, 3, 0), (0, 2, 2, 2, 0, 2, 0), (3, 3), (0, 1, 2, 2, 0, 2, 3), (3, 4), (3, 5), (1, 1, 0, 1),
    (0, 0, 1, 2, 3, 1, 2), (3, 6), (1, 0, 3, 0), (1, 2, 3, 0), (0, 3, 0, 3, 0, 3, 0), (0, 2, 2, 3, 0, 2, 0),
    (0, 1, 1, 0, 1, 1, 2), (3, 7), (1, 1, 7, 5), (0, 2, 1, 7, 4, 1, 4), (0, 3, 1, 7, 4, 2, 4), (3, 8), (3, 9),
    (0, 0, 1, 6, 3, 1, 2), (1, 3, 0, 0), (3, 10), (0, 0, 0, 3, 0, 0, 1), (0, 1, 3, 0, 0, 3, 3), (3, 11),
    (0, 2, 3, 0, 0, 3, 0), (3, 12), (1, 1, 1, 5), (1, 3, 1, 0), (3, 13), (0, 0, 3, 1, 0, 3, 1), (0, 1, 3, 1, 0, 3, 3),
    (1, 0, 0, 1), (1, 1, 4, 5), (0, 3, 1, 4, 4, 2, 4), (3, 14), (0, 2, 3, 1, 0, 3, 0), (1, 1, 5, 5), (3, 15),
    (0, 3, 1, 5, 4, 2, 4), (2, 1, 7), (1, 3, 2, 0), (1, 0, 7, 4), (0, 0, 3, 0, 0, 3, 1), (2, 1, 1),
    (0, 1, 3, 2, 0, 3, 3), (1, 1, 3, 5), (0, 2, 3, 2, 0, 3, 0), (2, 1, 4), (1, 2, 2, 3), (0, 3, 0, 7, 4, 3, 4),
    (2, 1, 5), (1, 3, 3, 0), (2, 0, 7), (0, 0, 3, 2, 0, 3, 1), (0, 1, 3, 3, 0, 3, 3), (2, 1, 3), (1, 1, 2, 5),
    (0, 2, 3, 3, 0, 3, 0), (2, 1, 2), (1, 1, 6, 5), (0, 3, 1, 6, 4, 2, 4), (1, 1, 0, 5), (2, 1, 6), (1, 2, 7, 4),
    (2, 1, 0), (0, 0, 3, 3, 0, 3, 1), (0, 1, 0, 3, 0, 0, 3), (2, 2, 7), (0, 2, 2, 7, 4, 2, 4), (0, 0, 2, 1, 0, 2, 1),
    (0, 1, 0, 0, 0, 0, 3), (1, 2, 4, 4), (2, 2, 4), (1, 0, 5, 4), (0, 3, 0, 5, 4, 3, 4), (0, 2, 2, 4, 4, 2, 4),
    (2, 0, 5), (1, 3, 1, 1), (0, 0, 0, 1, 0, 0, 1), (1, 2, 5, 4), (2, 2, 5), (0, 1, 3, 1, 1, 3, 2), (1, 0, 4, 4),
    (0, 3, 0, 4, 4, 3, 4), (2, 0, 4), (1, 3, 0, 1), (0, 2, 2, 5, 4, 2, 4), (1, 3, 2, 3), (0, 0, 3, 2, 3, 3, 2),
    (1, 3, 7, 4), (2, 3, 7), (0, 1, 3, 0, 1, 3, 2), (0, 2, 3, 7, 4, 3, 4), (1, 3, 3, 3), (1, 0, 6, 4),
    (0, 3, 0, 6, 4, 3, 4), (2, 0, 6), (0, 0, 3, 3, 3, 3, 2), (0, 1, 0, 2, 0, 0, 3), (1, 2, 6, 4), (2, 2, 6),
    (0, 2, 2, 6, 4, 2, 4), (1, 0, 3, 3), (0, 0, 0, 3, 3, 0, 2), (0, 1, 2, 3, 0, 2, 3), (1, 3, 5, 4), (2, 3, 5),
    (1, 2, 1, 1), (0, 2, 3, 5, 4, 3, 4), (0, 0, 2, 3, 0, 2, 1), (0, 1, 2, 1, 1, 2, 2), (1, 0, 1, 1), (1, 3, 1, 5),
    (1, 3, 4, 4), (2, 3, 1), (0, 2, 3, 4, 4, 3, 4), (2, 3, 4), (0, 0, 2, 0, 0, 2, 1), (0, 1, 0, 1, 1, 0, 2),
    (1, 3, 2, 5), (2, 3, 2), (1, 3, 0, 5), (2, 3, 0), (1, 3, 6, 4), (0, 0, 0, 2, 0, 0, 1), (2, 3, 6),
    (0, 2, 3, 6, 4, 3, 4), (0, 1, 0, 1, 0, 0, 3), (1, 3, 3, 5), (2, 3, 3), (1, 0, 2, 3), (0, 0, 0, 2, 3, 0, 2),
    (0, 1, 0, 0, 1, 0, 2), (0, 2, 1, 4, 4, 1, 4), (1, 0, 3, 5), (2, 0, 3), (1, 2, 3, 3), (0, 0, 2, 2, 3, 2, 2),
    (0, 1, 2, 1, 0, 2, 3), (0, 2, 1, 5, 4, 1, 4), (0, 1, 2, 0, 0, 2, 3), (0, 0, 2, 3, 3, 2, 2), (1, 2, 0, 1),
    (0, 2, 1, 6, 4, 1, 4), (0, 0, 2, 2, 0, 2, 1), (0, 1, 2, 0, 1, 2, 2), (1, 0, 1, 5), (2, 0, 1), (1, 0, 2, 5),
    (1, 0, 0, 5), (2, 0, 2), (2, 0, 0), (1, 2, 1, 5), (2, 2, 1), (1, 2, 3, 5), (2, 2, 3), (1, 2, 2, 5), (1, 2, 0, 5),
    (2, 2, 2), (2, 2, 0),
))
GROUPS = ((0, 0, 0, 0, 0, 0, 0, 0, 0, 0, 0, 0, 0, 0, 0, 0, 0, 0, 0, 0, 0, 0, 0, 0, 0, 0, 0, 0, 0, 0, 0, 0, 0, 0, 0, 0, 0, 0, 0, 0, 0, 0, 0, 0, 0, 0, 0, 0, 0, 0, 0, 0, 0, 0, 0, 0, 0, 0, 0, 0, 0, 0, 0, 0, 0, 0, 0, 1), (0, 0, 0, 0, 0, 0, 0, 0, 0, 0, 0, 0, 0, 0, 0, 0, 0, 0, 0, 0, 0, 0, 0, 0, 0, 0, 0, 0, 0, 0, 0, 0, 0, 0, 0, 0, 0, 0, 0, 0, 0, 0, 0, 0, 0, 0, 0, 0, 0, 0, 0, 0, 0, 0, 0, 0, 0, 0, 0, 0, 0, 0, 0, 0, 0, 0, 0, 0, 0, 0, 0, 0, 0, 0, 0, 0, 0, 0, 0, 0, 0, 0, 0, 0, 1, 1, 1, 1, 1, 1, 1, 1, 1, 1, 1, 1, 1, 1, 1, 1))
SHAPES = (((16, 46), (12, 1)), ((16, 60), (4, 53)))
ARRIVALS = tuple(tuple(op[1:] for op in order if op[0] == 1) for order in ORDERS)


def passed_along(block, axis, distance):
    devices = range(lax.axis_size(axis))
    route = [((i - distance) % len(devices), i) for i in devices]
    return lax.ppermute(block, axis, route)


def masked_weight(weight, mask):
    row_blocks, col_blocks = mask.shape
    shaped = weight.reshape(
        row_blocks, weight.shape[0] // row_blocks, col_blocks, weight.shape[1] // col_blocks
    )
    return (shaped * mask.astype(jnp.bfloat16)[:, None, :, None]).reshape(weight.shape)


def project(token_rows, weight):
    return lax.dot_general(
        token_rows, weight, (((1,), (1,)), ((), ())), preferred_element_type=jnp.float32
    )


def gated_block(token_rows, gate_part, up_part):
    gate = project(token_rows, gate_part)
    up_values = project(token_rows, up_part)
    return (jax.nn.silu(gate) * up_values).astype(jnp.bfloat16)


def collect_panels(stacked):
    panel_count = lax.axis_size("panel")
    collected = [(stacked, 0)]
    moving = stacked
    for distance in range(1, panel_count):
        moving = passed_along(moving, "panel", 1)
        collected.append((moving, distance))
    return collected


def general_shards(tokens, gate_weight, up_weight, gate_mask, up_mask):
    panel_count = lax.axis_size("panel")
    my_panel = lax.axis_index("panel")
    width_rows = gate_weight.shape[0]
    stacked = jnp.stack([masked_weight(gate_weight, gate_mask), masked_weight(up_weight, up_mask)])
    collected = collect_panels(stacked)
    gathered = lax.all_gather(tokens, "seq", axis=0, tiled=True)
    tile = jnp.zeros((gathered.shape[0], panel_count * width_rows), jnp.bfloat16)
    for pair, distance in collected:
        source = (my_panel - distance) % panel_count
        result = gated_block(gathered, pair[0], pair[1])
        tile = lax.dynamic_update_slice_in_dim(tile, result, source * width_rows, 1)
    return lax.all_to_all(tile, "seq", split_axis=0, concat_axis=1, tiled=True)


def kernel(
    tok, gw, uw, gm, um, out,
    held, w, masks, wide, hid,
    total, recv_sem, send_sem, part_send, part_recv, local_sem, out_send, out_recv, out_local,
):
    rows, width = tok.shape
    wrows = gw.shape[0]
    seq, panel = lax.axis_index("seq"), lax.axis_index("panel")
    z, x = seq // 2, seq % 2
    y, core = panel // 2, panel % 2

    def device(bz, bx, by):
        return (bz * 2 + bx, by * 2 + core)

    low = z < NZ // 2
    toward = jnp.where(low, 1, -1)
    at_end = jnp.logical_or(z == 0, z == NZ - 1)

    def plane_z(p):
        return jnp.where(low, p, NZ - 1 - p)

    xdev, ydev = device(z, 1 - x, y), device(z, x, 1 - y)
    inward, outward = device(z + toward, x, y), device(z - toward, x, y)
    partner = (seq, y * 2 + 1 - core)

    barrier = pltpu.get_barrier_semaphore()
    for dev in (xdev, ydev, partner, inward):
        pl.semaphore_signal(barrier, inc=1, device_id=dev, device_id_type=MESH)

    @pl.when(jnp.logical_not(at_end))
    def _():
        pl.semaphore_signal(barrier, inc=1, device_id=outward, device_id_type=MESH)

    def slot(p, b):
        return pl.ds((p * 4 + b) * rows, rows) if b < 4 else pl.ds(p * 4 * rows, 4 * rows)

    own = pl.ds(pl.multiple_of(core * wrows, wrows), wrows)
    own_up = pl.ds(pl.multiple_of((2 + core) * wrows, wrows), wrows)
    weight_parts = (
        (gw, w.at[own]), (uw, w.at[own_up]), (gm, masks.at[core]), (um, masks.at[2 + core]),
    )
    keep_tokens = [
        pltpu.make_async_copy(tok, held.at[slot(q, 0)], local_sem.at[2]) for q in range(2)
    ]
    when_q = (at_end, jnp.logical_not(at_end))
    for q in range(2):
        pl.when(when_q[q])(keep_tokens[q].start)
    pl.semaphore_wait(barrier, jnp.where(at_end, 4, 5))
    pltpu.make_async_copy(tok, held.at[slot(0, 0)], local_sem.at[2]).wait()

    unit = width // 64

    def cols(k):
        return pl.ds(PIECES[k][0] * unit, PIECES[k][1] * unit)

    def arrival(q, p, k, b):
        last_hop = b in ((1, 2), (2, 3))[PIECES[k][2]]
        return ARRIVALS[q].index((p, k, 5 if last_hop else b))

    half = 2 * wrows

    def out_cols(bz, bx, by):
        block = (bz * 2 + bx) * 2 + by
        return pl.ds(pl.multiple_of(block * half, half), half)

    def relative(b):
        return (x + (b in (1, 2))) % 2, (y + (b in (2, 3))) % 2

    swaps = [
        pltpu.make_async_remote_copy(
            src_ref=src, dst_ref=dst, send_sem=part_send.at[i // 2], recv_sem=part_recv.at[i // 2],
            device_id=partner, device_id_type=MESH,
        )
        for i, (src, dst) in enumerate(weight_parts)
    ]

    def prune(i, state):
        if i == 0:
            for j, ref in enumerate((w.at[pl.ds(0, half)], masks.at[pl.ds(0, 2)])):
                for sem in (local_sem, part_send, part_recv):
                    pltpu.make_async_copy(ref, ref, sem.at[j]).wait()
            row = lax.broadcasted_iota(jnp.int32, (8, masks.shape[2]), 0)
            table = jnp.zeros((8, masks.shape[2]), jnp.float32)
            for r in range(4):
                table = jnp.where(row == r, masks[r].astype(jnp.float32), table)
            state["table"] = table.astype(jnp.bfloat16)
        step = width // PRUNES
        block = width // masks.shape[2]
        start = i * step
        where_ = lax.broadcasted_iota(jnp.int32, (masks.shape[2], step), 0)
        col = lax.broadcasted_iota(jnp.int32, (masks.shape[2], step), 1) + start
        first = where_ * block
        inside = jnp.logical_and(col >= first, col < first + block)
        select = jnp.where(inside, 1.0, 0.0).astype(jnp.bfloat16)
        wide[...] = jnp.dot(state["table"], select, preferred_element_type=jnp.float32)
        for r in range(4):
            at = (pl.ds(r * wrows, wrows), pl.ds(start, step))
            keep = jnp.broadcast_to(wide[r:r + 1, :], (wrows, step))
            w[at] = (w[at].astype(jnp.float32) * keep).astype(jnp.bfloat16)

    def program(q, table):
        links = (xdev, ydev, inward if q == 0 else outward, inward)
        sends, state = [], {}

        def finish(p, both):
            gate = both[:, :half]
            hid[slot(p, 4), :] = (gate / (1.0 + jnp.exp(-gate)) * both[:, half:]).astype(jnp.bfloat16)
            for b in (2, 1, 3, 0):
                if (p, b) == (q, 0):
                    state["kept_out"] = pltpu.make_async_copy(
                        hid.at[slot(p, 0)], out.at[:, out_cols(z, x, y)], out_local
                    )
                    state["kept_out"].start()
                    continue
                tx, ty = relative(b)
                pltpu.make_async_remote_copy(
                    src_ref=hid.at[slot(p, b)], dst_ref=out.at[:, out_cols(z, x, y)],
                    send_sem=out_send, recv_sem=out_recv,
                    device_id=device(plane_z(p), tx, ty), device_id_type=MESH,
                ).start()

        def multiply(p, k):
            at = slot(p, 4)
            both = lax.dot_general(
                held[at, cols(k)], w[:, cols(k)], (((1,), (1,)), ((), ())), preferred_element_type=jnp.float32
            )
            done = state.get(p, 0)
            if done:
                both = both + total[at, :]
            state[p] = done + 1
            if done + 1 < len(PIECES):
                total[at, :] = both
            else:
                finish(p, both)

        for op in table:
            if op[0] == 0:
                _, link, p, k, src, p2, dst = op
                q2 = 1 - q if link == 2 else q
                source = held.at[slot(p, src), cols(k)]
                copy = pltpu.make_async_remote_copy(
                    src_ref=source, dst_ref=held.at[slot(p2, dst), cols(k)],
                    send_sem=send_sem.at[GROUPS[q][len(sends)]], recv_sem=recv_sem.at[arrival(q2, p2, k, dst)],
                    device_id=links[link], device_id_type=MESH,
                )
                copy.start()
                sends.append(op)
            elif op[0] == 1:
                _, p, k, b = op
                at = slot(p, b) if b < 5 else pl.ds((p * 4 + 1 + PIECES[k][2]) * rows, 2 * rows)
                ref = held.at[at, cols(k)]
                pltpu.make_async_copy(ref, ref, recv_sem.at[ARRIVALS[q].index((p, k, b))]).wait()
            elif op[0] == 2:
                multiply(op[1], op[2])
            elif op[0] == 3:
                prune(op[1], state)
            else:
                for copy in swaps:
                    copy.start()
                for i, (src, dst) in enumerate(weight_parts):
                    pltpu.make_async_copy(src, dst, local_sem.at[i // 2]).start()
        for group, (high, wide_) in enumerate(SHAPES[q]):
            ref = held.at[pl.ds(0, high * rows), pl.ds(0, wide_ * unit)]
            pltpu.make_async_copy(ref, ref, send_sem.at[group]).wait()
        others = 4 * NZ - 1
        ref = hid.at[pl.ds(0, others * rows)]
        pltpu.make_async_copy(ref, ref, out_send).wait()
        state["kept_out"].wait()
        ref = out.at[:, pl.ds(0, others * half)]
        pltpu.make_async_copy(ref, ref, out_recv).wait()

    for q in range(2):
        pl.when(when_q[q])(functools.partial(program, q, ORDERS[q]))


def shards(tokens, gate_weight, up_weight, gate_mask, up_mask):
    rows, width = tokens.shape
    wrows = gate_weight.shape[0]
    blocks = lax.axis_size("seq") * lax.axis_size("panel") // 2
    hidden = lax.axis_size("seq") * lax.axis_size("panel") * wrows
    dma = pltpu.SemaphoreType.DMA
    return pl.pallas_call(
        kernel,
        out_shape=pltpu.VMEM((rows, hidden), jnp.bfloat16),
        in_specs=[pl.BlockSpec(memory_space=pl.ANY)] * 5,
        out_specs=pl.BlockSpec(memory_space=pltpu.VMEM),
        scratch_shapes=[
            pltpu.VMEM((blocks * rows, width), jnp.bfloat16),
            pltpu.VMEM((4 * wrows, width), jnp.bfloat16),
            pltpu.VMEM((4, 1, gate_mask.shape[1]), jnp.int32),
            pltpu.VMEM((8, width // PRUNES), jnp.float32),
            pltpu.VMEM((blocks * rows, 2 * wrows), jnp.bfloat16),
            pltpu.VMEM((blocks * rows, 4 * wrows), jnp.float32),
            dma((max(map(len, ARRIVALS)),)), dma((max(map(len, SHAPES)),)),
            dma((2,)), dma((2,)), dma((3,)), dma, dma, dma,
        ],
        compiler_params=pltpu.CompilerParams(collective_id=0, has_side_effects=True),
    )(tokens, gate_weight, up_weight, gate_mask, up_mask)


def solution(mesh):
    spec = P(("seq", "panel"), None)
    fits = mesh.shape["seq"] == 2 * NZ and mesh.shape["panel"] == 4
    body = shards if fits else general_shards
    return jax.shard_map(
        body, mesh=mesh, in_specs=(spec,) * 5, out_specs=spec, check_vma=False
    )
```

```python
import functools

import jax
import jax.numpy as jnp
from jax import lax
from jax.experimental import pallas as pl
from jax.experimental.pallas import tpu as pltpu
from jax.sharding import PartitionSpec as P

MESH = pl.DeviceIdType.MESH
NZ = 4
PRUNES = 16
PIECES = ((0, 13, 1), (13, 12, 1), (25, 13, 0), (38, 12, 0), (50, 4, 1), (54, 3, 1), (57, 4, 0), (61, 3, 0))
ORDERS = ((
    (0, 0, 0, 0, 0, 0, 1), (0, 0, 0, 1, 0, 0, 1), (0, 1, 0, 0, 0, 0, 3), (0, 1, 0, 6, 0, 0, 3), (0, 2, 0, 0, 0, 0, 0),
    (0, 2, 0, 1, 0, 0, 0), (0, 1, 0, 7, 0, 0, 3), (0, 1, 0, 2, 0, 0, 3), (4, 0), (0, 0, 0, 2, 0, 0, 1),
    (0, 2, 0, 2, 0, 0, 0), (0, 1, 0, 1, 0, 0, 3), (0, 0, 0, 3, 0, 0, 1), (0, 2, 0, 3, 0, 0, 0), (0, 1, 0, 3, 0, 0, 3),
    (1, 1, 3, 0), (1, 0, 0, 1), (0, 0, 0, 4, 0, 0, 1), (1, 0, 6, 3), (0, 0, 0, 5, 0, 0, 1), (1, 0, 7, 3),
    (0, 1, 0, 5, 0, 0, 3), (0, 0, 0, 6, 0, 0, 1), (0, 1, 0, 4, 0, 0, 3), (1, 0, 1, 1), (1, 1, 0, 0),
    (0, 0, 0, 7, 0, 0, 1), (0, 1, 0, 0, 1, 0, 2), (0, 0, 0, 7, 3, 0, 2), (3, 0), (0, 0, 0, 6, 3, 0, 2), (1, 0, 2, 3),
    (3, 1), (0, 0, 0, 2, 3, 0, 2), (3, 2), (1, 1, 1, 0), (3, 3), (0, 1, 1, 1, 0, 1, 3), (3, 4), (3, 5),
    (0, 0, 1, 3, 0, 1, 1), (1, 1, 2, 0), (3, 6), (0, 1, 0, 1, 1, 0, 2), (1, 0, 4, 1), (3, 7), (1, 0, 3, 3),
    (1, 0, 5, 1), (3, 8), (0, 0, 0, 3, 3, 0, 2), (1, 2, 0, 0), (3, 9), (0, 1, 0, 4, 1, 0, 2), (1, 0, 7, 5),
    (0, 2, 0, 7, 4, 0, 4), (3, 10), (0, 1, 0, 5, 1, 0, 2), (3, 11), (1, 0, 6, 5), (0, 2, 0, 6, 4, 0, 4),
    (0, 0, 2, 0, 0, 2, 1), (0, 1, 2, 0, 0, 2, 3), (3, 12), (1, 2, 2, 0), (1, 0, 0, 5), (3, 13), (3, 14), (1, 0, 2, 5),
    (0, 0, 2, 2, 0, 2, 1), (0, 1, 2, 2, 0, 2, 3), (3, 15), (1, 2, 3, 0), (2, 0, 7), (2, 0, 6), (2, 0, 0),
    (0, 0, 2, 3, 0, 2, 1), (0, 1, 2, 3, 0, 2, 3), (2, 0, 2), (1, 2, 1, 0), (1, 0, 1, 5), (2, 0, 1), (1, 0, 4, 5),
    (0, 2, 0, 4, 4, 0, 4), (2, 0, 4), (1, 0, 3, 5), (1, 0, 5, 5), (0, 2, 0, 5, 4, 0, 4), (2, 0, 3),
    (0, 0, 2, 1, 0, 2, 1), (0, 1, 2, 1, 0, 2, 3), (1, 3, 0, 0), (2, 0, 5), (1, 2, 0, 1), (0, 0, 3, 0, 0, 3, 1),
    (0, 1, 2, 0, 1, 2, 2), (1, 3, 1, 0), (1, 2, 2, 3), (0, 0, 2, 2, 3, 2, 2), (0, 1, 3, 0, 0, 3, 3), (1, 3, 2, 0),
    (1, 2, 3, 3), (0, 0, 2, 3, 3, 2, 2), (0, 1, 3, 2, 0, 3, 3), (1, 1, 4, 4), (2, 1, 4), (1, 2, 1, 1),
    (0, 0, 3, 1, 0, 3, 1), (0, 1, 2, 1, 1, 2, 2), (1, 3, 3, 0), (1, 3, 0, 1), (1, 2, 0, 5), (2, 2, 0),
    (0, 0, 3, 3, 0, 3, 1), (0, 1, 3, 3, 0, 3, 3), (1, 2, 5, 4), (2, 2, 5), (1, 2, 2, 5), (2, 2, 2),
    (0, 0, 3, 2, 0, 3, 1), (0, 1, 3, 1, 0, 3, 3), (1, 2, 6, 4), (2, 2, 6), (1, 2, 3, 5), (1, 3, 2, 3), (2, 2, 3),
    (0, 0, 3, 2, 3, 3, 2), (0, 1, 3, 0, 1, 3, 2), (1, 3, 1, 1), (1, 2, 1, 5), (2, 2, 1), (1, 2, 4, 4),
    (0, 0, 1, 0, 0, 1, 1), (0, 1, 3, 1, 1, 3, 2), (2, 2, 4), (1, 3, 3, 3), (1, 2, 7, 4), (2, 2, 7),
    (0, 1, 1, 2, 0, 1, 3), (0, 0, 3, 3, 3, 3, 2), (1, 3, 7, 4), (2, 3, 7), (0, 1, 1, 3, 0, 1, 3),
    (0, 0, 1, 1, 0, 1, 1), (1, 3, 2, 5), (1, 3, 0, 5), (2, 3, 0), (0, 1, 1, 0, 0, 1, 3), (0, 0, 1, 2, 0, 1, 1),
    (2, 3, 2), (1, 3, 6, 4), (2, 3, 6), (1, 3, 1, 5), (2, 3, 1), (1, 1, 0, 1), (0, 1, 1, 0, 1, 1, 2), (1, 3, 5, 4),
    (2, 3, 5), (1, 1, 2, 3), (1, 3, 3, 5), (0, 0, 1, 2, 3, 1, 2), (2, 3, 3), (1, 3, 4, 4), (2, 3, 4), (1, 1, 3, 3),
    (1, 1, 1, 1), (0, 0, 1, 3, 3, 1, 2), (0, 1, 1, 1, 1, 1, 2), (1, 1, 5, 4), (2, 1, 5), (1, 1, 6, 4), (2, 1, 6),
    (1, 1, 0, 5), (1, 1, 2, 5), (2, 1, 0), (2, 1, 2), (1, 1, 7, 4), (2, 1, 7), (1, 1, 3, 5), (1, 1, 1, 5), (2, 1, 3),
    (2, 1, 1),
), (
    (0, 0, 1, 5, 0, 1, 1), (0, 0, 1, 6, 0, 1, 1), (0, 0, 1, 7, 0, 1, 1), (0, 0, 1, 0, 0, 1, 1), (0, 1, 1, 5, 0, 1, 3),
    (0, 1, 1, 6, 0, 1, 3), (0, 1, 1, 1, 0, 1, 3), (0, 2, 1, 3, 0, 1, 0), (0, 2, 1, 0, 0, 1, 0), (0, 3, 1, 0, 0, 2, 0),
    (0, 3, 1, 2, 0, 2, 0), (0, 1, 1, 0, 0, 1, 3), (0, 0, 1, 4, 0, 1, 1), (4, 0), (0, 2, 1, 1, 0, 1, 0),
    (0, 3, 1, 3, 0, 2, 0), (0, 0, 1, 2, 0, 1, 1), (0, 1, 1, 3, 0, 1, 3), (0, 2, 1, 2, 0, 1, 0), (0, 3, 1, 1, 0, 2, 0),
    (1, 1, 5, 1), (0, 0, 1, 1, 0, 1, 1), (1, 1, 6, 3), (0, 1, 1, 2, 0, 1, 3), (1, 0, 0, 0), (1, 2, 0, 0),
    (0, 3, 0, 0, 0, 3, 0), (0, 2, 2, 0, 0, 2, 0), (0, 0, 1, 6, 3, 1, 2), (0, 0, 0, 0, 0, 0, 1), (0, 1, 1, 4, 0, 1, 3),
    (1, 1, 0, 1), (1, 0, 1, 0), (0, 1, 1, 5, 1, 1, 2), (1, 2, 2, 0), (1, 1, 4, 1), (0, 3, 0, 1, 0, 3, 0),
    (0, 2, 2, 2, 0, 2, 0), (0, 1, 1, 7, 0, 1, 3), (3, 0), (0, 1, 1, 0, 1, 1, 2), (3, 1), (0, 0, 1, 3, 0, 1, 1),
    (3, 2), (1, 0, 2, 0), (1, 2, 3, 0), (0, 3, 0, 2, 0, 3, 0), (3, 3), (0, 2, 2, 3, 0, 2, 0), (1, 1, 3, 3), (3, 4),
    (0, 1, 0, 2, 0, 0, 3), (0, 0, 1, 3, 3, 1, 2), (3, 5), (1, 0, 3, 0), (1, 2, 1, 0), (1, 1, 1, 1), (3, 6),
    (0, 3, 0, 3, 0, 3, 0), (0, 2, 2, 1, 0, 2, 0), (3, 7), (1, 1, 6, 5), (1, 1, 2, 3), (0, 1, 1, 4, 1, 1, 2),
    (0, 0, 1, 2, 3, 1, 2), (3, 8), (0, 1, 1, 1, 1, 1, 2), (1, 3, 0, 0), (3, 9), (1, 1, 5, 5), (0, 2, 3, 0, 0, 3, 0),
    (0, 3, 1, 5, 4, 2, 4), (1, 1, 7, 3), (3, 10), (1, 0, 0, 1), (0, 0, 1, 7, 3, 1, 2), (3, 11), (0, 1, 3, 0, 0, 3, 3),
    (0, 0, 0, 3, 0, 0, 1), (3, 12), (1, 3, 1, 0), (0, 3, 1, 6, 4, 2, 4), (0, 2, 3, 1, 0, 3, 0), (3, 13), (1, 1, 0, 5),
    (3, 14), (0, 0, 3, 1, 0, 3, 1), (3, 15), (0, 1, 3, 1, 0, 3, 3), (1, 3, 2, 0), (2, 1, 6), (0, 2, 3, 2, 0, 3, 0),
    (2, 1, 5), (1, 0, 2, 3), (1, 1, 3, 5), (2, 1, 0), (1, 1, 4, 5), (0, 3, 1, 4, 4, 2, 4), (0, 0, 3, 0, 0, 3, 1),
    (0, 1, 0, 0, 1, 0, 2), (2, 1, 3), (1, 3, 3, 0), (1, 0, 7, 4), (0, 2, 1, 4, 4, 1, 4), (2, 1, 4), (1, 1, 2, 5),
    (2, 0, 7), (0, 3, 0, 7, 4, 3, 4), (1, 1, 1, 5), (1, 1, 7, 5), (2, 1, 2), (0, 0, 3, 3, 0, 3, 1),
    (0, 1, 3, 3, 0, 3, 3), (1, 2, 5, 4), (2, 1, 1), (1, 0, 6, 4), (2, 1, 7), (0, 2, 3, 3, 0, 3, 0), (2, 2, 5),
    (0, 3, 1, 7, 4, 2, 4), (0, 0, 3, 2, 0, 3, 1), (2, 0, 6), (0, 1, 3, 2, 0, 3, 3), (1, 2, 6, 4), (2, 2, 6),
    (0, 2, 2, 5, 4, 2, 4), (0, 3, 0, 6, 4, 3, 4), (1, 3, 1, 1), (0, 0, 0, 2, 3, 0, 2), (0, 1, 0, 3, 0, 0, 3),
    (1, 0, 4, 4), (2, 0, 4), (0, 2, 2, 6, 4, 2, 4), (1, 2, 4, 4), (2, 2, 4), (1, 3, 0, 1), (0, 0, 0, 1, 0, 0, 1),
    (0, 1, 3, 0, 1, 3, 2), (0, 3, 0, 4, 4, 3, 4), (1, 0, 5, 4), (2, 0, 5), (1, 3, 7, 4), (2, 3, 7),
    (0, 2, 2, 4, 4, 2, 4), (1, 3, 3, 3), (0, 0, 3, 3, 3, 3, 2), (0, 1, 3, 1, 1, 3, 2), (0, 3, 0, 5, 4, 3, 4),
    (1, 2, 7, 4), (2, 2, 7), (1, 3, 2, 3), (0, 0, 3, 2, 3, 3, 2), (0, 1, 2, 2, 0, 2, 3), (0, 2, 2, 7, 4, 2, 4),
    (1, 3, 6, 4), (1, 0, 3, 3), (2, 3, 6), (0, 0, 0, 3, 3, 0, 2), (0, 1, 0, 0, 0, 0, 3), (0, 2, 3, 7, 4, 3, 4),
    (1, 0, 1, 1), (1, 3, 0, 5), (2, 3, 0), (0, 0, 2, 1, 0, 2, 1), (0, 2, 3, 6, 4, 3, 4), (0, 1, 0, 1, 1, 0, 2),
    (1, 3, 4, 4), (2, 3, 4), (1, 3, 3, 5), (2, 3, 3), (1, 3, 1, 5), (0, 0, 0, 2, 0, 0, 1), (2, 3, 1),
    (0, 1, 0, 1, 0, 0, 3), (1, 3, 5, 4), (2, 3, 5), (0, 2, 3, 5, 4, 3, 4), (1, 3, 2, 5), (2, 3, 2), (1, 2, 2, 3),
    (0, 0, 2, 0, 0, 2, 1), (0, 1, 2, 3, 0, 2, 3), (0, 2, 3, 4, 4, 3, 4), (1, 0, 3, 5), (2, 0, 3), (1, 0, 0, 5),
    (0, 0, 2, 2, 0, 2, 1), (0, 1, 2, 1, 0, 2, 3), (2, 0, 0), (0, 2, 1, 5, 4, 1, 4), (1, 2, 1, 1),
    (0, 1, 2, 1, 1, 2, 2), (0, 0, 2, 2, 3, 2, 2), (0, 2, 1, 6, 4, 1, 4), (1, 0, 2, 5), (2, 0, 2), (1, 0, 1, 5),
    (0, 1, 2, 0, 0, 2, 3), (2, 0, 1), (0, 0, 2, 3, 0, 2, 1), (0, 2, 1, 7, 4, 1, 4), (1, 2, 0, 1), (1, 2, 3, 3),
    (0, 1, 2, 0, 1, 2, 2), (0, 0, 2, 3, 3, 2, 2), (1, 2, 1, 5), (2, 2, 1), (1, 2, 2, 5), (2, 2, 2), (1, 2, 0, 5),
    (1, 2, 3, 5), (2, 2, 0), (2, 2, 3),
))
GROUPS = ((0, 0, 0, 0, 0, 0, 0, 0, 0, 0, 0, 0, 0, 0, 0, 0, 0, 0, 0, 0, 0, 0, 0, 0, 0, 0, 0, 0, 0, 0, 0, 0, 0, 0, 0, 0, 0, 0, 0, 0, 0, 0, 0, 0, 0, 0, 0, 0, 0, 0, 0, 0, 0, 0, 0, 0, 0, 0, 0, 0, 0, 0, 0, 0, 0, 0, 0, 1), (0, 0, 0, 0, 0, 0, 0, 0, 0, 0, 0, 0, 0, 0, 0, 0, 0, 0, 0, 0, 0, 0, 0, 0, 0, 0, 0, 0, 0, 0, 0, 0, 0, 0, 0, 0, 0, 0, 0, 0, 0, 0, 0, 0, 0, 0, 0, 0, 1, 1, 1, 1, 1, 1, 1, 1, 1, 1, 1, 1, 1, 1, 1, 1, 1, 1, 1, 1, 1, 1, 1, 1, 1, 1, 1, 1, 1, 1, 1, 1, 1, 1, 1, 1, 1, 1, 1, 1, 1, 1, 1, 1, 1, 1, 1, 1, 1, 1, 1, 1))
SHAPES = (((16, 46), (12, 1)), ((16, 31), (13, 52)))
ARRIVALS = tuple(tuple(op[1:] for op in order if op[0] == 1) for order in ORDERS)
ARRIVAL_SEMS = ((0, 1, 2, 3, 4, 5, 6, 7, 8, 9, 10, 11, 12, 13, 14, 15, 16, 17, 18, 19, 20, 21, 22, 23, 24, 4, 25, 0, 26, 2, 12, 6, 14, 8, 27, 11, 5, 18, 1, 7, 16, 10, 20, 24, 19, 23, 25, 15, 9, 13, 12, 17, 14, 4, 21, 6, 2, 3, 22, 26, 0, 28, 29, 30), (0, 1, 2, 3, 4, 5, 6, 7, 8, 9, 10, 11, 12, 13, 14, 15, 16, 17, 18, 19, 20, 21, 22, 23, 24, 25, 26, 0, 27, 28, 29, 3, 2, 7, 1, 10, 9, 8, 12, 11, 14, 16, 13, 20, 15, 23, 6, 25, 19, 5, 27, 17, 2, 30, 4, 3, 21, 29, 28, 0, 26, 24, 22, 18))


def passed_along(block, axis, distance):
    devices = range(lax.axis_size(axis))
    route = [((i - distance) % len(devices), i) for i in devices]
    return lax.ppermute(block, axis, route)


def masked_weight(weight, mask):
    row_blocks, col_blocks = mask.shape
    shaped = weight.reshape(
        row_blocks, weight.shape[0] // row_blocks, col_blocks, weight.shape[1] // col_blocks
    )
    return (shaped * mask.astype(jnp.bfloat16)[:, None, :, None]).reshape(weight.shape)


def project(token_rows, weight):
    return lax.dot_general(
        token_rows, weight, (((1,), (1,)), ((), ())), preferred_element_type=jnp.float32
    )


def gated_block(token_rows, gate_part, up_part):
    gate = project(token_rows, gate_part)
    up_values = project(token_rows, up_part)
    return (jax.nn.silu(gate) * up_values).astype(jnp.bfloat16)


def collect_panels(stacked):
    panel_count = lax.axis_size("panel")
    collected = [(stacked, 0)]
    moving = stacked
    for distance in range(1, panel_count):
        moving = passed_along(moving, "panel", 1)
        collected.append((moving, distance))
    return collected


def general_shards(tokens, gate_weight, up_weight, gate_mask, up_mask):
    panel_count = lax.axis_size("panel")
    my_panel = lax.axis_index("panel")
    width_rows = gate_weight.shape[0]
    stacked = jnp.stack([masked_weight(gate_weight, gate_mask), masked_weight(up_weight, up_mask)])
    collected = collect_panels(stacked)
    gathered = lax.all_gather(tokens, "seq", axis=0, tiled=True)
    tile = jnp.zeros((gathered.shape[0], panel_count * width_rows), jnp.bfloat16)
    for pair, distance in collected:
        source = (my_panel - distance) % panel_count
        result = gated_block(gathered, pair[0], pair[1])
        tile = lax.dynamic_update_slice_in_dim(tile, result, source * width_rows, 1)
    return lax.all_to_all(tile, "seq", split_axis=0, concat_axis=1, tiled=True)


def kernel(
    tok, gw, uw, gm, um, out,
    held, w, masks, wide, hid,
    total, recv_sem, send_sem, part_send, part_recv, local_sem, out_send, out_recv, out_local,
):
    rows, width = tok.shape
    wrows = gw.shape[0]
    seq, panel = lax.axis_index("seq"), lax.axis_index("panel")
    z, x = seq // 2, seq % 2
    y, core = panel // 2, panel % 2

    def device(bz, bx, by):
        return (bz * 2 + bx, by * 2 + core)

    low = z < NZ // 2
    toward = jnp.where(low, 1, -1)
    at_end = jnp.logical_or(z == 0, z == NZ - 1)

    def plane_z(p):
        return jnp.where(low, p, NZ - 1 - p)

    xdev, ydev = device(z, 1 - x, y), device(z, x, 1 - y)
    inward, outward = device(z + toward, x, y), device(z - toward, x, y)
    partner = (seq, y * 2 + 1 - core)

    barrier = pltpu.get_barrier_semaphore()
    for dev in (xdev, ydev, partner, inward):
        pl.semaphore_signal(barrier, inc=1, device_id=dev, device_id_type=MESH)

    @pl.when(jnp.logical_not(at_end))
    def _():
        pl.semaphore_signal(barrier, inc=1, device_id=outward, device_id_type=MESH)

    def slot(p, b):
        return pl.ds((p * 4 + b) * rows, rows) if b < 4 else pl.ds(p * 4 * rows, 4 * rows)

    own = pl.ds(pl.multiple_of(core * wrows, wrows), wrows)
    own_up = pl.ds(pl.multiple_of((2 + core) * wrows, wrows), wrows)
    weight_parts = (
        (gw, w.at[own]), (uw, w.at[own_up]), (gm, masks.at[core]), (um, masks.at[2 + core]),
    )
    keep_tokens = [
        pltpu.make_async_copy(tok, held.at[slot(q, 0)], local_sem.at[2]) for q in range(2)
    ]
    when_q = (at_end, jnp.logical_not(at_end))
    for q in range(2):
        pl.when(when_q[q])(keep_tokens[q].start)
    pl.semaphore_wait(barrier, jnp.where(at_end, 4, 5))
    pltpu.make_async_copy(tok, held.at[slot(0, 0)], local_sem.at[2]).wait()

    unit = width // 64

    def cols(k):
        return pl.ds(PIECES[k][0] * unit, PIECES[k][1] * unit)

    def arrival(q, p, k, b):
        last_hop = b in ((1, 2), (2, 3))[PIECES[k][2]]
        return ARRIVAL_SEMS[q][ARRIVALS[q].index((p, k, 5 if last_hop else b))]

    half = 2 * wrows

    def out_cols(bz, bx, by):
        block = (bz * 2 + bx) * 2 + by
        return pl.ds(pl.multiple_of(block * half, half), half)

    def relative(b):
        return (x + (b in (1, 2))) % 2, (y + (b in (2, 3))) % 2

    swaps = [
        pltpu.make_async_remote_copy(
            src_ref=src, dst_ref=dst, send_sem=part_send.at[i // 2], recv_sem=part_recv.at[i // 2],
            device_id=partner, device_id_type=MESH,
        )
        for i, (src, dst) in enumerate(weight_parts)
    ]

    def prune(i, state):
        if i == 0:
            for j, ref in enumerate((w.at[pl.ds(0, half)], masks.at[pl.ds(0, 2)])):
                for sem in (local_sem, part_send, part_recv):
                    pltpu.make_async_copy(ref, ref, sem.at[j]).wait()
            row = lax.broadcasted_iota(jnp.int32, (8, masks.shape[2]), 0)
            table = jnp.zeros((8, masks.shape[2]), jnp.float32)
            for r in range(4):
                table = jnp.where(row == r, masks[r].astype(jnp.float32), table)
            state["table"] = table.astype(jnp.bfloat16)
        step = width // PRUNES
        block = width // masks.shape[2]
        start = i * step
        where_ = lax.broadcasted_iota(jnp.int32, (masks.shape[2], step), 0)
        col = lax.broadcasted_iota(jnp.int32, (masks.shape[2], step), 1) + start
        first = where_ * block
        inside = jnp.logical_and(col >= first, col < first + block)
        select = jnp.where(inside, 1.0, 0.0).astype(jnp.bfloat16)
        wide[...] = jnp.dot(state["table"], select, preferred_element_type=jnp.float32)
        for r in range(4):
            at = (pl.ds(r * wrows, wrows), pl.ds(start, step))
            keep = jnp.broadcast_to(wide[r:r + 1, :], (wrows, step))
            w[at] = (w[at].astype(jnp.float32) * keep).astype(jnp.bfloat16)

    def program(q, table):
        links = (xdev, ydev, inward if q == 0 else outward, inward)
        sends, state = [], {}

        def finish(p, both):
            gate = both[:, :half]
            hid[slot(p, 4), :] = (gate / (1.0 + jnp.exp(-gate)) * both[:, half:]).astype(jnp.bfloat16)
            for b in (2, 1, 3, 0):
                if (p, b) == (q, 0):
                    state["kept_out"] = pltpu.make_async_copy(
                        hid.at[slot(p, 0)], out.at[:, out_cols(z, x, y)], out_local
                    )
                    state["kept_out"].start()
                    continue
                tx, ty = relative(b)
                pltpu.make_async_remote_copy(
                    src_ref=hid.at[slot(p, b)], dst_ref=out.at[:, out_cols(z, x, y)],
                    send_sem=out_send, recv_sem=out_recv,
                    device_id=device(plane_z(p), tx, ty), device_id_type=MESH,
                ).start()

        def multiply(p, k):
            at = slot(p, 4)
            both = lax.dot_general(
                held[at, cols(k)], w[:, cols(k)], (((1,), (1,)), ((), ())), preferred_element_type=jnp.float32
            )
            done = state.get(p, 0)
            if done:
                both = both + total[at, :]
            state[p] = done + 1
            if done + 1 < len(PIECES):
                total[at, :] = both
            else:
                finish(p, both)

        for op in table:
            if op[0] == 0:
                _, link, p, k, src, p2, dst = op
                q2 = 1 - q if link == 2 else q
                source = held.at[slot(p, src), cols(k)]
                copy = pltpu.make_async_remote_copy(
                    src_ref=source, dst_ref=held.at[slot(p2, dst), cols(k)],
                    send_sem=send_sem.at[GROUPS[q][len(sends)]], recv_sem=recv_sem.at[arrival(q2, p2, k, dst)],
                    device_id=links[link], device_id_type=MESH,
                )
                copy.start()
                sends.append(op)
            elif op[0] == 1:
                _, p, k, b = op
                at = slot(p, b) if b < 5 else pl.ds((p * 4 + 1 + PIECES[k][2]) * rows, 2 * rows)
                ref = held.at[at, cols(k)]
                pltpu.make_async_copy(ref, ref, recv_sem.at[ARRIVAL_SEMS[q][ARRIVALS[q].index((p, k, b))]]).wait()
            elif op[0] == 2:
                multiply(op[1], op[2])
            elif op[0] == 3:
                prune(op[1], state)
            else:
                for copy in swaps:
                    copy.start()
                for i, (src, dst) in enumerate(weight_parts):
                    pltpu.make_async_copy(src, dst, local_sem.at[i // 2]).start()
        for group, (high, wide_) in enumerate(SHAPES[q]):
            ref = held.at[pl.ds(0, high * rows), pl.ds(0, wide_ * unit)]
            pltpu.make_async_copy(ref, ref, send_sem.at[group]).wait()
        others = 4 * NZ - 1
        ref = hid.at[pl.ds(0, others * rows)]
        pltpu.make_async_copy(ref, ref, out_send).wait()
        state["kept_out"].wait()
        ref = out.at[:, pl.ds(0, others * half)]
        pltpu.make_async_copy(ref, ref, out_recv).wait()

    for q in range(2):
        pl.when(when_q[q])(functools.partial(program, q, ORDERS[q]))


def shards(tokens, gate_weight, up_weight, gate_mask, up_mask):
    rows, width = tokens.shape
    wrows = gate_weight.shape[0]
    blocks = lax.axis_size("seq") * lax.axis_size("panel") // 2
    hidden = lax.axis_size("seq") * lax.axis_size("panel") * wrows
    dma = pltpu.SemaphoreType.DMA
    return pl.pallas_call(
        kernel,
        out_shape=pltpu.VMEM((rows, hidden), jnp.bfloat16),
        in_specs=[pl.BlockSpec(memory_space=pl.ANY)] * 5,
        out_specs=pl.BlockSpec(memory_space=pltpu.VMEM),
        scratch_shapes=[
            pltpu.VMEM((blocks * rows, width), jnp.bfloat16),
            pltpu.VMEM((4 * wrows, width), jnp.bfloat16),
            pltpu.VMEM((4, 1, gate_mask.shape[1]), jnp.int32),
            pltpu.VMEM((8, width // PRUNES), jnp.float32),
            pltpu.VMEM((blocks * rows, 2 * wrows), jnp.bfloat16),
            pltpu.VMEM((blocks * rows, 4 * wrows), jnp.float32),
            dma((1 + max(map(max, ARRIVAL_SEMS)),)), dma((max(map(len, SHAPES)),)),
            dma((2,)), dma((2,)), dma((3,)), dma, dma, dma,
        ],
        compiler_params=pltpu.CompilerParams(collective_id=0, has_side_effects=True),
    )(tokens, gate_weight, up_weight, gate_mask, up_mask)


def solution(mesh):
    spec = P(("seq", "panel"), None)
    fits = mesh.shape["seq"] == 2 * NZ and mesh.shape["panel"] == 4
    body = shards if fits else general_shards
    return jax.shard_map(
        body, mesh=mesh, in_specs=(spec,) * 5, out_specs=spec, check_vma=False
    )
```

```python
import functools

import jax
import jax.numpy as jnp
from jax import lax
from jax.experimental import pallas as pl
from jax.experimental.pallas import tpu as pltpu
from jax.sharding import PartitionSpec as P

MESH = pl.DeviceIdType.MESH
NZ = 4
PRUNES = 32
PIECES = ((0, 13, 1), (13, 12, 1), (25, 13, 0), (38, 12, 0), (50, 4, 1), (54, 3, 1), (57, 4, 0), (61, 3, 0))
ORDERS = ((
    (0, 0, 0, 0, 0, 0, 1), (0, 0, 0, 1, 0, 0, 1), (0, 1, 0, 0, 0, 0, 3), (0, 1, 0, 6, 0, 0, 3), (0, 2, 0, 0, 0, 0, 0),
    (0, 2, 0, 1, 0, 0, 0), (0, 1, 0, 7, 0, 0, 3), (0, 1, 0, 2, 0, 0, 3), (4, 0), (0, 0, 0, 2, 0, 0, 1),
    (0, 2, 0, 2, 0, 0, 0), (0, 1, 0, 1, 0, 0, 3), (0, 0, 0, 3, 0, 0, 1), (0, 2, 0, 3, 0, 0, 0), (0, 1, 0, 3, 0, 0, 3),
    (1, 1, 3, 0), (1, 0, 0, 1), (0, 0, 0, 4, 0, 0, 1), (1, 0, 6, 3), (0, 0, 0, 5, 0, 0, 1), (1, 0, 7, 3),
    (0, 1, 0, 5, 0, 0, 3), (0, 0, 0, 6, 0, 0, 1), (3, 0), (0, 1, 0, 4, 0, 0, 3), (1, 0, 1, 1), (1, 1, 0, 0),
    (0, 0, 0, 7, 0, 0, 1), (3, 1), (3, 2), (0, 1, 0, 0, 1, 0, 2), (0, 0, 0, 7, 3, 0, 2), (3, 3),
    (0, 0, 0, 6, 3, 0, 2), (1, 0, 2, 3), (3, 4), (3, 5), (0, 0, 0, 2, 3, 0, 2), (1, 1, 1, 0), (3, 6), (3, 7),
    (0, 1, 1, 1, 0, 1, 3), (3, 8), (3, 9), (3, 10), (0, 0, 1, 3, 0, 1, 1), (3, 11), (1, 1, 2, 0), (3, 12),
    (0, 1, 0, 1, 1, 0, 2), (1, 0, 4, 1), (3, 13), (1, 0, 3, 3), (1, 0, 5, 1), (3, 14), (3, 15), (0, 0, 0, 3, 3, 0, 2),
    (3, 16), (1, 2, 0, 0), (3, 17), (0, 1, 0, 4, 1, 0, 2), (3, 18), (1, 0, 7, 5), (0, 2, 0, 7, 4, 0, 4), (3, 19),
    (0, 1, 0, 5, 1, 0, 2), (1, 0, 6, 5), (0, 2, 0, 6, 4, 0, 4), (3, 20), (0, 0, 2, 0, 0, 2, 1), (0, 1, 2, 0, 0, 2, 3),
    (3, 21), (1, 2, 2, 0), (3, 22), (1, 0, 0, 5), (3, 23), (3, 24), (3, 25), (1, 0, 2, 5), (3, 26),
    (0, 0, 2, 2, 0, 2, 1), (0, 1, 2, 2, 0, 2, 3), (3, 27), (1, 2, 3, 0), (3, 28), (3, 29), (3, 30), (3, 31),
    (0, 0, 2, 3, 0, 2, 1), (0, 1, 2, 3, 0, 2, 3), (1, 2, 1, 0), (2, 0, 7), (1, 0, 1, 5), (2, 0, 6), (1, 0, 4, 5),
    (0, 2, 0, 4, 4, 0, 4), (2, 0, 0), (1, 0, 3, 5), (1, 0, 5, 5), (0, 2, 0, 5, 4, 0, 4), (0, 0, 2, 1, 0, 2, 1),
    (0, 1, 2, 1, 0, 2, 3), (2, 0, 2), (1, 3, 0, 0), (2, 0, 1), (2, 0, 4), (1, 2, 0, 1), (2, 0, 3),
    (0, 0, 3, 0, 0, 3, 1), (0, 1, 2, 0, 1, 2, 2), (2, 0, 5), (1, 3, 1, 0), (1, 2, 2, 3), (0, 0, 2, 2, 3, 2, 2),
    (0, 1, 3, 0, 0, 3, 3), (1, 3, 2, 0), (1, 2, 3, 3), (0, 0, 2, 3, 3, 2, 2), (0, 1, 3, 2, 0, 3, 3), (1, 1, 4, 4),
    (2, 1, 4), (1, 2, 1, 1), (0, 0, 3, 1, 0, 3, 1), (0, 1, 2, 1, 1, 2, 2), (1, 3, 3, 0), (1, 3, 0, 1), (1, 2, 0, 5),
    (2, 2, 0), (0, 0, 3, 3, 0, 3, 1), (0, 1, 3, 3, 0, 3, 3), (1, 2, 5, 4), (2, 2, 5), (1, 2, 2, 5), (2, 2, 2),
    (0, 0, 3, 2, 0, 3, 1), (0, 1, 3, 1, 0, 3, 3), (1, 2, 6, 4), (2, 2, 6), (1, 2, 3, 5), (1, 3, 2, 3), (2, 2, 3),
    (0, 0, 3, 2, 3, 3, 2), (0, 1, 3, 0, 1, 3, 2), (1, 3, 1, 1), (1, 2, 1, 5), (2, 2, 1), (1, 2, 4, 4),
    (0, 0, 1, 0, 0, 1, 1), (0, 1, 3, 1, 1, 3, 2), (2, 2, 4), (1, 3, 3, 3), (1, 2, 7, 4), (2, 2, 7),
    (0, 1, 1, 2, 0, 1, 3), (0, 0, 3, 3, 3, 3, 2), (1, 3, 7, 4), (2, 3, 7), (0, 1, 1, 3, 0, 1, 3),
    (0, 0, 1, 1, 0, 1, 1), (1, 3, 2, 5), (1, 3, 0, 5), (2, 3, 0), (0, 1, 1, 0, 0, 1, 3), (0, 0, 1, 2, 0, 1, 1),
    (2, 3, 2), (1, 3, 6, 4), (2, 3, 6), (1, 3, 1, 5), (2, 3, 1), (1, 1, 0, 1), (0, 1, 1, 0, 1, 1, 2), (1, 3, 5, 4),
    (2, 3, 5), (1, 1, 2, 3), (1, 3, 3, 5), (0, 0, 1, 2, 3, 1, 2), (2, 3, 3), (1, 3, 4, 4), (2, 3, 4), (1, 1, 3, 3),
    (1, 1, 1, 1), (0, 0, 1, 3, 3, 1, 2), (0, 1, 1, 1, 1, 1, 2), (1, 1, 5, 4), (2, 1, 5), (1, 1, 6, 4), (2, 1, 6),
    (1, 1, 0, 5), (1, 1, 2, 5), (2, 1, 0), (2, 1, 2), (1, 1, 7, 4), (2, 1, 7), (1, 1, 3, 5), (1, 1, 1, 5), (2, 1, 3),
    (2, 1, 1),
), (
    (0, 0, 1, 5, 0, 1, 1), (0, 0, 1, 6, 0, 1, 1), (0, 0, 1, 7, 0, 1, 1), (0, 0, 1, 0, 0, 1, 1), (0, 1, 1, 5, 0, 1, 3),
    (0, 1, 1, 6, 0, 1, 3), (0, 1, 1, 1, 0, 1, 3), (0, 2, 1, 3, 0, 1, 0), (0, 2, 1, 0, 0, 1, 0), (0, 3, 1, 0, 0, 2, 0),
    (0, 3, 1, 2, 0, 2, 0), (0, 1, 1, 0, 0, 1, 3), (0, 0, 1, 4, 0, 1, 1), (4, 0), (0, 2, 1, 1, 0, 1, 0),
    (0, 3, 1, 3, 0, 2, 0), (0, 0, 1, 2, 0, 1, 1), (0, 1, 1, 3, 0, 1, 3), (0, 2, 1, 2, 0, 1, 0), (0, 3, 1, 1, 0, 2, 0),
    (1, 1, 5, 1), (0, 0, 1, 1, 0, 1, 1), (1, 1, 6, 3), (0, 1, 1, 2, 0, 1, 3), (1, 0, 0, 0), (1, 2, 0, 0),
    (0, 3, 0, 0, 0, 3, 0), (0, 2, 2, 0, 0, 2, 0), (0, 0, 1, 6, 3, 1, 2), (0, 0, 0, 0, 0, 0, 1), (0, 1, 1, 4, 0, 1, 3),
    (1, 1, 0, 1), (3, 0), (1, 0, 1, 0), (0, 1, 1, 5, 1, 1, 2), (1, 2, 2, 0), (3, 1), (1, 1, 4, 1),
    (0, 3, 0, 1, 0, 3, 0), (0, 2, 2, 2, 0, 2, 0), (3, 2), (0, 1, 1, 7, 0, 1, 3), (3, 3), (0, 1, 1, 0, 1, 1, 2),
    (3, 4), (0, 0, 1, 3, 0, 1, 1), (3, 5), (1, 0, 2, 0), (1, 2, 3, 0), (3, 6), (0, 3, 0, 2, 0, 3, 0), (3, 7),
    (0, 2, 2, 3, 0, 2, 0), (3, 8), (1, 1, 3, 3), (0, 1, 0, 2, 0, 0, 3), (3, 9), (0, 0, 1, 3, 3, 1, 2), (3, 10),
    (3, 11), (1, 0, 3, 0), (1, 2, 1, 0), (1, 1, 1, 1), (3, 12), (0, 3, 0, 3, 0, 3, 0), (0, 2, 2, 1, 0, 2, 0), (3, 13),
    (1, 1, 6, 5), (1, 1, 2, 3), (3, 14), (0, 1, 1, 4, 1, 1, 2), (0, 0, 1, 2, 3, 1, 2), (3, 15), (3, 16),
    (0, 1, 1, 1, 1, 1, 2), (1, 3, 0, 0), (1, 1, 5, 5), (3, 17), (0, 2, 3, 0, 0, 3, 0), (0, 3, 1, 5, 4, 2, 4), (3, 18),
    (1, 1, 7, 3), (3, 19), (1, 0, 0, 1), (0, 0, 1, 7, 3, 1, 2), (3, 20), (3, 21), (0, 1, 3, 0, 0, 3, 3),
    (0, 0, 0, 3, 0, 0, 1), (1, 3, 1, 0), (3, 22), (0, 3, 1, 6, 4, 2, 4), (0, 2, 3, 1, 0, 3, 0), (3, 23), (1, 1, 0, 5),
    (3, 24), (3, 25), (3, 26), (0, 0, 3, 1, 0, 3, 1), (0, 1, 3, 1, 0, 3, 3), (3, 27), (1, 3, 2, 0),
    (0, 2, 3, 2, 0, 3, 0), (3, 28), (3, 29), (1, 0, 2, 3), (1, 1, 3, 5), (3, 30), (1, 1, 4, 5), (0, 3, 1, 4, 4, 2, 4),
    (3, 31), (0, 0, 3, 0, 0, 3, 1), (0, 1, 0, 0, 1, 0, 2), (1, 3, 3, 0), (1, 0, 7, 4), (2, 1, 6),
    (0, 2, 1, 4, 4, 1, 4), (2, 1, 5), (1, 1, 2, 5), (2, 1, 0), (0, 3, 0, 7, 4, 3, 4), (1, 1, 1, 5), (1, 1, 7, 5),
    (0, 0, 3, 3, 0, 3, 1), (2, 1, 3), (0, 1, 3, 3, 0, 3, 3), (1, 2, 5, 4), (2, 1, 4), (1, 0, 6, 4), (2, 0, 7),
    (0, 2, 3, 3, 0, 3, 0), (0, 3, 1, 7, 4, 2, 4), (2, 1, 2), (0, 0, 3, 2, 0, 3, 1), (0, 1, 3, 2, 0, 3, 3), (2, 1, 1),
    (2, 1, 7), (1, 2, 6, 4), (0, 2, 2, 5, 4, 2, 4), (2, 2, 5), (0, 3, 0, 6, 4, 3, 4), (1, 3, 1, 1), (2, 0, 6),
    (0, 0, 0, 2, 3, 0, 2), (0, 1, 0, 3, 0, 0, 3), (2, 2, 6), (1, 0, 4, 4), (2, 0, 4), (0, 2, 2, 6, 4, 2, 4),
    (1, 2, 4, 4), (2, 2, 4), (1, 3, 0, 1), (0, 0, 0, 1, 0, 0, 1), (0, 1, 3, 0, 1, 3, 2), (0, 3, 0, 4, 4, 3, 4),
    (1, 0, 5, 4), (2, 0, 5), (1, 3, 7, 4), (2, 3, 7), (0, 2, 2, 4, 4, 2, 4), (1, 3, 3, 3), (0, 0, 3, 3, 3, 3, 2),
    (0, 1, 3, 1, 1, 3, 2), (0, 3, 0, 5, 4, 3, 4), (1, 2, 7, 4), (2, 2, 7), (1, 3, 2, 3), (0, 0, 3, 2, 3, 3, 2),
    (0, 1, 2, 2, 0, 2, 3), (0, 2, 2, 7, 4, 2, 4), (1, 3, 6, 4), (1, 0, 3, 3), (2, 3, 6), (0, 0, 0, 3, 3, 0, 2),
    (0, 1, 0, 0, 0, 0, 3), (0, 2, 3, 7, 4, 3, 4), (1, 0, 1, 1), (1, 3, 0, 5), (2, 3, 0), (0, 0, 2, 1, 0, 2, 1),
    (0, 2, 3, 6, 4, 3, 4), (0, 1, 0, 1, 1, 0, 2), (1, 3, 4, 4), (2, 3, 4), (1, 3, 3, 5), (2, 3, 3), (1, 3, 1, 5),
    (0, 0, 0, 2, 0, 0, 1), (2, 3, 1), (0, 1, 0, 1, 0, 0, 3), (1, 3, 5, 4), (2, 3, 5), (0, 2, 3, 5, 4, 3, 4),
    (1, 3, 2, 5), (2, 3, 2), (1, 2, 2, 3), (0, 0, 2, 0, 0, 2, 1), (0, 1, 2, 3, 0, 2, 3), (0, 2, 3, 4, 4, 3, 4),
    (1, 0, 3, 5), (2, 0, 3), (1, 0, 0, 5), (0, 0, 2, 2, 0, 2, 1), (0, 1, 2, 1, 0, 2, 3), (2, 0, 0),
    (0, 2, 1, 5, 4, 1, 4), (1, 2, 1, 1), (0, 1, 2, 1, 1, 2, 2), (0, 0, 2, 2, 3, 2, 2), (0, 2, 1, 6, 4, 1, 4),
    (1, 0, 2, 5), (2, 0, 2), (1, 0, 1, 5), (0, 1, 2, 0, 0, 2, 3), (2, 0, 1), (0, 0, 2, 3, 0, 2, 1),
    (0, 2, 1, 7, 4, 1, 4), (1, 2, 0, 1), (1, 2, 3, 3), (0, 1, 2, 0, 1, 2, 2), (0, 0, 2, 3, 3, 2, 2), (1, 2, 1, 5),
    (2, 2, 1), (1, 2, 2, 5), (2, 2, 2), (1, 2, 0, 5), (1, 2, 3, 5), (2, 2, 0), (2, 2, 3),
))
GROUPS = ((0, 0, 0, 0, 0, 0, 0, 0, 0, 0, 0, 0, 0, 0, 0, 0, 0, 0, 0, 0, 0, 0, 0, 0, 0, 0, 0, 0, 0, 0, 0, 0, 0, 0, 0, 0, 0, 0, 0, 0, 0, 0, 0, 0, 0, 0, 0, 0, 0, 0, 0, 0, 0, 0, 0, 0, 0, 0, 0, 0, 0, 0, 0, 0, 0, 0, 0, 1), (0, 0, 0, 0, 0, 0, 0, 0, 0, 0, 0, 0, 0, 0, 0, 0, 0, 0, 0, 0, 0, 0, 0, 0, 0, 0, 0, 0, 0, 0, 0, 0, 0, 0, 0, 0, 0, 0, 0, 0, 0, 0, 0, 0, 0, 0, 0, 0, 1, 1, 1, 1, 1, 1, 1, 1, 1, 1, 1, 1, 1, 1, 1, 1, 1, 1, 1, 1, 1, 1, 1, 1, 1, 1, 1, 1, 1, 1, 1, 1, 1, 1, 1, 1, 1, 1, 1, 1, 1, 1, 1, 1, 1, 1, 1, 1, 1, 1, 1, 1))
SHAPES = (((16, 46), (12, 1)), ((16, 31), (13, 52)))
ARRIVALS = tuple(tuple(op[1:] for op in order if op[0] == 1) for order in ORDERS)
ARRIVAL_SEMS = ((0, 1, 2, 3, 4, 5, 6, 7, 8, 9, 10, 11, 12, 13, 14, 15, 16, 17, 18, 19, 20, 21, 22, 23, 24, 4, 25, 0, 26, 2, 12, 6, 14, 8, 27, 11, 5, 18, 1, 7, 16, 10, 20, 24, 19, 23, 25, 15, 9, 13, 12, 17, 14, 4, 21, 6, 2, 3, 22, 26, 0, 28, 29, 30), (0, 1, 2, 3, 4, 5, 6, 7, 8, 9, 10, 11, 12, 13, 14, 15, 16, 17, 18, 19, 20, 21, 22, 23, 24, 25, 26, 0, 27, 28, 29, 3, 2, 7, 1, 10, 9, 8, 12, 11, 14, 16, 13, 20, 15, 23, 6, 25, 19, 5, 27, 17, 2, 30, 4, 3, 21, 29, 28, 0, 26, 24, 22, 18))


def passed_along(block, axis, distance):
    devices = range(lax.axis_size(axis))
    route = [((i - distance) % len(devices), i) for i in devices]
    return lax.ppermute(block, axis, route)


def masked_weight(weight, mask):
    row_blocks, col_blocks = mask.shape
    shaped = weight.reshape(
        row_blocks, weight.shape[0] // row_blocks, col_blocks, weight.shape[1] // col_blocks
    )
    return (shaped * mask.astype(jnp.bfloat16)[:, None, :, None]).reshape(weight.shape)


def project(token_rows, weight):
    return lax.dot_general(
        token_rows, weight, (((1,), (1,)), ((), ())), preferred_element_type=jnp.float32
    )


def gated_block(token_rows, gate_part, up_part):
    gate = project(token_rows, gate_part)
    up_values = project(token_rows, up_part)
    return (jax.nn.silu(gate) * up_values).astype(jnp.bfloat16)


def collect_panels(stacked):
    panel_count = lax.axis_size("panel")
    collected = [(stacked, 0)]
    moving = stacked
    for distance in range(1, panel_count):
        moving = passed_along(moving, "panel", 1)
        collected.append((moving, distance))
    return collected


def general_shards(tokens, gate_weight, up_weight, gate_mask, up_mask):
    panel_count = lax.axis_size("panel")
    my_panel = lax.axis_index("panel")
    width_rows = gate_weight.shape[0]
    stacked = jnp.stack([masked_weight(gate_weight, gate_mask), masked_weight(up_weight, up_mask)])
    collected = collect_panels(stacked)
    gathered = lax.all_gather(tokens, "seq", axis=0, tiled=True)
    tile = jnp.zeros((gathered.shape[0], panel_count * width_rows), jnp.bfloat16)
    for pair, distance in collected:
        source = (my_panel - distance) % panel_count
        result = gated_block(gathered, pair[0], pair[1])
        tile = lax.dynamic_update_slice_in_dim(tile, result, source * width_rows, 1)
    return lax.all_to_all(tile, "seq", split_axis=0, concat_axis=1, tiled=True)


def kernel(
    tok, gw, uw, gm, um, out,
    held, w, turned, masks, wide, hid,
    total, recv_sem, send_sem, part_send, part_recv, local_sem, out_send, out_recv, out_local,
):
    rows, width = tok.shape
    wrows = gw.shape[0]
    seq, panel = lax.axis_index("seq"), lax.axis_index("panel")
    z, x = seq // 2, seq % 2
    y, core = panel // 2, panel % 2

    def device(bz, bx, by):
        return (bz * 2 + bx, by * 2 + core)

    low = z < NZ // 2
    toward = jnp.where(low, 1, -1)
    at_end = jnp.logical_or(z == 0, z == NZ - 1)

    def plane_z(p):
        return jnp.where(low, p, NZ - 1 - p)

    xdev, ydev = device(z, 1 - x, y), device(z, x, 1 - y)
    inward, outward = device(z + toward, x, y), device(z - toward, x, y)
    partner = (seq, y * 2 + 1 - core)

    barrier = pltpu.get_barrier_semaphore()
    for dev in (xdev, ydev, partner, inward):
        pl.semaphore_signal(barrier, inc=1, device_id=dev, device_id_type=MESH)

    @pl.when(jnp.logical_not(at_end))
    def _():
        pl.semaphore_signal(barrier, inc=1, device_id=outward, device_id_type=MESH)

    def slot(p, b):
        return pl.ds((p * 4 + b) * rows, rows) if b < 4 else pl.ds(p * 4 * rows, 4 * rows)

    own = pl.ds(pl.multiple_of(core * wrows, wrows), wrows)
    own_up = pl.ds(pl.multiple_of((2 + core) * wrows, wrows), wrows)
    weight_parts = (
        (gw, w.at[own]), (uw, w.at[own_up]), (gm, masks.at[core]), (um, masks.at[2 + core]),
    )
    keep_tokens = [
        pltpu.make_async_copy(tok, held.at[slot(q, 0)], local_sem.at[2]) for q in range(2)
    ]
    when_q = (at_end, jnp.logical_not(at_end))
    for q in range(2):
        pl.when(when_q[q])(keep_tokens[q].start)
    pl.semaphore_wait(barrier, jnp.where(at_end, 4, 5))
    pltpu.make_async_copy(tok, held.at[slot(0, 0)], local_sem.at[2]).wait()

    unit = width // 64

    def cols(k):
        return pl.ds(PIECES[k][0] * unit, PIECES[k][1] * unit)

    def arrival(q, p, k, b):
        last_hop = b in ((1, 2), (2, 3))[PIECES[k][2]]
        return ARRIVAL_SEMS[q][ARRIVALS[q].index((p, k, 5 if last_hop else b))]

    half = 2 * wrows

    def out_cols(bz, bx, by):
        block = (bz * 2 + bx) * 2 + by
        return pl.ds(pl.multiple_of(block * half, half), half)

    def relative(b):
        return (x + (b in (1, 2))) % 2, (y + (b in (2, 3))) % 2

    swaps = [
        pltpu.make_async_remote_copy(
            src_ref=src, dst_ref=dst, send_sem=part_send.at[i // 2], recv_sem=part_recv.at[i // 2],
            device_id=partner, device_id_type=MESH,
        )
        for i, (src, dst) in enumerate(weight_parts)
    ]

    def prune(i, state):
        if i == 0:
            for j, ref in enumerate((w.at[pl.ds(0, half)], masks.at[pl.ds(0, 2)])):
                for sem in (local_sem, part_send, part_recv):
                    pltpu.make_async_copy(ref, ref, sem.at[j]).wait()
            row = lax.broadcasted_iota(jnp.int32, (8, masks.shape[2]), 0)
            table = jnp.zeros((8, masks.shape[2]), jnp.float32)
            for r in range(4):
                table = jnp.where(row == r, masks[r].astype(jnp.float32), table)
            state["table"] = table.astype(jnp.bfloat16)
        step = width // PRUNES
        block = width // masks.shape[2]
        start = i * step
        where_ = lax.broadcasted_iota(jnp.int32, (masks.shape[2], step), 0)
        col = lax.broadcasted_iota(jnp.int32, (masks.shape[2], step), 1) + start
        first = where_ * block
        inside = jnp.logical_and(col >= first, col < first + block)
        select = jnp.where(inside, 1.0, 0.0).astype(jnp.bfloat16)
        wide[...] = jnp.dot(state["table"], select, preferred_element_type=jnp.float32)
        kept = []
        for r in range(4):
            keep = jnp.broadcast_to(wide[r:r + 1, :], (wrows, step))
            part = w[pl.ds(r * wrows, wrows), pl.ds(start, step)].astype(jnp.float32)
            kept.append((part * keep).astype(jnp.bfloat16))
        turned[pl.ds(start, step), :] = jnp.concatenate(kept, axis=0).T

    def program(q, table):
        links = (xdev, ydev, inward if q == 0 else outward, inward)
        sends, state = [], {}

        def finish(p, both):
            gate = both[:, :half]
            hid[slot(p, 4), :] = (gate / (1.0 + jnp.exp(-gate)) * both[:, half:]).astype(jnp.bfloat16)
            for b in (2, 1, 3, 0):
                if (p, b) == (q, 0):
                    state["kept_out"] = pltpu.make_async_copy(
                        hid.at[slot(p, 0)], out.at[:, out_cols(z, x, y)], out_local
                    )
                    state["kept_out"].start()
                    continue
                tx, ty = relative(b)
                pltpu.make_async_remote_copy(
                    src_ref=hid.at[slot(p, b)], dst_ref=out.at[:, out_cols(z, x, y)],
                    send_sem=out_send, recv_sem=out_recv,
                    device_id=device(plane_z(p), tx, ty), device_id_type=MESH,
                ).start()

        def multiply(p, k):
            at = slot(p, 4)
            both = jnp.dot(held[at, cols(k)], turned[cols(k), :], preferred_element_type=jnp.float32)
            done = state.get(p, 0)
            if done:
                both = both + total[at, :]
            state[p] = done + 1
            if done + 1 < len(PIECES):
                total[at, :] = both
            else:
                finish(p, both)

        for op in table:
            if op[0] == 0:
                _, link, p, k, src, p2, dst = op
                q2 = 1 - q if link == 2 else q
                source = held.at[slot(p, src), cols(k)]
                copy = pltpu.make_async_remote_copy(
                    src_ref=source, dst_ref=held.at[slot(p2, dst), cols(k)],
                    send_sem=send_sem.at[GROUPS[q][len(sends)]], recv_sem=recv_sem.at[arrival(q2, p2, k, dst)],
                    device_id=links[link], device_id_type=MESH,
                )
                copy.start()
                sends.append(op)
            elif op[0] == 1:
                _, p, k, b = op
                at = slot(p, b) if b < 5 else pl.ds((p * 4 + 1 + PIECES[k][2]) * rows, 2 * rows)
                ref = held.at[at, cols(k)]
                pltpu.make_async_copy(ref, ref, recv_sem.at[ARRIVAL_SEMS[q][ARRIVALS[q].index((p, k, b))]]).wait()
            elif op[0] == 2:
                multiply(op[1], op[2])
            elif op[0] == 3:
                prune(op[1], state)
            else:
                for copy in swaps:
                    copy.start()
                for i, (src, dst) in enumerate(weight_parts):
                    pltpu.make_async_copy(src, dst, local_sem.at[i // 2]).start()
        for group, (high, wide_) in enumerate(SHAPES[q]):
            ref = held.at[pl.ds(0, high * rows), pl.ds(0, wide_ * unit)]
            pltpu.make_async_copy(ref, ref, send_sem.at[group]).wait()
        others = 4 * NZ - 1
        ref = hid.at[pl.ds(0, others * rows)]
        pltpu.make_async_copy(ref, ref, out_send).wait()
        state["kept_out"].wait()
        ref = out.at[:, pl.ds(0, others * half)]
        pltpu.make_async_copy(ref, ref, out_recv).wait()

    for q in range(2):
        pl.when(when_q[q])(functools.partial(program, q, ORDERS[q]))


def shards(tokens, gate_weight, up_weight, gate_mask, up_mask):
    rows, width = tokens.shape
    wrows = gate_weight.shape[0]
    blocks = lax.axis_size("seq") * lax.axis_size("panel") // 2
    hidden = lax.axis_size("seq") * lax.axis_size("panel") * wrows
    dma = pltpu.SemaphoreType.DMA
    return pl.pallas_call(
        kernel,
        out_shape=pltpu.VMEM((rows, hidden), jnp.bfloat16),
        in_specs=[pl.BlockSpec(memory_space=pl.ANY)] * 5,
        out_specs=pl.BlockSpec(memory_space=pltpu.VMEM),
        scratch_shapes=[
            pltpu.VMEM((blocks * rows, width), jnp.bfloat16),
            pltpu.VMEM((4 * wrows, width), jnp.bfloat16),
            pltpu.VMEM((width, 4 * wrows), jnp.bfloat16),
            pltpu.VMEM((4, 1, gate_mask.shape[1]), jnp.int32),
            pltpu.VMEM((8, width // PRUNES), jnp.float32),
            pltpu.VMEM((blocks * rows, 2 * wrows), jnp.bfloat16),
            pltpu.VMEM((blocks * rows, 4 * wrows), jnp.float32),
            dma((1 + max(map(max, ARRIVAL_SEMS)),)), dma((max(map(len, SHAPES)),)),
            dma((2,)), dma((2,)), dma((3,)), dma, dma, dma,
        ],
        compiler_params=pltpu.CompilerParams(collective_id=0, has_side_effects=True),
    )(tokens, gate_weight, up_weight, gate_mask, up_mask)


def solution(mesh):
    spec = P(("seq", "panel"), None)
    fits = mesh.shape["seq"] == 2 * NZ and mesh.shape["panel"] == 4
    body = shards if fits else general_shards
    return jax.shard_map(
        body, mesh=mesh, in_specs=(spec,) * 5, out_specs=spec, check_vma=False
    )
```

```python
import functools

import jax
import jax.numpy as jnp
from jax import lax
from jax.experimental import pallas as pl
from jax.experimental.pallas import tpu as pltpu
from jax.sharding import PartitionSpec as P

MESH = pl.DeviceIdType.MESH
NZ = 4
PRUNES = 32
PIECES = ((0, 13, 1), (13, 12, 1), (25, 13, 0), (38, 12, 0), (50, 4, 1), (54, 3, 1), (57, 4, 0), (61, 3, 0))
ORDERS = ((
    (0, 0, 0, 1, 0, 0, 1), (0, 0, 0, 2, 0, 0, 1), (0, 1, 0, 5, 0, 0, 3), (0, 1, 0, 7, 0, 0, 3), (0, 1, 0, 6, 0, 0, 3),
    (0, 1, 0, 4, 0, 0, 3), (0, 2, 0, 1, 0, 0, 0), (0, 2, 0, 3, 0, 0, 0), (0, 1, 0, 1, 0, 0, 3), (0, 2, 0, 0, 0, 0, 0),
    (4, 0), (0, 0, 0, 3, 0, 0, 1), (0, 1, 0, 3, 0, 0, 3), (0, 0, 0, 4, 0, 0, 1), (0, 2, 0, 2, 0, 0, 0),
    (0, 1, 0, 2, 0, 0, 3), (0, 0, 0, 5, 0, 0, 1), (1, 0, 7, 3), (0, 0, 0, 7, 3, 0, 2), (1, 0, 6, 3),
    (0, 0, 0, 6, 3, 0, 2), (1, 0, 1, 1), (1, 1, 1, 0), (0, 1, 1, 1, 0, 1, 3), (0, 0, 0, 6, 0, 0, 1),
    (0, 0, 0, 7, 0, 0, 1), (0, 0, 0, 0, 0, 0, 1), (3, 0), (1, 1, 2, 0), (3, 1), (0, 1, 1, 2, 0, 1, 3), (3, 2), (3, 3),
    (3, 4), (3, 5), (0, 0, 1, 1, 0, 1, 1), (3, 6), (1, 1, 3, 0), (1, 0, 3, 3), (3, 7), (0, 1, 1, 3, 0, 1, 3),
    (1, 0, 4, 1), (3, 8), (3, 9), (1, 0, 5, 1), (3, 10), (0, 0, 0, 3, 3, 0, 2), (3, 11), (1, 1, 0, 0), (3, 12),
    (1, 0, 2, 3), (3, 13), (0, 1, 0, 5, 1, 0, 2), (3, 14), (1, 0, 6, 5), (0, 2, 0, 6, 4, 0, 4), (0, 1, 0, 4, 1, 0, 2),
    (3, 15), (1, 0, 7, 5), (0, 2, 0, 7, 4, 0, 4), (3, 16), (0, 0, 0, 2, 3, 0, 2), (0, 1, 1, 0, 0, 1, 3), (3, 17),
    (1, 2, 1, 0), (3, 18), (3, 19), (3, 20), (3, 21), (1, 0, 0, 1), (3, 22), (0, 0, 2, 1, 0, 2, 1),
    (0, 1, 2, 1, 0, 2, 3), (3, 23), (1, 2, 0, 0), (1, 1, 2, 3), (3, 24), (3, 25), (3, 26), (3, 27), (1, 1, 1, 1),
    (0, 0, 2, 0, 0, 2, 1), (0, 1, 2, 0, 0, 2, 3), (3, 28), (3, 29), (1, 2, 2, 0), (1, 1, 3, 3), (3, 30), (1, 0, 5, 5),
    (0, 2, 0, 5, 4, 0, 4), (3, 31), (1, 0, 3, 5), (1, 0, 4, 5), (0, 2, 0, 4, 4, 0, 4), (2, 0, 6),
    (0, 0, 1, 3, 3, 1, 2), (0, 1, 2, 2, 0, 2, 3), (2, 0, 7), (1, 2, 3, 0), (2, 0, 5), (2, 0, 4), (1, 0, 2, 5),
    (2, 0, 3), (0, 0, 2, 3, 0, 2, 1), (0, 1, 2, 3, 0, 2, 3), (1, 3, 1, 0), (2, 0, 2), (1, 2, 1, 1),
    (0, 0, 3, 1, 0, 3, 1), (0, 1, 2, 1, 1, 2, 2), (1, 3, 3, 0), (1, 2, 0, 1), (0, 0, 3, 3, 0, 3, 1),
    (0, 1, 3, 3, 0, 3, 3), (1, 3, 0, 0), (0, 0, 3, 0, 0, 3, 1), (1, 2, 2, 3), (0, 1, 3, 0, 0, 3, 3), (1, 3, 2, 0),
    (1, 2, 3, 3), (0, 0, 2, 3, 3, 2, 2), (0, 1, 3, 2, 0, 3, 3), (1, 1, 7, 4), (2, 1, 7), (1, 3, 1, 1), (1, 2, 1, 5),
    (2, 2, 1), (0, 0, 3, 2, 0, 3, 1), (0, 1, 3, 1, 1, 3, 2), (1, 2, 6, 4), (2, 2, 6), (1, 3, 3, 3),
    (0, 0, 2, 2, 3, 2, 2), (0, 1, 3, 1, 0, 3, 3), (1, 2, 7, 4), (2, 2, 7), (1, 3, 0, 1), (0, 0, 2, 2, 0, 2, 1),
    (0, 1, 3, 0, 1, 3, 2), (1, 3, 6, 4), (1, 2, 3, 5), (2, 2, 3), (1, 3, 2, 3), (2, 3, 6), (0, 0, 3, 3, 3, 3, 2),
    (0, 1, 2, 0, 1, 2, 2), (1, 3, 5, 4), (2, 3, 5), (0, 0, 3, 2, 3, 3, 2), (0, 1, 0, 0, 1, 0, 2), (1, 3, 7, 4),
    (2, 3, 7), (1, 3, 1, 5), (2, 3, 1), (0, 0, 1, 0, 0, 1, 1), (0, 1, 0, 0, 0, 0, 3), (1, 2, 2, 5), (1, 3, 0, 5),
    (2, 2, 2), (1, 3, 4, 4), (0, 0, 1, 3, 0, 1, 1), (2, 3, 0), (0, 1, 0, 1, 1, 0, 2), (2, 3, 4), (1, 3, 3, 5),
    (2, 3, 3), (1, 2, 0, 5), (0, 0, 1, 2, 0, 1, 1), (2, 2, 0), (0, 1, 1, 1, 1, 1, 2), (1, 2, 4, 4), (2, 2, 4),
    (1, 3, 2, 5), (2, 3, 2), (0, 0, 1, 2, 3, 1, 2), (1, 2, 5, 4), (2, 2, 5), (1, 1, 0, 1), (0, 1, 1, 0, 1, 1, 2),
    (1, 0, 0, 5), (2, 0, 0), (1, 1, 6, 4), (2, 1, 6), (1, 1, 3, 5), (2, 1, 3), (1, 0, 1, 5), (2, 0, 1), (1, 1, 4, 4),
    (2, 1, 4), (1, 1, 1, 5), (2, 1, 1), (1, 1, 5, 4), (2, 1, 5), (1, 1, 2, 5), (1, 1, 0, 5), (2, 1, 2), (2, 1, 0),
), (
    (0, 0, 1, 4, 0, 1, 1), (0, 0, 1, 6, 0, 1, 1), (0, 0, 1, 5, 0, 1, 1), (0, 0, 1, 7, 0, 1, 1), (0, 1, 1, 4, 0, 1, 3),
    (0, 1, 1, 7, 0, 1, 3), (0, 1, 1, 6, 0, 1, 3), (0, 1, 1, 5, 0, 1, 3), (0, 2, 1, 1, 0, 1, 0), (0, 2, 1, 2, 0, 1, 0),
    (0, 3, 1, 1, 0, 2, 0), (0, 3, 1, 0, 0, 2, 0), (0, 0, 1, 1, 0, 1, 1), (0, 1, 1, 3, 0, 1, 3), (4, 0),
    (0, 2, 1, 3, 0, 1, 0), (0, 3, 1, 2, 0, 2, 0), (0, 0, 1, 3, 0, 1, 1), (0, 1, 1, 1, 0, 1, 3), (0, 2, 1, 0, 0, 1, 0),
    (0, 3, 1, 3, 0, 2, 0), (0, 0, 1, 0, 0, 1, 1), (0, 1, 1, 0, 0, 1, 3), (1, 1, 4, 1), (1, 1, 7, 3), (1, 1, 5, 1),
    (1, 1, 6, 3), (1, 0, 1, 0), (1, 2, 1, 0), (0, 3, 0, 1, 0, 3, 0), (0, 2, 2, 1, 0, 2, 0), (0, 0, 1, 6, 3, 1, 2),
    (0, 1, 0, 1, 0, 0, 3), (0, 0, 1, 7, 3, 1, 2), (0, 0, 0, 1, 0, 0, 1), (3, 0), (1, 0, 3, 0), (1, 2, 0, 0), (3, 1),
    (1, 1, 1, 1), (1, 1, 3, 3), (0, 3, 0, 3, 0, 3, 0), (0, 2, 2, 0, 0, 2, 0), (0, 1, 0, 3, 0, 0, 3), (3, 2), (3, 3),
    (3, 4), (3, 5), (0, 0, 1, 3, 3, 1, 2), (3, 6), (1, 0, 0, 0), (1, 2, 2, 0), (0, 3, 0, 0, 0, 3, 0), (3, 7),
    (0, 1, 0, 0, 0, 0, 3), (0, 2, 2, 2, 0, 2, 0), (3, 8), (3, 9), (3, 10), (0, 0, 0, 3, 0, 0, 1), (3, 11),
    (1, 0, 2, 0), (1, 2, 3, 0), (3, 12), (1, 1, 0, 1), (0, 3, 0, 2, 0, 3, 0), (3, 13), (0, 1, 0, 2, 0, 0, 3),
    (0, 2, 2, 3, 0, 2, 0), (3, 14), (1, 1, 6, 5), (3, 15), (1, 1, 7, 5), (3, 16), (0, 0, 0, 2, 0, 0, 1), (3, 17),
    (1, 3, 1, 0), (3, 18), (0, 2, 3, 1, 0, 3, 0), (0, 3, 1, 6, 4, 2, 4), (3, 19), (0, 1, 2, 1, 0, 2, 3), (3, 20),
    (3, 21), (1, 0, 1, 1), (0, 0, 3, 1, 0, 3, 1), (3, 22), (1, 3, 3, 0), (3, 23), (1, 0, 3, 3), (3, 24),
    (0, 2, 3, 3, 0, 3, 0), (0, 1, 3, 1, 0, 3, 3), (3, 25), (3, 26), (0, 3, 1, 7, 4, 2, 4), (1, 1, 3, 5), (3, 27),
    (0, 0, 0, 0, 0, 0, 1), (3, 28), (1, 3, 0, 0), (3, 29), (0, 2, 3, 0, 0, 3, 0), (3, 30), (0, 1, 3, 0, 0, 3, 3),
    (3, 31), (1, 0, 6, 4), (0, 3, 0, 6, 4, 3, 4), (2, 1, 6), (0, 0, 3, 0, 0, 3, 1), (2, 1, 7), (1, 3, 2, 0),
    (1, 0, 2, 3), (0, 2, 3, 2, 0, 3, 0), (2, 1, 3), (0, 1, 3, 3, 0, 3, 3), (1, 0, 7, 4), (2, 0, 6), (2, 0, 7),
    (0, 3, 0, 7, 4, 3, 4), (0, 0, 3, 2, 0, 3, 1), (0, 2, 1, 7, 4, 1, 4), (0, 1, 3, 2, 0, 3, 3), (1, 2, 6, 4),
    (2, 2, 6), (1, 3, 1, 1), (0, 0, 3, 3, 0, 3, 1), (1, 0, 5, 4), (0, 3, 0, 5, 4, 3, 4), (2, 0, 5),
    (0, 2, 2, 6, 4, 2, 4), (0, 1, 1, 4, 1, 1, 2), (1, 2, 7, 4), (2, 2, 7), (0, 1, 1, 5, 1, 1, 2), (1, 0, 0, 1),
    (0, 0, 1, 2, 0, 1, 1), (0, 1, 1, 1, 1, 1, 2), (1, 0, 4, 4), (0, 3, 0, 4, 4, 3, 4), (2, 0, 4),
    (0, 2, 2, 7, 4, 2, 4), (1, 3, 6, 4), (2, 3, 6), (1, 3, 0, 1), (0, 1, 1, 0, 1, 1, 2), (0, 0, 0, 3, 3, 0, 2),
    (1, 3, 3, 3), (0, 2, 3, 6, 4, 3, 4), (1, 3, 7, 4), (2, 3, 7), (0, 1, 2, 3, 0, 2, 3), (0, 0, 3, 3, 3, 3, 2),
    (1, 3, 2, 3), (1, 1, 4, 5), (0, 3, 1, 4, 4, 2, 4), (2, 1, 4), (1, 3, 5, 4), (1, 1, 5, 5), (0, 3, 1, 5, 4, 2, 4),
    (2, 3, 5), (0, 2, 3, 5, 4, 3, 4), (0, 1, 2, 2, 0, 2, 3), (0, 0, 3, 2, 3, 3, 2), (2, 1, 5), (1, 1, 1, 5),
    (2, 1, 1), (0, 2, 3, 7, 4, 3, 4), (1, 3, 4, 4), (0, 1, 3, 0, 1, 3, 2), (0, 0, 2, 3, 0, 2, 1), (2, 3, 4),
    (0, 2, 3, 4, 4, 3, 4), (1, 1, 0, 5), (1, 0, 3, 5), (2, 0, 3), (0, 0, 2, 1, 0, 2, 1), (0, 1, 0, 1, 1, 0, 2),
    (2, 1, 0), (1, 2, 4, 4), (2, 2, 4), (1, 2, 3, 3), (1, 3, 3, 5), (2, 3, 3), (0, 0, 2, 3, 3, 2, 2),
    (0, 1, 1, 2, 0, 1, 3), (0, 2, 2, 4, 4, 2, 4), (1, 2, 5, 4), (2, 2, 5), (1, 2, 2, 3), (1, 3, 2, 5), (2, 3, 2),
    (0, 0, 2, 0, 0, 2, 1), (0, 1, 0, 0, 1, 0, 2), (0, 2, 2, 5, 4, 2, 4), (1, 3, 0, 5), (2, 3, 0),
    (0, 0, 2, 2, 0, 2, 1), (0, 1, 3, 1, 1, 3, 2), (0, 2, 1, 6, 4, 1, 4), (1, 2, 1, 1), (1, 0, 1, 5), (2, 0, 1),
    (0, 0, 0, 2, 3, 0, 2), (0, 1, 2, 1, 1, 2, 2), (0, 2, 1, 4, 4, 1, 4), (1, 2, 3, 5), (2, 2, 3), (1, 1, 2, 3),
    (0, 0, 1, 2, 3, 1, 2), (0, 1, 2, 0, 0, 2, 3), (1, 2, 0, 1), (0, 2, 1, 5, 4, 1, 4), (1, 0, 0, 5), (2, 0, 0),
    (0, 0, 2, 2, 3, 2, 2), (0, 1, 2, 0, 1, 2, 2), (1, 3, 1, 5), (2, 3, 1), (1, 0, 2, 5), (1, 2, 1, 5), (2, 2, 1),
    (2, 0, 2), (1, 1, 2, 5), (2, 1, 2), (1, 2, 2, 5), (1, 2, 0, 5), (2, 2, 0), (2, 2, 2),
))
GROUPS = ((0, 0, 0, 0, 0, 0, 0, 0, 0, 0, 0, 0, 0, 0, 0, 0, 0, 0, 0, 0, 0, 0, 0, 0, 0, 0, 0, 0, 0, 0, 0, 0, 0, 0, 0, 0, 0, 0, 0, 0, 0, 0, 0, 0, 0, 0, 0, 0, 0, 0, 0, 0, 0, 0, 0, 0, 0, 0, 0, 0, 0, 0, 0, 0, 0, 0, 0, 1), (0, 0, 0, 0, 0, 0, 0, 0, 0, 0, 0, 0, 0, 0, 0, 0, 0, 0, 0, 0, 0, 0, 0, 0, 0, 0, 0, 0, 0, 0, 0, 0, 0, 0, 0, 0, 0, 0, 0, 0, 0, 0, 0, 0, 0, 0, 0, 0, 0, 0, 0, 0, 0, 0, 0, 0, 0, 0, 0, 0, 0, 0, 0, 0, 0, 0, 0, 0, 0, 0, 0, 0, 0, 0, 0, 0, 0, 0, 1, 1, 1, 1, 1, 1, 1, 1, 1, 1, 1, 1, 1, 1, 1, 1, 1, 1, 1, 1, 1, 1))
SHAPES = (((15, 49), (13, 1)), ((14, 63), (10, 29)))
ARRIVALS = tuple(tuple(op[1:] for op in order if op[0] == 1) for order in ORDERS)
ARRIVAL_SEMS = ((0, 1, 2, 3, 4, 5, 6, 7, 8, 9, 10, 11, 12, 13, 14, 15, 16, 17, 18, 19, 20, 21, 22, 23, 24, 25, 0, 26, 3, 27, 1, 7, 2, 5, 12, 28, 19, 8, 16, 10, 13, 6, 23, 17, 18, 25, 24, 9, 20, 15, 4, 22, 0, 21, 27, 3, 14, 29, 30, 11, 31, 32, 26, 33), (0, 1, 2, 3, 4, 5, 6, 7, 8, 9, 10, 11, 12, 13, 14, 15, 16, 17, 18, 19, 20, 21, 22, 23, 24, 25, 26, 4, 1, 8, 5, 6, 11, 10, 3, 12, 14, 13, 27, 16, 28, 29, 20, 30, 31, 26, 24, 17, 1, 4, 9, 7, 23, 32, 21, 25, 22, 33, 2, 0, 34, 19, 18, 15))


def passed_along(block, axis, distance):
    devices = range(lax.axis_size(axis))
    route = [((i - distance) % len(devices), i) for i in devices]
    return lax.ppermute(block, axis, route)


def masked_weight(weight, mask):
    row_blocks, col_blocks = mask.shape
    shaped = weight.reshape(
        row_blocks, weight.shape[0] // row_blocks, col_blocks, weight.shape[1] // col_blocks
    )
    return (shaped * mask.astype(jnp.bfloat16)[:, None, :, None]).reshape(weight.shape)


def project(token_rows, weight):
    return lax.dot_general(
        token_rows, weight, (((1,), (1,)), ((), ())), preferred_element_type=jnp.float32
    )


def gated_block(token_rows, gate_part, up_part):
    gate = project(token_rows, gate_part)
    up_values = project(token_rows, up_part)
    return (jax.nn.silu(gate) * up_values).astype(jnp.bfloat16)


def collect_panels(stacked):
    panel_count = lax.axis_size("panel")
    collected = [(stacked, 0)]
    moving = stacked
    for distance in range(1, panel_count):
        moving = passed_along(moving, "panel", 1)
        collected.append((moving, distance))
    return collected


def general_shards(tokens, gate_weight, up_weight, gate_mask, up_mask):
    panel_count = lax.axis_size("panel")
    my_panel = lax.axis_index("panel")
    width_rows = gate_weight.shape[0]
    stacked = jnp.stack([masked_weight(gate_weight, gate_mask), masked_weight(up_weight, up_mask)])
    collected = collect_panels(stacked)
    gathered = lax.all_gather(tokens, "seq", axis=0, tiled=True)
    tile = jnp.zeros((gathered.shape[0], panel_count * width_rows), jnp.bfloat16)
    for pair, distance in collected:
        source = (my_panel - distance) % panel_count
        result = gated_block(gathered, pair[0], pair[1])
        tile = lax.dynamic_update_slice_in_dim(tile, result, source * width_rows, 1)
    return lax.all_to_all(tile, "seq", split_axis=0, concat_axis=1, tiled=True)


def kernel(
    tok, gw, uw, gm, um, out,
    held, w, turned, masks, wide, hid,
    total, recv_sem, send_sem, part_send, part_recv, local_sem, out_send, out_recv, out_local,
):
    rows, width = tok.shape
    wrows = gw.shape[0]
    seq, panel = lax.axis_index("seq"), lax.axis_index("panel")
    z, x = seq // 2, seq % 2
    y, core = panel // 2, panel % 2

    def device(bz, bx, by):
        return (bz * 2 + bx, by * 2 + core)

    low = z < NZ // 2
    toward = jnp.where(low, 1, -1)
    at_end = jnp.logical_or(z == 0, z == NZ - 1)

    def plane_z(p):
        return jnp.where(low, p, NZ - 1 - p)

    xdev, ydev = device(z, 1 - x, y), device(z, x, 1 - y)
    inward, outward = device(z + toward, x, y), device(z - toward, x, y)
    partner = (seq, y * 2 + 1 - core)

    barrier = pltpu.get_barrier_semaphore()
    for dev in (xdev, ydev, partner, inward):
        pl.semaphore_signal(barrier, inc=1, device_id=dev, device_id_type=MESH)

    @pl.when(jnp.logical_not(at_end))
    def _():
        pl.semaphore_signal(barrier, inc=1, device_id=outward, device_id_type=MESH)

    def slot(p, b):
        return pl.ds((p * 4 + b) * rows, rows) if b < 4 else pl.ds(p * 4 * rows, 4 * rows)

    own = pl.ds(pl.multiple_of(core * wrows, wrows), wrows)
    own_up = pl.ds(pl.multiple_of((2 + core) * wrows, wrows), wrows)
    weight_parts = (
        (gw, w.at[own]), (uw, w.at[own_up]), (gm, masks.at[core]), (um, masks.at[2 + core]),
    )
    keep_tokens = [
        pltpu.make_async_copy(tok, held.at[slot(q, 0)], local_sem.at[2]) for q in range(2)
    ]
    when_q = (at_end, jnp.logical_not(at_end))
    for q in range(2):
        pl.when(when_q[q])(keep_tokens[q].start)
    pl.semaphore_wait(barrier, jnp.where(at_end, 4, 5))
    pltpu.make_async_copy(tok, held.at[slot(0, 0)], local_sem.at[2]).wait()

    unit = width // 64

    def cols(k):
        return pl.ds(PIECES[k][0] * unit, PIECES[k][1] * unit)

    def arrival(q, p, k, b):
        last_hop = b in ((1, 2), (2, 3))[PIECES[k][2]]
        return ARRIVAL_SEMS[q][ARRIVALS[q].index((p, k, 5 if last_hop else b))]

    half = 2 * wrows

    def out_cols(bz, bx, by):
        block = (bz * 2 + bx) * 2 + by
        return pl.ds(pl.multiple_of(block * half, half), half)

    def relative(b):
        return (x + (b in (1, 2))) % 2, (y + (b in (2, 3))) % 2

    swaps = [
        pltpu.make_async_remote_copy(
            src_ref=src, dst_ref=dst, send_sem=part_send.at[i // 2], recv_sem=part_recv.at[i // 2],
            device_id=partner, device_id_type=MESH,
        )
        for i, (src, dst) in enumerate(weight_parts)
    ]

    def prune(i, state):
        if i == 0:
            for j, ref in enumerate((w.at[pl.ds(0, half)], masks.at[pl.ds(0, 2)])):
                for sem in (local_sem, part_send, part_recv):
                    pltpu.make_async_copy(ref, ref, sem.at[j]).wait()
            row = lax.broadcasted_iota(jnp.int32, (8, masks.shape[2]), 0)
            table = jnp.zeros((8, masks.shape[2]), jnp.float32)
            for r in range(4):
                table = jnp.where(row == r, masks[r].astype(jnp.float32), table)
            state["table"] = table.astype(jnp.bfloat16)
        step = width // PRUNES
        block = width // masks.shape[2]
        start = i * step
        where_ = lax.broadcasted_iota(jnp.int32, (masks.shape[2], step), 0)
        col = lax.broadcasted_iota(jnp.int32, (masks.shape[2], step), 1) + start
        first = where_ * block
        inside = jnp.logical_and(col >= first, col < first + block)
        select = jnp.where(inside, 1.0, 0.0).astype(jnp.bfloat16)
        wide[...] = jnp.dot(state["table"], select, preferred_element_type=jnp.float32)
        kept = []
        for r in range(4):
            keep = jnp.broadcast_to(wide[r:r + 1, :], (wrows, step))
            part = w[pl.ds(r * wrows, wrows), pl.ds(start, step)].astype(jnp.float32)
            kept.append((part * keep).astype(jnp.bfloat16))
        turned[pl.ds(start, step), :] = jnp.concatenate(kept, axis=0).T

    def program(q, table):
        links = (xdev, ydev, inward if q == 0 else outward, inward)
        sends, state = [], {}

        def finish(p, both):
            gate = both[:, :half]
            hid[slot(p, 4), :] = (gate / (1.0 + jnp.exp(-gate)) * both[:, half:]).astype(jnp.bfloat16)
            for b in (2, 1, 3, 0):
                if (p, b) == (q, 0):
                    state["kept_out"] = pltpu.make_async_copy(
                        hid.at[slot(p, 0)], out.at[:, out_cols(z, x, y)], out_local
                    )
                    state["kept_out"].start()
                    continue
                tx, ty = relative(b)
                pltpu.make_async_remote_copy(
                    src_ref=hid.at[slot(p, b)], dst_ref=out.at[:, out_cols(z, x, y)],
                    send_sem=out_send, recv_sem=out_recv,
                    device_id=device(plane_z(p), tx, ty), device_id_type=MESH,
                ).start()

        def multiply(p, k):
            at = slot(p, 4)
            both = jnp.dot(held[at, cols(k)], turned[cols(k), :], preferred_element_type=jnp.float32)
            done = state.get(p, 0)
            if done:
                both = both + total[at, :]
            state[p] = done + 1
            if done + 1 < len(PIECES):
                total[at, :] = both
            else:
                finish(p, both)

        for op in table:
            if op[0] == 0:
                _, link, p, k, src, p2, dst = op
                q2 = 1 - q if link == 2 else q
                source = held.at[slot(p, src), cols(k)]
                copy = pltpu.make_async_remote_copy(
                    src_ref=source, dst_ref=held.at[slot(p2, dst), cols(k)],
                    send_sem=send_sem.at[GROUPS[q][len(sends)]], recv_sem=recv_sem.at[arrival(q2, p2, k, dst)],
                    device_id=links[link], device_id_type=MESH,
                )
                copy.start()
                sends.append(op)
            elif op[0] == 1:
                _, p, k, b = op
                at = slot(p, b) if b < 5 else pl.ds((p * 4 + 1 + PIECES[k][2]) * rows, 2 * rows)
                ref = held.at[at, cols(k)]
                pltpu.make_async_copy(ref, ref, recv_sem.at[ARRIVAL_SEMS[q][ARRIVALS[q].index((p, k, b))]]).wait()
            elif op[0] == 2:
                multiply(op[1], op[2])
            elif op[0] == 3:
                prune(op[1], state)
            else:
                for copy in swaps:
                    copy.start()
                for i, (src, dst) in enumerate(weight_parts):
                    pltpu.make_async_copy(src, dst, local_sem.at[i // 2]).start()
        for group, (high, wide_) in enumerate(SHAPES[q]):
            ref = held.at[pl.ds(0, high * rows), pl.ds(0, wide_ * unit)]
            pltpu.make_async_copy(ref, ref, send_sem.at[group]).wait()
        others = 4 * NZ - 1
        ref = hid.at[pl.ds(0, others * rows)]
        pltpu.make_async_copy(ref, ref, out_send).wait()
        state["kept_out"].wait()
        ref = out.at[:, pl.ds(0, others * half)]
        pltpu.make_async_copy(ref, ref, out_recv).wait()

    for q in range(2):
        pl.when(when_q[q])(functools.partial(program, q, ORDERS[q]))


def shards(tokens, gate_weight, up_weight, gate_mask, up_mask):
    rows, width = tokens.shape
    wrows = gate_weight.shape[0]
    blocks = lax.axis_size("seq") * lax.axis_size("panel") // 2
    hidden = lax.axis_size("seq") * lax.axis_size("panel") * wrows
    dma = pltpu.SemaphoreType.DMA
    return pl.pallas_call(
        kernel,
        out_shape=pltpu.VMEM((rows, hidden), jnp.bfloat16),
        in_specs=[pl.BlockSpec(memory_space=pl.ANY)] * 5,
        out_specs=pl.BlockSpec(memory_space=pltpu.VMEM),
        scratch_shapes=[
            pltpu.VMEM((blocks * rows, width), jnp.bfloat16),
            pltpu.VMEM((4 * wrows, width), jnp.bfloat16),
            pltpu.VMEM((width, 4 * wrows), jnp.bfloat16),
            pltpu.VMEM((4, 1, gate_mask.shape[1]), jnp.int32),
            pltpu.VMEM((8, width // PRUNES), jnp.float32),
            pltpu.VMEM((blocks * rows, 2 * wrows), jnp.bfloat16),
            pltpu.VMEM((blocks * rows, 4 * wrows), jnp.float32),
            dma((1 + max(map(max, ARRIVAL_SEMS)),)), dma((max(map(len, SHAPES)),)),
            dma((2,)), dma((2,)), dma((3,)), dma, dma, dma,
        ],
        compiler_params=pltpu.CompilerParams(collective_id=0, has_side_effects=True),
    )(tokens, gate_weight, up_weight, gate_mask, up_mask)


def solution(mesh):
    spec = P(("seq", "panel"), None)
    fits = mesh.shape["seq"] == 2 * NZ and mesh.shape["panel"] == 4
    body = shards if fits else general_shards
    return jax.shard_map(
        body, mesh=mesh, in_specs=(spec,) * 5, out_specs=spec, check_vma=False
    )
```

```python
import functools

import jax
import jax.numpy as jnp
from jax import lax
from jax.experimental import pallas as pl
from jax.experimental.pallas import tpu as pltpu
from jax.sharding import PartitionSpec as P

MESH = pl.DeviceIdType.MESH
NZ = 4
PRUNES = 32
PIECES = ((0, 13, 1), (13, 12, 1), (25, 13, 0), (38, 12, 0), (50, 4, 1), (54, 3, 1), (57, 4, 0), (61, 3, 0))
ORDERS = ((
    (0, 0, 0, 5, 0, 0, 1), (0, 0, 0, 6, 0, 0, 1), (0, 0, 0, 0, 0, 0, 1), (0, 1, 0, 5, 0, 0, 3), (0, 1, 0, 6, 0, 0, 3),
    (0, 1, 0, 2, 0, 0, 3), (0, 2, 0, 3, 0, 0, 0), (0, 2, 0, 2, 0, 0, 0), (0, 0, 0, 1, 0, 0, 1), (0, 1, 0, 4, 0, 0, 3),
    (0, 1, 0, 3, 0, 0, 3), (4, 0), (0, 2, 0, 1, 0, 0, 0), (0, 0, 0, 4, 0, 0, 1), (0, 1, 0, 7, 0, 0, 3),
    (0, 0, 0, 2, 0, 0, 1), (1, 0, 5, 1), (0, 2, 0, 0, 0, 0, 0), (0, 1, 0, 5, 1, 0, 2), (1, 0, 6, 3),
    (0, 1, 0, 0, 0, 0, 3), (1, 1, 2, 0), (0, 0, 0, 6, 3, 0, 2), (0, 0, 0, 7, 0, 0, 1), (1, 0, 0, 1), (1, 0, 2, 3),
    (0, 1, 0, 0, 1, 0, 2), (0, 0, 1, 2, 0, 1, 1), (3, 0), (1, 1, 3, 0), (3, 1), (3, 2), (3, 3), (1, 0, 1, 1), (3, 4),
    (0, 1, 0, 1, 1, 0, 2), (0, 0, 1, 3, 0, 1, 1), (3, 5), (1, 0, 3, 3), (1, 0, 4, 1), (1, 1, 0, 0), (3, 6),
    (1, 0, 7, 3), (3, 7), (1, 0, 5, 5), (0, 2, 0, 5, 4, 0, 4), (3, 8), (3, 9), (0, 1, 0, 4, 1, 0, 2), (3, 10),
    (0, 0, 0, 7, 3, 0, 2), (3, 11), (1, 1, 1, 0), (0, 1, 1, 0, 0, 1, 3), (0, 0, 1, 1, 0, 1, 1), (3, 12), (1, 0, 6, 5),
    (0, 2, 0, 6, 4, 0, 4), (3, 13), (3, 14), (3, 15), (3, 16), (1, 2, 1, 0), (0, 0, 2, 1, 0, 2, 1), (3, 17),
    (0, 1, 2, 1, 0, 2, 3), (3, 18), (3, 19), (1, 0, 0, 5), (3, 20), (3, 21), (3, 22), (0, 0, 0, 3, 0, 0, 1),
    (1, 2, 0, 0), (0, 1, 2, 0, 0, 2, 3), (3, 23), (3, 24), (3, 25), (3, 26), (1, 0, 4, 5), (1, 0, 7, 5),
    (0, 2, 0, 4, 4, 0, 4), (3, 27), (0, 0, 2, 0, 0, 2, 1), (3, 28), (0, 2, 0, 7, 4, 0, 4), (1, 2, 2, 0),
    (0, 1, 2, 2, 0, 2, 3), (3, 29), (3, 30), (3, 31), (1, 1, 1, 1), (2, 0, 5), (0, 0, 2, 2, 0, 2, 1), (2, 0, 6),
    (1, 2, 3, 0), (0, 1, 1, 1, 1, 1, 2), (2, 0, 0), (2, 0, 4), (1, 2, 1, 1), (2, 0, 7), (1, 3, 3, 0),
    (0, 0, 2, 3, 0, 2, 1), (0, 1, 2, 1, 1, 2, 2), (0, 0, 3, 3, 0, 3, 1), (1, 3, 2, 0), (0, 1, 2, 3, 0, 2, 3),
    (1, 2, 0, 1), (1, 2, 2, 3), (0, 0, 2, 2, 3, 2, 2), (1, 3, 1, 0), (0, 1, 3, 1, 0, 3, 3), (0, 0, 3, 2, 0, 3, 1),
    (0, 1, 3, 3, 0, 3, 3), (1, 3, 0, 0), (1, 2, 1, 5), (2, 2, 1), (0, 1, 3, 2, 0, 3, 3), (1, 3, 5, 4),
    (0, 0, 3, 0, 0, 3, 1), (2, 3, 5), (1, 2, 3, 3), (0, 1, 3, 0, 0, 3, 3), (0, 0, 3, 1, 0, 3, 1), (1, 3, 6, 4),
    (2, 3, 6), (1, 2, 2, 5), (2, 2, 2), (0, 1, 1, 3, 0, 1, 3), (0, 0, 2, 3, 3, 2, 2), (1, 2, 4, 4), (2, 2, 4),
    (1, 3, 3, 3), (0, 1, 2, 0, 1, 2, 2), (0, 0, 3, 3, 3, 3, 2), (1, 2, 5, 4), (2, 2, 5), (1, 3, 2, 3), (1, 3, 0, 1),
    (0, 0, 3, 2, 3, 3, 2), (0, 1, 3, 0, 1, 3, 2), (1, 2, 7, 4), (2, 2, 7), (1, 3, 1, 1), (0, 0, 1, 0, 0, 1, 1),
    (0, 1, 3, 1, 1, 3, 2), (1, 1, 3, 3), (1, 2, 3, 5), (2, 2, 3), (1, 2, 6, 4), (2, 2, 6), (0, 0, 1, 3, 3, 1, 2),
    (0, 1, 1, 2, 0, 1, 3), (1, 3, 3, 5), (2, 3, 3), (1, 2, 0, 5), (2, 2, 0), (0, 0, 0, 2, 3, 0, 2), (1, 3, 4, 4),
    (0, 1, 1, 1, 0, 1, 3), (2, 3, 4), (1, 3, 2, 5), (2, 3, 2), (1, 3, 0, 5), (2, 3, 0), (1, 3, 7, 4),
    (0, 0, 0, 3, 3, 0, 2), (0, 1, 0, 1, 0, 0, 3), (2, 3, 7), (1, 1, 0, 1), (1, 3, 1, 5), (2, 3, 1),
    (0, 1, 1, 0, 1, 1, 2), (1, 1, 4, 4), (2, 1, 4), (1, 1, 3, 5), (2, 1, 3), (1, 1, 2, 3), (0, 0, 1, 2, 3, 1, 2),
    (1, 1, 5, 4), (2, 1, 5), (1, 0, 2, 5), (1, 1, 1, 5), (2, 0, 2), (2, 1, 1), (1, 1, 6, 4), (2, 1, 6), (1, 0, 3, 5),
    (1, 0, 1, 5), (2, 0, 1), (2, 0, 3), (1, 1, 7, 4), (2, 1, 7), (1, 1, 0, 5), (1, 1, 2, 5), (2, 1, 2), (2, 1, 0),
), (
    (0, 0, 1, 5, 0, 1, 1), (0, 0, 1, 0, 0, 1, 1), (0, 1, 1, 1, 0, 1, 3), (0, 1, 1, 2, 0, 1, 3), (0, 2, 1, 2, 0, 1, 0),
    (0, 2, 1, 3, 0, 1, 0), (0, 3, 1, 1, 0, 2, 0), (0, 3, 1, 0, 0, 2, 0), (0, 0, 1, 1, 0, 1, 1), (4, 0),
    (0, 1, 1, 0, 0, 1, 3), (0, 2, 1, 0, 0, 1, 0), (0, 3, 1, 2, 0, 2, 0), (0, 0, 1, 2, 0, 1, 1), (1, 1, 5, 1),
    (0, 1, 1, 3, 0, 1, 3), (0, 2, 1, 1, 0, 1, 0), (0, 3, 1, 3, 0, 2, 0), (0, 0, 1, 3, 0, 1, 1), (1, 0, 3, 0),
    (1, 2, 1, 0), (1, 1, 0, 1), (0, 1, 1, 0, 1, 1, 2), (0, 3, 0, 3, 0, 3, 0), (0, 2, 2, 1, 0, 2, 0),
    (0, 0, 1, 4, 0, 1, 1), (0, 0, 1, 6, 0, 1, 1), (3, 0), (1, 0, 2, 0), (1, 1, 2, 3), (1, 2, 0, 0),
    (0, 0, 1, 2, 3, 1, 2), (3, 1), (1, 1, 1, 1), (0, 3, 0, 2, 0, 3, 0), (0, 2, 2, 0, 0, 2, 0), (0, 1, 1, 4, 0, 1, 3),
    (3, 2), (3, 3), (0, 1, 1, 6, 0, 1, 3), (3, 4), (3, 5), (1, 0, 1, 0), (0, 1, 1, 7, 0, 1, 3), (1, 2, 2, 0), (3, 6),
    (0, 0, 0, 1, 0, 0, 1), (0, 1, 2, 0, 0, 2, 3), (3, 7), (0, 3, 0, 1, 0, 3, 0), (0, 2, 2, 2, 0, 2, 0), (3, 8),
    (3, 9), (3, 10), (3, 11), (1, 0, 0, 0), (1, 1, 3, 3), (1, 2, 3, 0), (3, 12), (0, 0, 1, 3, 3, 1, 2),
    (0, 3, 0, 0, 0, 3, 0), (0, 1, 1, 5, 1, 1, 2), (3, 13), (0, 2, 2, 3, 0, 2, 0), (3, 14), (0, 1, 1, 1, 1, 1, 2),
    (1, 1, 4, 1), (3, 15), (3, 16), (1, 3, 3, 0), (3, 17), (1, 1, 0, 5), (0, 0, 0, 2, 0, 0, 1), (3, 18),
    (0, 2, 3, 3, 0, 3, 0), (3, 19), (0, 1, 1, 4, 1, 1, 2), (3, 20), (3, 21), (1, 1, 6, 3), (0, 1, 1, 5, 0, 1, 3),
    (3, 22), (1, 1, 2, 5), (1, 1, 7, 3), (1, 0, 5, 4), (0, 3, 0, 5, 4, 3, 4), (1, 3, 2, 0), (0, 1, 0, 3, 0, 0, 3),
    (3, 23), (0, 0, 1, 6, 3, 1, 2), (3, 24), (0, 2, 3, 2, 0, 3, 0), (3, 25), (0, 0, 1, 7, 0, 1, 1), (3, 26),
    (0, 0, 1, 7, 3, 1, 2), (3, 27), (1, 0, 1, 1), (3, 28), (1, 3, 1, 0), (0, 1, 0, 2, 0, 0, 3), (0, 0, 0, 0, 0, 0, 1),
    (3, 29), (1, 0, 6, 4), (0, 3, 0, 6, 4, 3, 4), (3, 30), (0, 2, 3, 1, 0, 3, 0), (3, 31), (2, 1, 0), (1, 1, 3, 5),
    (2, 1, 2), (1, 3, 0, 0), (0, 1, 0, 1, 0, 0, 3), (0, 0, 2, 2, 0, 2, 1), (1, 1, 1, 5), (0, 2, 3, 0, 0, 3, 0),
    (2, 0, 5), (1, 1, 4, 5), (0, 3, 1, 4, 4, 2, 4), (2, 0, 6), (1, 1, 5, 5), (2, 1, 3), (0, 3, 1, 5, 4, 2, 4),
    (1, 3, 5, 4), (0, 1, 0, 0, 0, 0, 3), (0, 0, 0, 3, 0, 0, 1), (2, 1, 1), (1, 1, 6, 5), (0, 2, 3, 5, 4, 3, 4),
    (2, 1, 4), (2, 1, 5), (1, 0, 4, 4), (1, 0, 3, 3), (1, 1, 7, 5), (0, 3, 1, 7, 4, 2, 4), (2, 3, 5),
    (0, 1, 0, 1, 1, 0, 2), (0, 0, 0, 3, 3, 0, 2), (2, 1, 6), (1, 3, 6, 4), (0, 2, 3, 6, 4, 3, 4), (2, 0, 4),
    (1, 0, 7, 4), (2, 1, 7), (1, 0, 2, 3), (1, 0, 0, 1), (0, 3, 1, 6, 4, 2, 4), (0, 1, 0, 0, 1, 0, 2),
    (0, 0, 0, 2, 3, 0, 2), (2, 3, 6), (2, 0, 7), (1, 2, 4, 4), (2, 2, 4), (0, 2, 2, 4, 4, 2, 4),
    (0, 3, 0, 4, 4, 3, 4), (0, 1, 2, 1, 0, 2, 3), (0, 0, 2, 0, 0, 2, 1), (1, 2, 5, 4), (2, 2, 5),
    (0, 2, 2, 5, 4, 2, 4), (0, 1, 3, 2, 0, 3, 3), (0, 0, 3, 3, 0, 3, 1), (0, 3, 0, 7, 4, 3, 4), (1, 2, 7, 4),
    (2, 2, 7), (1, 0, 1, 5), (1, 0, 3, 5), (2, 0, 3), (0, 2, 2, 7, 4, 2, 4), (2, 0, 1), (0, 1, 3, 0, 0, 3, 3),
    (0, 0, 3, 2, 0, 3, 1), (1, 2, 6, 4), (1, 0, 0, 5), (1, 0, 2, 5), (2, 0, 2), (0, 2, 2, 6, 4, 2, 4), (2, 0, 0),
    (0, 1, 3, 1, 0, 3, 3), (0, 0, 3, 1, 0, 3, 1), (2, 2, 6), (1, 2, 0, 1), (1, 3, 4, 4), (2, 3, 4),
    (0, 2, 3, 4, 4, 3, 4), (0, 1, 3, 3, 0, 3, 3), (0, 0, 3, 0, 0, 3, 1), (1, 3, 2, 3), (1, 3, 7, 4), (2, 3, 7),
    (0, 1, 2, 3, 0, 2, 3), (0, 0, 3, 2, 3, 3, 2), (0, 2, 3, 7, 4, 3, 4), (0, 1, 2, 2, 0, 2, 3), (0, 0, 2, 3, 0, 2, 1),
    (0, 2, 1, 4, 4, 1, 4), (1, 3, 1, 1), (0, 1, 3, 1, 1, 3, 2), (0, 0, 2, 1, 0, 2, 1), (0, 2, 1, 5, 4, 1, 4),
    (1, 3, 3, 3), (1, 3, 0, 1), (0, 1, 3, 0, 1, 3, 2), (0, 0, 3, 3, 3, 3, 2), (0, 2, 1, 6, 4, 1, 4), (1, 2, 3, 3),
    (1, 3, 2, 5), (2, 3, 2), (0, 1, 2, 0, 1, 2, 2), (0, 0, 2, 3, 3, 2, 2), (1, 2, 2, 3), (0, 2, 1, 7, 4, 1, 4),
    (0, 0, 2, 2, 3, 2, 2), (1, 3, 1, 5), (2, 3, 1), (1, 2, 1, 1), (0, 1, 2, 1, 1, 2, 2), (1, 3, 0, 5), (1, 3, 3, 5),
    (2, 3, 3), (2, 3, 0), (1, 2, 3, 5), (2, 2, 3), (1, 2, 0, 5), (2, 2, 0), (1, 2, 2, 5), (1, 2, 1, 5), (2, 2, 1),
    (2, 2, 2),
))
GROUPS = ((0, 0, 0, 0, 0, 0, 0, 0, 0, 0, 0, 0, 0, 0, 0, 0, 0, 0, 0, 0, 0, 0, 0, 0, 0, 0, 0, 0, 0, 0, 0, 0, 0, 0, 0, 0, 0, 0, 0, 0, 0, 0, 0, 0, 0, 0, 0, 0, 0, 0, 0, 0, 0, 0, 0, 0, 0, 0, 0, 0, 0, 0, 0, 0, 0, 0, 0, 1), (0, 0, 0, 0, 0, 0, 0, 0, 0, 0, 0, 0, 0, 0, 0, 0, 0, 0, 0, 0, 0, 0, 0, 0, 0, 0, 0, 0, 0, 0, 0, 0, 0, 0, 0, 0, 0, 0, 0, 0, 0, 0, 0, 0, 0, 0, 0, 0, 0, 0, 0, 0, 0, 0, 0, 0, 0, 0, 0, 0, 0, 0, 0, 0, 0, 0, 0, 0, 0, 0, 0, 0, 0, 0, 0, 0, 0, 0, 0, 0, 0, 0, 0, 0, 0, 0, 1, 1, 1, 1, 1, 1, 1, 1, 1, 1, 1, 1, 1, 1))
SHAPES = (((15, 49), (13, 1)), ((16, 62), (15, 12)))
ARRIVALS = tuple(tuple(op[1:] for op in order if op[0] == 1) for order in ORDERS)
ARRIVAL_SEMS = ((0, 1, 2, 3, 4, 5, 6, 7, 8, 9, 10, 11, 12, 13, 14, 15, 16, 17, 18, 19, 20, 0, 1, 21, 9, 3, 4, 13, 7, 22, 10, 5, 18, 11, 15, 19, 16, 1, 6, 17, 14, 9, 8, 12, 2, 23, 24, 25, 21, 26, 0, 27, 28, 29, 20, 30, 31, 32, 33, 34, 35, 36, 37, 38), (0, 1, 2, 3, 4, 5, 6, 7, 8, 9, 10, 11, 12, 13, 14, 15, 16, 17, 18, 19, 20, 21, 22, 0, 23, 24, 25, 26, 27, 1, 28, 6, 7, 5, 9, 3, 8, 2, 10, 12, 19, 4, 11, 0, 15, 29, 22, 26, 20, 25, 6, 28, 1, 27, 24, 23, 21, 18, 17, 16, 14, 30, 31, 13))


def passed_along(block, axis, distance):
    devices = range(lax.axis_size(axis))
    route = [((i - distance) % len(devices), i) for i in devices]
    return lax.ppermute(block, axis, route)


def masked_weight(weight, mask):
    row_blocks, col_blocks = mask.shape
    shaped = weight.reshape(
        row_blocks, weight.shape[0] // row_blocks, col_blocks, weight.shape[1] // col_blocks
    )
    return (shaped * mask.astype(jnp.bfloat16)[:, None, :, None]).reshape(weight.shape)


def project(token_rows, weight):
    return lax.dot_general(
        token_rows, weight, (((1,), (1,)), ((), ())), preferred_element_type=jnp.float32
    )


def gated_block(token_rows, gate_part, up_part):
    gate = project(token_rows, gate_part)
    up_values = project(token_rows, up_part)
    return (jax.nn.silu(gate) * up_values).astype(jnp.bfloat16)


def collect_panels(stacked):
    panel_count = lax.axis_size("panel")
    collected = [(stacked, 0)]
    moving = stacked
    for distance in range(1, panel_count):
        moving = passed_along(moving, "panel", 1)
        collected.append((moving, distance))
    return collected


def general_shards(tokens, gate_weight, up_weight, gate_mask, up_mask):
    panel_count = lax.axis_size("panel")
    my_panel = lax.axis_index("panel")
    width_rows = gate_weight.shape[0]
    stacked = jnp.stack([masked_weight(gate_weight, gate_mask), masked_weight(up_weight, up_mask)])
    collected = collect_panels(stacked)
    gathered = lax.all_gather(tokens, "seq", axis=0, tiled=True)
    tile = jnp.zeros((gathered.shape[0], panel_count * width_rows), jnp.bfloat16)
    for pair, distance in collected:
        source = (my_panel - distance) % panel_count
        result = gated_block(gathered, pair[0], pair[1])
        tile = lax.dynamic_update_slice_in_dim(tile, result, source * width_rows, 1)
    return lax.all_to_all(tile, "seq", split_axis=0, concat_axis=1, tiled=True)


def kernel(
    tok, gw, uw, gm, um, out,
    held, w, turned, masks, wide, hid,
    total, recv_sem, send_sem, part_send, part_recv, local_sem, out_send, out_recv, out_local,
):
    rows, width = tok.shape
    wrows = gw.shape[0]
    seq, panel = lax.axis_index("seq"), lax.axis_index("panel")
    z, x = seq // 2, seq % 2
    y, core = panel // 2, panel % 2

    def device(bz, bx, by):
        return (bz * 2 + bx, by * 2 + core)

    low = z < NZ // 2
    toward = jnp.where(low, 1, -1)
    at_end = jnp.logical_or(z == 0, z == NZ - 1)

    def plane_z(p):
        return jnp.where(low, p, NZ - 1 - p)

    xdev, ydev = device(z, 1 - x, y), device(z, x, 1 - y)
    inward, outward = device(z + toward, x, y), device(z - toward, x, y)
    partner = (seq, y * 2 + 1 - core)

    barrier = pltpu.get_barrier_semaphore()
    for dev in (xdev, ydev, partner, inward):
        pl.semaphore_signal(barrier, inc=1, device_id=dev, device_id_type=MESH)

    @pl.when(jnp.logical_not(at_end))
    def _():
        pl.semaphore_signal(barrier, inc=1, device_id=outward, device_id_type=MESH)

    def slot(p, b):
        return pl.ds((p * 4 + b) * rows, rows) if b < 4 else pl.ds(p * 4 * rows, 4 * rows)

    own = pl.ds(pl.multiple_of(core * wrows, wrows), wrows)
    own_up = pl.ds(pl.multiple_of((2 + core) * wrows, wrows), wrows)
    weight_parts = (
        (gw, w.at[own]), (uw, w.at[own_up]), (gm, masks.at[core]), (um, masks.at[2 + core]),
    )
    keep_tokens = [
        pltpu.make_async_copy(tok, held.at[slot(q, 0)], local_sem.at[2]) for q in range(2)
    ]
    when_q = (at_end, jnp.logical_not(at_end))
    for q in range(2):
        pl.when(when_q[q])(keep_tokens[q].start)
    pl.semaphore_wait(barrier, jnp.where(at_end, 4, 5))
    pltpu.make_async_copy(tok, held.at[slot(0, 0)], local_sem.at[2]).wait()

    unit = width // 64

    def cols(k):
        return pl.ds(PIECES[k][0] * unit, PIECES[k][1] * unit)

    def arrival(q, p, k, b):
        last_hop = b in ((1, 2), (2, 3))[PIECES[k][2]]
        return ARRIVAL_SEMS[q][ARRIVALS[q].index((p, k, 5 if last_hop else b))]

    half = 2 * wrows

    def out_cols(bz, bx, by):
        block = (bz * 2 + bx) * 2 + by
        return pl.ds(pl.multiple_of(block * half, half), half)

    def relative(b):
        return (x + (b in (1, 2))) % 2, (y + (b in (2, 3))) % 2

    swaps = [
        pltpu.make_async_remote_copy(
            src_ref=src, dst_ref=dst, send_sem=part_send.at[i // 2], recv_sem=part_recv.at[i // 2],
            device_id=partner, device_id_type=MESH,
        )
        for i, (src, dst) in enumerate(weight_parts)
    ]

    def prune(i, state):
        if i == 0:
            for j, ref in enumerate((w.at[pl.ds(0, half)], masks.at[pl.ds(0, 2)])):
                for sem in (local_sem, part_send, part_recv):
                    pltpu.make_async_copy(ref, ref, sem.at[j]).wait()
            row = lax.broadcasted_iota(jnp.int32, (8, masks.shape[2]), 0)
            table = jnp.zeros((8, masks.shape[2]), jnp.float32)
            for r in range(4):
                table = jnp.where(row == r, masks[r].astype(jnp.float32), table)
            state["table"] = table.astype(jnp.bfloat16)
        step = width // PRUNES
        block = width // masks.shape[2]
        start = i * step
        where_ = lax.broadcasted_iota(jnp.int32, (masks.shape[2], step), 0)
        col = lax.broadcasted_iota(jnp.int32, (masks.shape[2], step), 1) + start
        first = where_ * block
        inside = jnp.logical_and(col >= first, col < first + block)
        select = jnp.where(inside, 1.0, 0.0).astype(jnp.bfloat16)
        wide[...] = jnp.dot(state["table"], select, preferred_element_type=jnp.float32)
        kept = []
        for r in range(4):
            keep = jnp.broadcast_to(wide[r:r + 1, :], (wrows, step))
            part = w[pl.ds(r * wrows, wrows), pl.ds(start, step)].astype(jnp.float32)
            kept.append((part * keep).astype(jnp.bfloat16))
        turned[pl.ds(start, step), :] = jnp.concatenate(kept, axis=0).T

    def program(q, table):
        links = (xdev, ydev, inward if q == 0 else outward, inward)
        sends, state = [], {}

        def finish(p, both):
            gate = both[:, :half]
            hid[slot(p, 4), :] = (gate / (1.0 + jnp.exp(-gate)) * both[:, half:]).astype(jnp.bfloat16)
            for b in (2, 1, 3, 0):
                if (p, b) == (q, 0):
                    state["kept_out"] = pltpu.make_async_copy(
                        hid.at[slot(p, 0)], out.at[:, out_cols(z, x, y)], out_local
                    )
                    state["kept_out"].start()
                    continue
                tx, ty = relative(b)
                pltpu.make_async_remote_copy(
                    src_ref=hid.at[slot(p, b)], dst_ref=out.at[:, out_cols(z, x, y)],
                    send_sem=out_send, recv_sem=out_recv,
                    device_id=device(plane_z(p), tx, ty), device_id_type=MESH,
                ).start()

        def multiply(p, k):
            at = slot(p, 4)
            both = jnp.dot(held[at, cols(k)], turned[cols(k), :], preferred_element_type=jnp.float32)
            done = state.get(p, 0)
            if done:
                both = both + total[at, :]
            state[p] = done + 1
            if done + 1 < len(PIECES):
                total[at, :] = both
            else:
                finish(p, both)

        for op in table:
            if op[0] == 0:
                _, link, p, k, src, p2, dst = op
                q2 = 1 - q if link == 2 else q
                source = held.at[slot(p, src), cols(k)]
                copy = pltpu.make_async_remote_copy(
                    src_ref=source, dst_ref=held.at[slot(p2, dst), cols(k)],
                    send_sem=send_sem.at[GROUPS[q][len(sends)]], recv_sem=recv_sem.at[arrival(q2, p2, k, dst)],
                    device_id=links[link], device_id_type=MESH,
                )
                copy.start()
                sends.append(op)
            elif op[0] == 1:
                _, p, k, b = op
                at = slot(p, b) if b < 5 else pl.ds((p * 4 + 1 + PIECES[k][2]) * rows, 2 * rows)
                ref = held.at[at, cols(k)]
                pltpu.make_async_copy(ref, ref, recv_sem.at[ARRIVAL_SEMS[q][ARRIVALS[q].index((p, k, b))]]).wait()
            elif op[0] == 2:
                multiply(op[1], op[2])
            elif op[0] == 3:
                prune(op[1], state)
            else:
                for copy in swaps:
                    copy.start()
                for i, (src, dst) in enumerate(weight_parts):
                    pltpu.make_async_copy(src, dst, local_sem.at[i // 2]).start()
        for group, (high, wide_) in enumerate(SHAPES[q]):
            ref = held.at[pl.ds(0, high * rows), pl.ds(0, wide_ * unit)]
            pltpu.make_async_copy(ref, ref, send_sem.at[group]).wait()
        others = 4 * NZ - 1
        ref = hid.at[pl.ds(0, others * rows)]
        pltpu.make_async_copy(ref, ref, out_send).wait()
        state["kept_out"].wait()
        ref = out.at[:, pl.ds(0, others * half)]
        pltpu.make_async_copy(ref, ref, out_recv).wait()

    for q in range(2):
        pl.when(when_q[q])(functools.partial(program, q, ORDERS[q]))


def shards(tokens, gate_weight, up_weight, gate_mask, up_mask):
    rows, width = tokens.shape
    wrows = gate_weight.shape[0]
    blocks = lax.axis_size("seq") * lax.axis_size("panel") // 2
    hidden = lax.axis_size("seq") * lax.axis_size("panel") * wrows
    dma = pltpu.SemaphoreType.DMA
    return pl.pallas_call(
        kernel,
        out_shape=pltpu.VMEM((rows, hidden), jnp.bfloat16),
        in_specs=[pl.BlockSpec(memory_space=pl.ANY)] * 5,
        out_specs=pl.BlockSpec(memory_space=pltpu.VMEM),
        scratch_shapes=[
            pltpu.VMEM((blocks * rows, width), jnp.bfloat16),
            pltpu.VMEM((4 * wrows, width), jnp.bfloat16),
            pltpu.VMEM((width, 4 * wrows), jnp.bfloat16),
            pltpu.VMEM((4, 1, gate_mask.shape[1]), jnp.int32),
            pltpu.VMEM((8, width // PRUNES), jnp.float32),
            pltpu.VMEM((blocks * rows, 2 * wrows), jnp.bfloat16),
            pltpu.VMEM((blocks * rows, 4 * wrows), jnp.float32),
            dma((1 + max(map(max, ARRIVAL_SEMS)),)), dma((max(map(len, SHAPES)),)),
            dma((2,)), dma((2,)), dma((3,)), dma, dma, dma,
        ],
        compiler_params=pltpu.CompilerParams(collective_id=0, has_side_effects=True),
    )(tokens, gate_weight, up_weight, gate_mask, up_mask)


def solution(mesh):
    spec = P(("seq", "panel"), None)
    fits = mesh.shape["seq"] == 2 * NZ and mesh.shape["panel"] == 4
    body = shards if fits else general_shards
    return jax.shard_map(
        body, mesh=mesh, in_specs=(spec,) * 5, out_specs=spec, check_vma=False
    )
```

```python
import functools

import jax
import jax.numpy as jnp
from jax import lax
from jax.experimental import pallas as pl
from jax.experimental.pallas import tpu as pltpu
from jax.sharding import PartitionSpec as P

MESH = pl.DeviceIdType.MESH
NZ = 4
PRUNES = 32
PIECES = ((0, 13, 1), (13, 12, 1), (25, 13, 0), (38, 12, 0), (50, 4, 1), (54, 3, 1), (57, 4, 0), (61, 3, 0))
ORDERS = ((
    (0, 0, 0, 1, 0, 0, 1), (0, 0, 0, 2, 0, 0, 1), (0, 1, 0, 5, 0, 0, 3), (0, 1, 0, 7, 0, 0, 3), (0, 1, 0, 6, 0, 0, 3),
    (0, 1, 0, 4, 0, 0, 3), (0, 2, 0, 1, 0, 0, 0), (0, 2, 0, 3, 0, 0, 0), (0, 1, 0, 1, 0, 0, 3), (0, 2, 0, 0, 0, 0, 0),
    (4, 0), (0, 0, 0, 3, 0, 0, 1), (0, 1, 0, 3, 0, 0, 3), (0, 0, 0, 4, 0, 0, 1), (0, 2, 0, 2, 0, 0, 0),
    (0, 1, 0, 2, 0, 0, 3), (0, 0, 0, 5, 0, 0, 1), (1, 0, 7, 3), (0, 0, 0, 7, 3, 0, 2), (1, 0, 6, 3),
    (0, 0, 0, 6, 3, 0, 2), (1, 0, 1, 1), (1, 1, 1, 0), (0, 1, 1, 1, 0, 1, 3), (0, 0, 0, 6, 0, 0, 1),
    (0, 0, 0, 7, 0, 0, 1), (0, 0, 0, 0, 0, 0, 1), (3, 0), (1, 1, 2, 0), (3, 1), (0, 1, 1, 2, 0, 1, 3), (3, 2), (3, 3),
    (3, 4), (3, 5), (0, 0, 1, 1, 0, 1, 1), (3, 6), (1, 1, 3, 0), (1, 0, 3, 3), (3, 7), (0, 1, 1, 3, 0, 1, 3),
    (1, 0, 4, 1), (3, 8), (3, 9), (1, 0, 5, 1), (3, 10), (0, 0, 0, 3, 3, 0, 2), (3, 11), (1, 1, 0, 0), (3, 12),
    (1, 0, 2, 3), (3, 13), (0, 1, 0, 5, 1, 0, 2), (3, 14), (1, 0, 6, 5), (0, 2, 0, 6, 4, 0, 4), (0, 1, 0, 4, 1, 0, 2),
    (3, 15), (1, 0, 7, 5), (0, 2, 0, 7, 4, 0, 4), (3, 16), (0, 0, 0, 2, 3, 0, 2), (0, 1, 1, 0, 0, 1, 3), (3, 17),
    (1, 2, 1, 0), (3, 18), (3, 19), (3, 20), (3, 21), (1, 0, 0, 1), (3, 22), (0, 0, 2, 1, 0, 2, 1),
    (0, 1, 2, 1, 0, 2, 3), (3, 23), (1, 2, 0, 0), (1, 1, 2, 3), (3, 24), (3, 25), (3, 26), (3, 27), (1, 1, 1, 1),
    (0, 0, 2, 0, 0, 2, 1), (0, 1, 2, 0, 0, 2, 3), (3, 28), (3, 29), (1, 2, 2, 0), (1, 1, 3, 3), (3, 30), (1, 0, 5, 5),
    (0, 2, 0, 5, 4, 0, 4), (3, 31), (2, 0, 6), (1, 0, 3, 5), (1, 0, 4, 5), (0, 2, 0, 4, 4, 0, 4), (2, 0, 7),
    (2, 0, 5), (0, 0, 1, 3, 3, 1, 2), (0, 1, 2, 2, 0, 2, 3), (2, 0, 4), (1, 2, 3, 0), (2, 0, 3), (1, 0, 2, 5),
    (2, 0, 2), (0, 0, 2, 3, 0, 2, 1), (0, 1, 2, 3, 0, 2, 3), (1, 3, 1, 0), (1, 2, 1, 1), (0, 0, 3, 1, 0, 3, 1),
    (0, 1, 2, 1, 1, 2, 2), (1, 3, 3, 0), (1, 2, 0, 1), (0, 0, 3, 3, 0, 3, 1), (0, 1, 3, 3, 0, 3, 3), (1, 3, 0, 0),
    (0, 0, 3, 0, 0, 3, 1), (1, 2, 2, 3), (0, 1, 3, 0, 0, 3, 3), (1, 3, 2, 0), (1, 2, 3, 3), (0, 0, 2, 3, 3, 2, 2),
    (0, 1, 3, 2, 0, 3, 3), (1, 1, 7, 4), (2, 1, 7), (1, 3, 1, 1), (1, 2, 1, 5), (2, 2, 1), (0, 0, 3, 2, 0, 3, 1),
    (0, 1, 3, 1, 1, 3, 2), (1, 2, 6, 4), (2, 2, 6), (1, 3, 3, 3), (0, 0, 2, 2, 3, 2, 2), (0, 1, 3, 1, 0, 3, 3),
    (1, 2, 7, 4), (2, 2, 7), (1, 3, 0, 1), (0, 0, 2, 2, 0, 2, 1), (0, 1, 3, 0, 1, 3, 2), (1, 3, 6, 4), (1, 2, 3, 5),
    (2, 2, 3), (2, 3, 6), (1, 3, 2, 3), (0, 0, 3, 3, 3, 3, 2), (0, 1, 2, 0, 1, 2, 2), (1, 3, 5, 4), (2, 3, 5),
    (0, 0, 3, 2, 3, 3, 2), (0, 1, 0, 0, 1, 0, 2), (1, 3, 7, 4), (2, 3, 7), (1, 3, 1, 5), (2, 3, 1),
    (0, 0, 1, 0, 0, 1, 1), (0, 1, 0, 0, 0, 0, 3), (1, 2, 2, 5), (1, 3, 0, 5), (2, 2, 2), (1, 3, 4, 4), (2, 3, 0),
    (0, 0, 1, 3, 0, 1, 1), (2, 3, 4), (0, 1, 0, 1, 1, 0, 2), (1, 3, 3, 5), (2, 3, 3), (1, 2, 0, 5), (2, 2, 0),
    (0, 0, 1, 2, 0, 1, 1), (0, 1, 1, 1, 1, 1, 2), (1, 2, 4, 4), (2, 2, 4), (1, 3, 2, 5), (2, 3, 2),
    (0, 0, 1, 2, 3, 1, 2), (1, 2, 5, 4), (2, 2, 5), (1, 1, 0, 1), (0, 1, 1, 0, 1, 1, 2), (1, 0, 0, 5), (2, 0, 0),
    (1, 1, 6, 4), (2, 1, 6), (1, 1, 3, 5), (2, 1, 3), (1, 0, 1, 5), (2, 0, 1), (1, 1, 4, 4), (2, 1, 4), (1, 1, 1, 5),
    (2, 1, 1), (1, 1, 5, 4), (2, 1, 5), (1, 1, 2, 5), (1, 1, 0, 5), (2, 1, 2), (2, 1, 0),
), (
    (0, 0, 1, 4, 0, 1, 1), (0, 0, 1, 6, 0, 1, 1), (0, 0, 1, 5, 0, 1, 1), (0, 0, 1, 7, 0, 1, 1), (0, 1, 1, 4, 0, 1, 3),
    (0, 1, 1, 7, 0, 1, 3), (0, 1, 1, 6, 0, 1, 3), (0, 1, 1, 5, 0, 1, 3), (0, 2, 1, 1, 0, 1, 0), (0, 2, 1, 2, 0, 1, 0),
    (0, 3, 1, 1, 0, 2, 0), (0, 3, 1, 0, 0, 2, 0), (0, 0, 1, 1, 0, 1, 1), (0, 1, 1, 3, 0, 1, 3), (4, 0),
    (0, 2, 1, 3, 0, 1, 0), (0, 3, 1, 2, 0, 2, 0), (0, 0, 1, 3, 0, 1, 1), (0, 1, 1, 1, 0, 1, 3), (0, 2, 1, 0, 0, 1, 0),
    (0, 3, 1, 3, 0, 2, 0), (0, 0, 1, 0, 0, 1, 1), (0, 1, 1, 0, 0, 1, 3), (1, 1, 4, 1), (1, 1, 7, 3), (1, 1, 5, 1),
    (1, 1, 6, 3), (1, 0, 1, 0), (1, 2, 1, 0), (0, 3, 0, 1, 0, 3, 0), (0, 2, 2, 1, 0, 2, 0), (0, 0, 1, 6, 3, 1, 2),
    (0, 1, 0, 1, 0, 0, 3), (0, 0, 1, 7, 3, 1, 2), (0, 0, 0, 1, 0, 0, 1), (3, 0), (1, 0, 3, 0), (1, 2, 0, 0), (3, 1),
    (1, 1, 1, 1), (1, 1, 3, 3), (0, 3, 0, 3, 0, 3, 0), (0, 2, 2, 0, 0, 2, 0), (0, 1, 0, 3, 0, 0, 3), (3, 2), (3, 3),
    (3, 4), (3, 5), (0, 0, 1, 3, 3, 1, 2), (3, 6), (1, 0, 0, 0), (1, 2, 2, 0), (0, 3, 0, 0, 0, 3, 0), (3, 7),
    (0, 1, 0, 0, 0, 0, 3), (0, 2, 2, 2, 0, 2, 0), (3, 8), (3, 9), (3, 10), (0, 0, 0, 3, 0, 0, 1), (3, 11),
    (1, 0, 2, 0), (1, 2, 3, 0), (3, 12), (1, 1, 0, 1), (0, 3, 0, 2, 0, 3, 0), (3, 13), (0, 1, 0, 2, 0, 0, 3),
    (0, 2, 2, 3, 0, 2, 0), (3, 14), (1, 1, 6, 5), (3, 15), (1, 1, 7, 5), (3, 16), (0, 0, 0, 2, 0, 0, 1), (3, 17),
    (1, 3, 1, 0), (3, 18), (0, 2, 3, 1, 0, 3, 0), (0, 3, 1, 6, 4, 2, 4), (3, 19), (0, 1, 2, 1, 0, 2, 3), (3, 20),
    (3, 21), (1, 0, 1, 1), (0, 0, 3, 1, 0, 3, 1), (3, 22), (1, 3, 3, 0), (3, 23), (1, 0, 3, 3), (3, 24),
    (0, 2, 3, 3, 0, 3, 0), (0, 1, 3, 1, 0, 3, 3), (3, 25), (3, 26), (0, 3, 1, 7, 4, 2, 4), (1, 1, 3, 5), (3, 27),
    (0, 0, 0, 0, 0, 0, 1), (3, 28), (1, 3, 0, 0), (3, 29), (0, 2, 3, 0, 0, 3, 0), (3, 30), (0, 1, 3, 0, 0, 3, 3),
    (3, 31), (1, 0, 6, 4), (0, 3, 0, 6, 4, 3, 4), (2, 1, 6), (2, 1, 7), (2, 1, 3), (0, 0, 3, 0, 0, 3, 1), (2, 0, 6),
    (1, 3, 2, 0), (1, 0, 2, 3), (0, 2, 3, 2, 0, 3, 0), (0, 1, 3, 3, 0, 3, 3), (1, 0, 7, 4), (2, 0, 7),
    (0, 3, 0, 7, 4, 3, 4), (0, 0, 3, 2, 0, 3, 1), (0, 2, 1, 7, 4, 1, 4), (0, 1, 3, 2, 0, 3, 3), (1, 2, 6, 4),
    (2, 2, 6), (1, 3, 1, 1), (0, 0, 3, 3, 0, 3, 1), (1, 0, 5, 4), (0, 3, 0, 5, 4, 3, 4), (2, 0, 5),
    (0, 2, 2, 6, 4, 2, 4), (0, 1, 1, 4, 1, 1, 2), (1, 2, 7, 4), (2, 2, 7), (0, 1, 1, 5, 1, 1, 2), (1, 0, 0, 1),
    (0, 0, 1, 2, 0, 1, 1), (0, 1, 1, 1, 1, 1, 2), (1, 0, 4, 4), (0, 3, 0, 4, 4, 3, 4), (2, 0, 4),
    (0, 2, 2, 7, 4, 2, 4), (1, 3, 6, 4), (2, 3, 6), (1, 3, 0, 1), (0, 1, 1, 0, 1, 1, 2), (0, 0, 0, 3, 3, 0, 2),
    (1, 3, 3, 3), (0, 2, 3, 6, 4, 3, 4), (1, 3, 7, 4), (2, 3, 7), (0, 1, 2, 3, 0, 2, 3), (0, 0, 3, 3, 3, 3, 2),
    (1, 3, 2, 3), (1, 1, 4, 5), (0, 3, 1, 4, 4, 2, 4), (2, 1, 4), (1, 3, 5, 4), (2, 3, 5), (1, 1, 5, 5),
    (0, 3, 1, 5, 4, 2, 4), (2, 1, 5), (0, 2, 3, 5, 4, 3, 4), (0, 1, 2, 2, 0, 2, 3), (0, 0, 3, 2, 3, 3, 2),
    (1, 1, 1, 5), (2, 1, 1), (0, 2, 3, 7, 4, 3, 4), (1, 3, 4, 4), (2, 3, 4), (0, 1, 3, 0, 1, 3, 2),
    (0, 0, 2, 3, 0, 2, 1), (0, 2, 3, 4, 4, 3, 4), (1, 1, 0, 5), (1, 0, 3, 5), (2, 0, 3), (2, 1, 0),
    (0, 0, 2, 1, 0, 2, 1), (0, 1, 0, 1, 1, 0, 2), (1, 2, 4, 4), (2, 2, 4), (1, 2, 3, 3), (1, 3, 3, 5), (2, 3, 3),
    (0, 0, 2, 3, 3, 2, 2), (0, 1, 1, 2, 0, 1, 3), (0, 2, 2, 4, 4, 2, 4), (1, 2, 5, 4), (2, 2, 5), (1, 2, 2, 3),
    (1, 3, 2, 5), (2, 3, 2), (0, 0, 2, 0, 0, 2, 1), (0, 1, 0, 0, 1, 0, 2), (0, 2, 2, 5, 4, 2, 4), (1, 3, 0, 5),
    (2, 3, 0), (0, 0, 2, 2, 0, 2, 1), (0, 1, 3, 1, 1, 3, 2), (0, 2, 1, 6, 4, 1, 4), (1, 2, 1, 1), (1, 0, 1, 5),
    (2, 0, 1), (0, 0, 0, 2, 3, 0, 2), (0, 1, 2, 1, 1, 2, 2), (0, 2, 1, 4, 4, 1, 4), (1, 2, 3, 5), (2, 2, 3),
    (1, 1, 2, 3), (0, 0, 1, 2, 3, 1, 2), (0, 1, 2, 0, 0, 2, 3), (1, 2, 0, 1), (0, 2, 1, 5, 4, 1, 4), (1, 0, 0, 5),
    (2, 0, 0), (0, 0, 2, 2, 3, 2, 2), (0, 1, 2, 0, 1, 2, 2), (1, 3, 1, 5), (2, 3, 1), (1, 0, 2, 5), (1, 2, 1, 5),
    (2, 2, 1), (2, 0, 2), (1, 1, 2, 5), (2, 1, 2), (1, 2, 2, 5), (1, 2, 0, 5), (2, 2, 0), (2, 2, 2),
))
GROUPS = ((0, 0, 0, 0, 0, 0, 0, 0, 0, 0, 0, 0, 0, 0, 0, 0, 0, 0, 0, 0, 0, 0, 0, 0, 0, 0, 0, 0, 0, 0, 0, 0, 0, 0, 0, 0, 0, 0, 0, 0, 0, 0, 0, 0, 0, 0, 0, 0, 0, 0, 0, 0, 0, 0, 0, 0, 0, 0, 0, 0, 0, 0, 0, 0, 0, 0, 0, 1), (0, 0, 0, 0, 0, 0, 0, 0, 0, 0, 0, 0, 0, 0, 0, 0, 0, 0, 0, 0, 0, 0, 0, 0, 0, 0, 0, 0, 0, 0, 0, 0, 0, 0, 0, 0, 0, 0, 0, 0, 0, 0, 0, 0, 0, 0, 0, 0, 0, 0, 0, 0, 0, 0, 0, 0, 0, 0, 0, 0, 0, 0, 0, 0, 0, 0, 0, 0, 0, 0, 0, 0, 0, 0, 0, 0, 0, 0, 1, 1, 1, 1, 1, 1, 1, 1, 1, 1, 1, 1, 1, 1, 1, 1, 1, 1, 1, 1, 1, 1))
SHAPES = (((15, 49), (13, 1)), ((14, 63), (10, 29)))
ARRIVALS = tuple(tuple(op[1:] for op in order if op[0] == 1) for order in ORDERS)
ARRIVAL_SEMS = ((0, 1, 2, 3, 4, 5, 6, 7, 8, 9, 10, 11, 12, 13, 14, 15, 16, 17, 18, 19, 20, 21, 22, 23, 24, 25, 0, 26, 3, 27, 1, 7, 2, 5, 12, 28, 19, 8, 16, 10, 13, 6, 23, 17, 18, 25, 24, 9, 20, 15, 4, 22, 0, 21, 27, 3, 14, 29, 30, 11, 31, 32, 26, 33), (0, 1, 2, 3, 4, 5, 6, 7, 8, 9, 10, 11, 12, 13, 14, 15, 16, 17, 18, 19, 20, 21, 22, 23, 24, 25, 26, 4, 1, 8, 5, 6, 11, 10, 3, 12, 14, 13, 27, 16, 28, 29, 20, 30, 31, 26, 24, 17, 1, 4, 9, 7, 23, 32, 21, 25, 22, 33, 2, 0, 34, 19, 18, 15))


def passed_along(block, axis, distance):
    devices = range(lax.axis_size(axis))
    route = [((i - distance) % len(devices), i) for i in devices]
    return lax.ppermute(block, axis, route)


def masked_weight(weight, mask):
    row_blocks, col_blocks = mask.shape
    shaped = weight.reshape(
        row_blocks, weight.shape[0] // row_blocks, col_blocks, weight.shape[1] // col_blocks
    )
    return (shaped * mask.astype(jnp.bfloat16)[:, None, :, None]).reshape(weight.shape)


def project(token_rows, weight):
    return lax.dot_general(
        token_rows, weight, (((1,), (1,)), ((), ())), preferred_element_type=jnp.float32
    )


def gated_block(token_rows, gate_part, up_part):
    gate = project(token_rows, gate_part)
    up_values = project(token_rows, up_part)
    return (jax.nn.silu(gate) * up_values).astype(jnp.bfloat16)


def collect_panels(stacked):
    panel_count = lax.axis_size("panel")
    collected = [(stacked, 0)]
    moving = stacked
    for distance in range(1, panel_count):
        moving = passed_along(moving, "panel", 1)
        collected.append((moving, distance))
    return collected


def general_shards(tokens, gate_weight, up_weight, gate_mask, up_mask):
    panel_count = lax.axis_size("panel")
    my_panel = lax.axis_index("panel")
    width_rows = gate_weight.shape[0]
    stacked = jnp.stack([masked_weight(gate_weight, gate_mask), masked_weight(up_weight, up_mask)])
    collected = collect_panels(stacked)
    gathered = lax.all_gather(tokens, "seq", axis=0, tiled=True)
    tile = jnp.zeros((gathered.shape[0], panel_count * width_rows), jnp.bfloat16)
    for pair, distance in collected:
        source = (my_panel - distance) % panel_count
        result = gated_block(gathered, pair[0], pair[1])
        tile = lax.dynamic_update_slice_in_dim(tile, result, source * width_rows, 1)
    return lax.all_to_all(tile, "seq", split_axis=0, concat_axis=1, tiled=True)


def kernel(
    tok, gw, uw, gm, um, out,
    held, w, turned, masks, wide, hid,
    total, recv_sem, send_sem, part_send, part_recv, local_sem, out_send, out_recv, out_local,
):
    rows, width = tok.shape
    wrows = gw.shape[0]
    seq, panel = lax.axis_index("seq"), lax.axis_index("panel")
    z, x = seq // 2, seq % 2
    y, core = panel // 2, panel % 2

    def device(bz, bx, by):
        return (bz * 2 + bx, by * 2 + core)

    low = z < NZ // 2
    toward = jnp.where(low, 1, -1)
    at_end = jnp.logical_or(z == 0, z == NZ - 1)

    def plane_z(p):
        return jnp.where(low, p, NZ - 1 - p)

    xdev, ydev = device(z, 1 - x, y), device(z, x, 1 - y)
    inward, outward = device(z + toward, x, y), device(z - toward, x, y)
    partner = (seq, y * 2 + 1 - core)

    barrier = pltpu.get_barrier_semaphore()
    for dev in (xdev, ydev, partner, inward):
        pl.semaphore_signal(barrier, inc=1, device_id=dev, device_id_type=MESH)

    @pl.when(jnp.logical_not(at_end))
    def _():
        pl.semaphore_signal(barrier, inc=1, device_id=outward, device_id_type=MESH)

    def slot(p, b):
        return pl.ds((p * 4 + b) * rows, rows) if b < 4 else pl.ds(p * 4 * rows, 4 * rows)

    own = pl.ds(pl.multiple_of(core * wrows, wrows), wrows)
    own_up = pl.ds(pl.multiple_of((2 + core) * wrows, wrows), wrows)
    weight_parts = (
        (gw, w.at[own]), (uw, w.at[own_up]), (gm, masks.at[core]), (um, masks.at[2 + core]),
    )
    keep_tokens = [
        pltpu.make_async_copy(tok, held.at[slot(q, 0)], local_sem.at[2]) for q in range(2)
    ]
    when_q = (at_end, jnp.logical_not(at_end))
    for q in range(2):
        pl.when(when_q[q])(keep_tokens[q].start)
    pl.semaphore_wait(barrier, jnp.where(at_end, 4, 5))
    pltpu.make_async_copy(tok, held.at[slot(0, 0)], local_sem.at[2]).wait()

    unit = width // 64

    def cols(k):
        return pl.ds(PIECES[k][0] * unit, PIECES[k][1] * unit)

    def arrival(q, p, k, b):
        last_hop = b in ((1, 2), (2, 3))[PIECES[k][2]]
        return ARRIVAL_SEMS[q][ARRIVALS[q].index((p, k, 5 if last_hop else b))]

    half = 2 * wrows

    def out_cols(bz, bx, by):
        block = (bz * 2 + bx) * 2 + by
        return pl.ds(pl.multiple_of(block * half, half), half)

    def relative(b):
        return (x + (b in (1, 2))) % 2, (y + (b in (2, 3))) % 2

    swaps = [
        pltpu.make_async_remote_copy(
            src_ref=src, dst_ref=dst, send_sem=part_send.at[i // 2], recv_sem=part_recv.at[i // 2],
            device_id=partner, device_id_type=MESH,
        )
        for i, (src, dst) in enumerate(weight_parts)
    ]

    def prune(i, state):
        if i == 0:
            for j, ref in enumerate((w.at[pl.ds(0, half)], masks.at[pl.ds(0, 2)])):
                for sem in (local_sem, part_send, part_recv):
                    pltpu.make_async_copy(ref, ref, sem.at[j]).wait()
            row = lax.broadcasted_iota(jnp.int32, (8, masks.shape[2]), 0)
            table = jnp.zeros((8, masks.shape[2]), jnp.float32)
            for r in range(4):
                table = jnp.where(row == r, masks[r].astype(jnp.float32), table)
            state["table"] = table.astype(jnp.bfloat16)
        step = width // PRUNES
        block = width // masks.shape[2]
        start = i * step
        where_ = lax.broadcasted_iota(jnp.int32, (masks.shape[2], step), 0)
        col = lax.broadcasted_iota(jnp.int32, (masks.shape[2], step), 1) + start
        first = where_ * block
        inside = jnp.logical_and(col >= first, col < first + block)
        select = jnp.where(inside, 1.0, 0.0).astype(jnp.bfloat16)
        wide[...] = jnp.dot(state["table"], select, preferred_element_type=jnp.float32)
        kept = []
        for r in range(4):
            keep = jnp.broadcast_to(wide[r:r + 1, :], (wrows, step))
            part = w[pl.ds(r * wrows, wrows), pl.ds(start, step)].astype(jnp.float32)
            kept.append((part * keep).astype(jnp.bfloat16))
        turned[pl.ds(start, step), :] = jnp.concatenate(kept, axis=0).T

    def program(q, table):
        links = (xdev, ydev, inward if q == 0 else outward, inward)
        sends, state = [], {}

        def finish(p, both):
            gate = both[:, :half]
            hid[slot(p, 4), :] = (gate / (1.0 + jnp.exp(-gate)) * both[:, half:]).astype(jnp.bfloat16)
            for b in (2, 1, 3, 0):
                if (p, b) == (q, 0):
                    state["kept_out"] = pltpu.make_async_copy(
                        hid.at[slot(p, 0)], out.at[:, out_cols(z, x, y)], out_local
                    )
                    state["kept_out"].start()
                    continue
                tx, ty = relative(b)
                pltpu.make_async_remote_copy(
                    src_ref=hid.at[slot(p, b)], dst_ref=out.at[:, out_cols(z, x, y)],
                    send_sem=out_send, recv_sem=out_recv,
                    device_id=device(plane_z(p), tx, ty), device_id_type=MESH,
                ).start()

        def multiply(p, k):
            at = slot(p, 4)
            both = jnp.dot(held[at, cols(k)], turned[cols(k), :], preferred_element_type=jnp.float32)
            done = state.get(p, 0)
            if done:
                both = both + total[at, :]
            state[p] = done + 1
            if done + 1 < len(PIECES):
                total[at, :] = both
            else:
                finish(p, both)

        for op in table:
            if op[0] == 0:
                _, link, p, k, src, p2, dst = op
                q2 = 1 - q if link == 2 else q
                source = held.at[slot(p, src), cols(k)]
                copy = pltpu.make_async_remote_copy(
                    src_ref=source, dst_ref=held.at[slot(p2, dst), cols(k)],
                    send_sem=send_sem.at[GROUPS[q][len(sends)]], recv_sem=recv_sem.at[arrival(q2, p2, k, dst)],
                    device_id=links[link], device_id_type=MESH,
                )
                copy.start()
                sends.append(op)
            elif op[0] == 1:
                _, p, k, b = op
                at = slot(p, b) if b < 5 else pl.ds((p * 4 + 1 + PIECES[k][2]) * rows, 2 * rows)
                ref = held.at[at, cols(k)]
                pltpu.make_async_copy(ref, ref, recv_sem.at[ARRIVAL_SEMS[q][ARRIVALS[q].index((p, k, b))]]).wait()
            elif op[0] == 2:
                multiply(op[1], op[2])
            elif op[0] == 3:
                prune(op[1], state)
            else:
                for copy in swaps:
                    copy.start()
                for i, (src, dst) in enumerate(weight_parts):
                    pltpu.make_async_copy(src, dst, local_sem.at[i // 2]).start()
        for group, (high, wide_) in enumerate(SHAPES[q]):
            ref = held.at[pl.ds(0, high * rows), pl.ds(0, wide_ * unit)]
            pltpu.make_async_copy(ref, ref, send_sem.at[group]).wait()
        others = 4 * NZ - 1
        ref = hid.at[pl.ds(0, others * rows)]
        pltpu.make_async_copy(ref, ref, out_send).wait()
        state["kept_out"].wait()
        ref = out.at[:, pl.ds(0, others * half)]
        pltpu.make_async_copy(ref, ref, out_recv).wait()

    for q in range(2):
        pl.when(when_q[q])(functools.partial(program, q, ORDERS[q]))


def shards(tokens, gate_weight, up_weight, gate_mask, up_mask):
    rows, width = tokens.shape
    wrows = gate_weight.shape[0]
    blocks = lax.axis_size("seq") * lax.axis_size("panel") // 2
    hidden = lax.axis_size("seq") * lax.axis_size("panel") * wrows
    dma = pltpu.SemaphoreType.DMA
    return pl.pallas_call(
        kernel,
        out_shape=pltpu.VMEM((rows, hidden), jnp.bfloat16),
        in_specs=[pl.BlockSpec(memory_space=pl.ANY)] * 5,
        out_specs=pl.BlockSpec(memory_space=pltpu.VMEM),
        scratch_shapes=[
            pltpu.VMEM((blocks * rows, width), jnp.bfloat16),
            pltpu.VMEM((4 * wrows, width), jnp.bfloat16),
            pltpu.VMEM((width, 4 * wrows), jnp.bfloat16),
            pltpu.VMEM((4, 1, gate_mask.shape[1]), jnp.int32),
            pltpu.VMEM((8, width // PRUNES), jnp.float32),
            pltpu.VMEM((blocks * rows, 2 * wrows), jnp.bfloat16),
            pltpu.VMEM((blocks * rows, 4 * wrows), jnp.float32),
            dma((1 + max(map(max, ARRIVAL_SEMS)),)), dma((max(map(len, SHAPES)),)),
            dma((2,)), dma((2,)), dma((3,)), dma, dma, dma,
        ],
        compiler_params=pltpu.CompilerParams(collective_id=0, has_side_effects=True),
    )(tokens, gate_weight, up_weight, gate_mask, up_mask)


def solution(mesh):
    spec = P(("seq", "panel"), None)
    fits = mesh.shape["seq"] == 2 * NZ and mesh.shape["panel"] == 4
    body = shards if fits else general_shards
    return jax.shard_map(
        body, mesh=mesh, in_specs=(spec,) * 5, out_specs=spec, check_vma=False
    )
```

```python
import functools

import jax
import jax.numpy as jnp
from jax import lax
from jax.experimental import pallas as pl
from jax.experimental.pallas import tpu as pltpu
from jax.sharding import PartitionSpec as P

MESH = pl.DeviceIdType.MESH
NZ = 4
PRUNES = 32
PIECES = ((0, 13, 1), (13, 12, 1), (25, 13, 0), (38, 12, 0), (50, 4, 1), (54, 3, 1), (57, 4, 0), (61, 3, 0))
ORDERS = ((
    (0, 0, 0, 1, 0, 0, 1), (0, 0, 0, 2, 0, 0, 1), (0, 1, 0, 5, 0, 0, 3), (0, 1, 0, 7, 0, 0, 3), (0, 1, 0, 6, 0, 0, 3),
    (0, 1, 0, 4, 0, 0, 3), (0, 2, 0, 1, 0, 0, 0), (0, 2, 0, 3, 0, 0, 0), (0, 1, 0, 1, 0, 0, 3), (0, 2, 0, 0, 0, 0, 0),
    (4, 0), (0, 0, 0, 3, 0, 0, 1), (0, 1, 0, 3, 0, 0, 3), (0, 0, 0, 4, 0, 0, 1), (0, 2, 0, 2, 0, 0, 0),
    (0, 1, 0, 2, 0, 0, 3), (0, 0, 0, 5, 0, 0, 1), (1, 0, 7, 3), (0, 0, 0, 7, 3, 0, 2), (1, 0, 6, 3),
    (0, 0, 0, 6, 3, 0, 2), (1, 0, 1, 1), (1, 1, 1, 0), (0, 1, 1, 1, 0, 1, 3), (0, 0, 0, 6, 0, 0, 1),
    (0, 0, 0, 7, 0, 0, 1), (0, 0, 0, 0, 0, 0, 1), (3, 0), (1, 1, 2, 0), (3, 1), (3, 2), (0, 1, 1, 2, 0, 1, 3), (3, 3),
    (3, 4), (3, 5), (3, 6), (0, 0, 1, 1, 0, 1, 1), (1, 1, 3, 0), (3, 7), (1, 0, 3, 3), (3, 8), (0, 1, 1, 3, 0, 1, 3),
    (1, 0, 4, 1), (3, 9), (3, 10), (1, 0, 5, 1), (3, 11), (0, 0, 0, 3, 3, 0, 2), (3, 12), (3, 13), (1, 1, 0, 0),
    (1, 0, 2, 3), (3, 14), (0, 1, 0, 5, 1, 0, 2), (3, 15), (1, 0, 6, 5), (0, 2, 0, 6, 4, 0, 4), (0, 1, 0, 4, 1, 0, 2),
    (3, 16), (3, 17), (1, 0, 7, 5), (0, 2, 0, 7, 4, 0, 4), (0, 0, 0, 2, 3, 0, 2), (0, 1, 1, 0, 0, 1, 3), (3, 18),
    (3, 19), (1, 2, 1, 0), (3, 20), (3, 21), (3, 22), (3, 23), (1, 0, 0, 1), (3, 24), (0, 0, 2, 1, 0, 2, 1),
    (0, 1, 2, 1, 0, 2, 3), (3, 25), (1, 2, 0, 0), (1, 1, 2, 3), (3, 26), (3, 27), (3, 28), (3, 29), (1, 1, 1, 1),
    (3, 30), (0, 0, 2, 0, 0, 2, 1), (0, 1, 2, 0, 0, 2, 3), (3, 31), (2, 0, 6), (2, 0, 7), (1, 2, 2, 0), (1, 1, 3, 3),
    (1, 0, 5, 5), (0, 2, 0, 5, 4, 0, 4), (2, 0, 5), (1, 0, 3, 5), (1, 0, 4, 5), (0, 2, 0, 4, 4, 0, 4), (2, 0, 4),
    (2, 0, 3), (0, 0, 1, 3, 3, 1, 2), (0, 1, 2, 2, 0, 2, 3), (1, 2, 3, 0), (1, 0, 2, 5), (2, 0, 2),
    (0, 0, 2, 3, 0, 2, 1), (0, 1, 2, 3, 0, 2, 3), (1, 3, 1, 0), (1, 2, 1, 1), (0, 0, 3, 1, 0, 3, 1),
    (0, 1, 2, 1, 1, 2, 2), (1, 3, 3, 0), (1, 2, 0, 1), (0, 0, 3, 3, 0, 3, 1), (0, 1, 3, 3, 0, 3, 3), (1, 3, 0, 0),
    (0, 0, 3, 0, 0, 3, 1), (1, 2, 2, 3), (0, 1, 3, 0, 0, 3, 3), (1, 3, 2, 0), (1, 2, 3, 3), (0, 0, 2, 3, 3, 2, 2),
    (0, 1, 3, 2, 0, 3, 3), (1, 1, 7, 4), (2, 1, 7), (1, 3, 1, 1), (1, 2, 1, 5), (2, 2, 1), (0, 0, 3, 2, 0, 3, 1),
    (0, 1, 3, 1, 1, 3, 2), (1, 2, 6, 4), (2, 2, 6), (1, 3, 3, 3), (0, 0, 2, 2, 3, 2, 2), (0, 1, 3, 1, 0, 3, 3),
    (1, 2, 7, 4), (2, 2, 7), (1, 3, 0, 1), (0, 0, 2, 2, 0, 2, 1), (0, 1, 3, 0, 1, 3, 2), (1, 3, 6, 4), (1, 2, 3, 5),
    (2, 2, 3), (2, 3, 6), (1, 3, 2, 3), (0, 0, 3, 3, 3, 3, 2), (0, 1, 2, 0, 1, 2, 2), (1, 3, 5, 4), (2, 3, 5),
    (0, 0, 3, 2, 3, 3, 2), (0, 1, 0, 0, 1, 0, 2), (1, 3, 7, 4), (2, 3, 7), (1, 3, 1, 5), (2, 3, 1),
    (0, 0, 1, 0, 0, 1, 1), (0, 1, 0, 0, 0, 0, 3), (1, 2, 2, 5), (1, 3, 0, 5), (2, 2, 2), (2, 3, 0), (1, 3, 4, 4),
    (2, 3, 4), (0, 0, 1, 3, 0, 1, 1), (0, 1, 0, 1, 1, 0, 2), (1, 3, 3, 5), (2, 3, 3), (1, 2, 0, 5), (2, 2, 0),
    (0, 0, 1, 2, 0, 1, 1), (0, 1, 1, 1, 1, 1, 2), (1, 2, 4, 4), (2, 2, 4), (1, 3, 2, 5), (2, 3, 2),
    (0, 0, 1, 2, 3, 1, 2), (1, 2, 5, 4), (2, 2, 5), (1, 1, 0, 1), (0, 1, 1, 0, 1, 1, 2), (1, 0, 0, 5), (2, 0, 0),
    (1, 1, 6, 4), (2, 1, 6), (1, 1, 3, 5), (2, 1, 3), (1, 0, 1, 5), (2, 0, 1), (1, 1, 4, 4), (2, 1, 4), (1, 1, 1, 5),
    (2, 1, 1), (1, 1, 5, 4), (2, 1, 5), (1, 1, 2, 5), (1, 1, 0, 5), (2, 1, 2), (2, 1, 0),
), (
    (0, 0, 1, 4, 0, 1, 1), (0, 0, 1, 6, 0, 1, 1), (0, 0, 1, 5, 0, 1, 1), (0, 0, 1, 7, 0, 1, 1), (0, 1, 1, 4, 0, 1, 3),
    (0, 1, 1, 7, 0, 1, 3), (0, 1, 1, 6, 0, 1, 3), (0, 1, 1, 5, 0, 1, 3), (0, 2, 1, 1, 0, 1, 0), (0, 2, 1, 2, 0, 1, 0),
    (0, 3, 1, 1, 0, 2, 0), (0, 3, 1, 0, 0, 2, 0), (0, 0, 1, 1, 0, 1, 1), (0, 1, 1, 3, 0, 1, 3), (4, 0),
    (0, 2, 1, 3, 0, 1, 0), (0, 3, 1, 2, 0, 2, 0), (0, 0, 1, 3, 0, 1, 1), (0, 1, 1, 1, 0, 1, 3), (0, 2, 1, 0, 0, 1, 0),
    (0, 3, 1, 3, 0, 2, 0), (0, 0, 1, 0, 0, 1, 1), (0, 1, 1, 0, 0, 1, 3), (1, 1, 4, 1), (1, 1, 7, 3), (1, 1, 5, 1),
    (1, 1, 6, 3), (1, 0, 1, 0), (1, 2, 1, 0), (0, 3, 0, 1, 0, 3, 0), (0, 2, 2, 1, 0, 2, 0), (0, 0, 1, 6, 3, 1, 2),
    (0, 1, 0, 1, 0, 0, 3), (0, 0, 1, 7, 3, 1, 2), (0, 0, 0, 1, 0, 0, 1), (3, 0), (1, 0, 3, 0), (1, 2, 0, 0), (3, 1),
    (1, 1, 1, 1), (1, 1, 3, 3), (0, 3, 0, 3, 0, 3, 0), (0, 2, 2, 0, 0, 2, 0), (3, 2), (0, 1, 0, 3, 0, 0, 3), (3, 3),
    (3, 4), (3, 5), (0, 0, 1, 3, 3, 1, 2), (3, 6), (1, 0, 0, 0), (3, 7), (1, 2, 2, 0), (0, 3, 0, 0, 0, 3, 0), (3, 8),
    (0, 1, 0, 0, 0, 0, 3), (0, 2, 2, 2, 0, 2, 0), (3, 9), (3, 10), (3, 11), (0, 0, 0, 3, 0, 0, 1), (3, 12), (3, 13),
    (1, 0, 2, 0), (1, 2, 3, 0), (1, 1, 0, 1), (0, 3, 0, 2, 0, 3, 0), (3, 14), (0, 1, 0, 2, 0, 0, 3),
    (0, 2, 2, 3, 0, 2, 0), (3, 15), (1, 1, 6, 5), (3, 16), (3, 17), (1, 1, 7, 5), (0, 0, 0, 2, 0, 0, 1), (3, 18),
    (3, 19), (1, 3, 1, 0), (3, 20), (0, 2, 3, 1, 0, 3, 0), (0, 3, 1, 6, 4, 2, 4), (0, 1, 2, 1, 0, 2, 3), (3, 21),
    (3, 22), (3, 23), (1, 0, 1, 1), (0, 0, 3, 1, 0, 3, 1), (3, 24), (1, 3, 3, 0), (3, 25), (1, 0, 3, 3), (3, 26),
    (0, 2, 3, 3, 0, 3, 0), (0, 1, 3, 1, 0, 3, 3), (3, 27), (3, 28), (0, 3, 1, 7, 4, 2, 4), (1, 1, 3, 5), (3, 29),
    (0, 0, 0, 0, 0, 0, 1), (3, 30), (3, 31), (2, 1, 6), (2, 1, 7), (2, 1, 3), (1, 3, 0, 0), (0, 2, 3, 0, 0, 3, 0),
    (0, 1, 3, 0, 0, 3, 3), (1, 0, 6, 4), (2, 0, 6), (0, 3, 0, 6, 4, 3, 4), (0, 0, 3, 0, 0, 3, 1), (1, 3, 2, 0),
    (1, 0, 2, 3), (0, 2, 3, 2, 0, 3, 0), (0, 1, 3, 3, 0, 3, 3), (1, 0, 7, 4), (2, 0, 7), (0, 3, 0, 7, 4, 3, 4),
    (0, 0, 3, 2, 0, 3, 1), (0, 2, 1, 7, 4, 1, 4), (0, 1, 3, 2, 0, 3, 3), (1, 2, 6, 4), (2, 2, 6), (1, 3, 1, 1),
    (0, 0, 3, 3, 0, 3, 1), (1, 0, 5, 4), (0, 3, 0, 5, 4, 3, 4), (2, 0, 5), (0, 2, 2, 6, 4, 2, 4),
    (0, 1, 1, 4, 1, 1, 2), (1, 2, 7, 4), (2, 2, 7), (0, 1, 1, 5, 1, 1, 2), (1, 0, 0, 1), (0, 0, 1, 2, 0, 1, 1),
    (0, 1, 1, 1, 1, 1, 2), (1, 0, 4, 4), (0, 3, 0, 4, 4, 3, 4), (2, 0, 4), (0, 2, 2, 7, 4, 2, 4), (1, 3, 6, 4),
    (2, 3, 6), (1, 3, 0, 1), (0, 1, 1, 0, 1, 1, 2), (0, 0, 0, 3, 3, 0, 2), (1, 3, 3, 3), (0, 2, 3, 6, 4, 3, 4),
    (1, 3, 7, 4), (2, 3, 7), (0, 1, 2, 3, 0, 2, 3), (0, 0, 3, 3, 3, 3, 2), (1, 3, 2, 3), (1, 1, 4, 5),
    (0, 3, 1, 4, 4, 2, 4), (2, 1, 4), (1, 3, 5, 4), (2, 3, 5), (1, 1, 5, 5), (0, 3, 1, 5, 4, 2, 4), (2, 1, 5),
    (0, 2, 3, 5, 4, 3, 4), (0, 1, 2, 2, 0, 2, 3), (0, 0, 3, 2, 3, 3, 2), (1, 1, 1, 5), (2, 1, 1),
    (0, 2, 3, 7, 4, 3, 4), (1, 3, 4, 4), (2, 3, 4), (0, 1, 3, 0, 1, 3, 2), (0, 0, 2, 3, 0, 2, 1),
    (0, 2, 3, 4, 4, 3, 4), (1, 1, 0, 5), (1, 0, 3, 5), (2, 0, 3), (2, 1, 0), (0, 0, 2, 1, 0, 2, 1),
    (0, 1, 0, 1, 1, 0, 2), (1, 2, 4, 4), (2, 2, 4), (1, 2, 3, 3), (1, 3, 3, 5), (2, 3, 3), (0, 0, 2, 3, 3, 2, 2),
    (0, 1, 1, 2, 0, 1, 3), (0, 2, 2, 4, 4, 2, 4), (1, 2, 5, 4), (2, 2, 5), (1, 2, 2, 3), (1, 3, 2, 5), (2, 3, 2),
    (0, 0, 2, 0, 0, 2, 1), (0, 1, 0, 0, 1, 0, 2), (0, 2, 2, 5, 4, 2, 4), (1, 3, 0, 5), (2, 3, 0),
    (0, 0, 2, 2, 0, 2, 1), (0, 1, 3, 1, 1, 3, 2), (0, 2, 1, 6, 4, 1, 4), (1, 2, 1, 1), (1, 0, 1, 5), (2, 0, 1),
    (0, 0, 0, 2, 3, 0, 2), (0, 1, 2, 1, 1, 2, 2), (0, 2, 1, 4, 4, 1, 4), (1, 2, 3, 5), (2, 2, 3), (1, 1, 2, 3),
    (0, 0, 1, 2, 3, 1, 2), (0, 1, 2, 0, 0, 2, 3), (1, 2, 0, 1), (0, 2, 1, 5, 4, 1, 4), (1, 0, 0, 5), (2, 0, 0),
    (0, 0, 2, 2, 3, 2, 2), (0, 1, 2, 0, 1, 2, 2), (1, 3, 1, 5), (2, 3, 1), (1, 0, 2, 5), (1, 2, 1, 5), (2, 2, 1),
    (2, 0, 2), (1, 1, 2, 5), (2, 1, 2), (1, 2, 2, 5), (1, 2, 0, 5), (2, 2, 0), (2, 2, 2),
))
GROUPS = ((0, 0, 0, 0, 0, 0, 0, 0, 0, 0, 0, 0, 0, 0, 0, 0, 0, 0, 0, 0, 0, 0, 0, 0, 0, 0, 0, 0, 0, 0, 0, 0, 0, 0, 0, 0, 0, 0, 0, 0, 0, 0, 0, 0, 0, 0, 0, 0, 0, 0, 0, 0, 0, 0, 0, 0, 0, 0, 0, 0, 0, 0, 0, 0, 0, 0, 0, 1), (0, 0, 0, 0, 0, 0, 0, 0, 0, 0, 0, 0, 0, 0, 0, 0, 0, 0, 0, 0, 0, 0, 0, 0, 0, 0, 0, 0, 0, 0, 0, 0, 0, 0, 0, 0, 0, 0, 0, 0, 0, 0, 0, 0, 0, 0, 0, 0, 0, 0, 0, 0, 0, 0, 0, 0, 0, 0, 0, 0, 0, 0, 0, 0, 0, 0, 0, 0, 0, 0, 0, 0, 0, 0, 0, 0, 0, 0, 1, 1, 1, 1, 1, 1, 1, 1, 1, 1, 1, 1, 1, 1, 1, 1, 1, 1, 1, 1, 1, 1))
SHAPES = (((15, 49), (13, 1)), ((14, 63), (10, 29)))
ARRIVALS = tuple(tuple(op[1:] for op in order if op[0] == 1) for order in ORDERS)
ARRIVAL_SEMS = ((0, 1, 2, 3, 4, 5, 6, 7, 8, 9, 10, 11, 12, 13, 14, 15, 16, 17, 18, 19, 20, 21, 22, 23, 24, 25, 0, 26, 3, 27, 1, 7, 2, 5, 12, 28, 19, 8, 16, 10, 13, 6, 23, 17, 18, 25, 24, 9, 20, 15, 4, 22, 0, 21, 27, 3, 14, 29, 30, 11, 31, 32, 26, 33), (0, 1, 2, 3, 4, 5, 6, 7, 8, 9, 10, 11, 12, 13, 14, 15, 16, 17, 18, 19, 20, 21, 22, 23, 24, 25, 26, 4, 1, 8, 5, 6, 11, 10, 3, 12, 14, 13, 27, 16, 28, 29, 20, 30, 31, 26, 24, 17, 1, 4, 9, 7, 23, 32, 21, 25, 22, 33, 2, 0, 34, 19, 18, 15))


def passed_along(block, axis, distance):
    devices = range(lax.axis_size(axis))
    route = [((i - distance) % len(devices), i) for i in devices]
    return lax.ppermute(block, axis, route)


def masked_weight(weight, mask):
    row_blocks, col_blocks = mask.shape
    shaped = weight.reshape(
        row_blocks, weight.shape[0] // row_blocks, col_blocks, weight.shape[1] // col_blocks
    )
    return (shaped * mask.astype(jnp.bfloat16)[:, None, :, None]).reshape(weight.shape)


def project(token_rows, weight):
    return lax.dot_general(
        token_rows, weight, (((1,), (1,)), ((), ())), preferred_element_type=jnp.float32
    )


def gated_block(token_rows, gate_part, up_part):
    gate = project(token_rows, gate_part)
    up_values = project(token_rows, up_part)
    return (jax.nn.silu(gate) * up_values).astype(jnp.bfloat16)


def collect_panels(stacked):
    panel_count = lax.axis_size("panel")
    collected = [(stacked, 0)]
    moving = stacked
    for distance in range(1, panel_count):
        moving = passed_along(moving, "panel", 1)
        collected.append((moving, distance))
    return collected


def general_shards(tokens, gate_weight, up_weight, gate_mask, up_mask):
    panel_count = lax.axis_size("panel")
    my_panel = lax.axis_index("panel")
    width_rows = gate_weight.shape[0]
    stacked = jnp.stack([masked_weight(gate_weight, gate_mask), masked_weight(up_weight, up_mask)])
    collected = collect_panels(stacked)
    gathered = lax.all_gather(tokens, "seq", axis=0, tiled=True)
    tile = jnp.zeros((gathered.shape[0], panel_count * width_rows), jnp.bfloat16)
    for pair, distance in collected:
        source = (my_panel - distance) % panel_count
        result = gated_block(gathered, pair[0], pair[1])
        tile = lax.dynamic_update_slice_in_dim(tile, result, source * width_rows, 1)
    return lax.all_to_all(tile, "seq", split_axis=0, concat_axis=1, tiled=True)


def kernel(
    tok, gw, uw, gm, um, out,
    held, w, turned, masks, wide, hid,
    total, recv_sem, send_sem, part_send, part_recv, local_sem, out_send, out_recv, out_local,
):
    rows, width = tok.shape
    wrows = gw.shape[0]
    seq, panel = lax.axis_index("seq"), lax.axis_index("panel")
    z, x = seq // 2, seq % 2
    y, core = panel // 2, panel % 2

    def device(bz, bx, by):
        return (bz * 2 + bx, by * 2 + core)

    low = z < NZ // 2
    toward = jnp.where(low, 1, -1)
    at_end = jnp.logical_or(z == 0, z == NZ - 1)

    def plane_z(p):
        return jnp.where(low, p, NZ - 1 - p)

    xdev, ydev = device(z, 1 - x, y), device(z, x, 1 - y)
    inward, outward = device(z + toward, x, y), device(z - toward, x, y)
    partner = (seq, y * 2 + 1 - core)

    barrier = pltpu.get_barrier_semaphore()
    for dev in (xdev, ydev, partner, inward):
        pl.semaphore_signal(barrier, inc=1, device_id=dev, device_id_type=MESH)

    @pl.when(jnp.logical_not(at_end))
    def _():
        pl.semaphore_signal(barrier, inc=1, device_id=outward, device_id_type=MESH)

    def slot(p, b):
        return pl.ds((p * 4 + b) * rows, rows) if b < 4 else pl.ds(p * 4 * rows, 4 * rows)

    own = pl.ds(pl.multiple_of(core * wrows, wrows), wrows)
    own_up = pl.ds(pl.multiple_of((2 + core) * wrows, wrows), wrows)
    weight_parts = (
        (gw, w.at[own]), (uw, w.at[own_up]), (gm, masks.at[core]), (um, masks.at[2 + core]),
    )
    keep_tokens = [
        pltpu.make_async_copy(tok, held.at[slot(q, 0)], local_sem.at[2]) for q in range(2)
    ]
    when_q = (at_end, jnp.logical_not(at_end))
    for q in range(2):
        pl.when(when_q[q])(keep_tokens[q].start)
    pl.semaphore_wait(barrier, jnp.where(at_end, 4, 5))
    pltpu.make_async_copy(tok, held.at[slot(0, 0)], local_sem.at[2]).wait()

    unit = width // 64

    def cols(k):
        return pl.ds(PIECES[k][0] * unit, PIECES[k][1] * unit)

    def arrival(q, p, k, b):
        last_hop = b in ((1, 2), (2, 3))[PIECES[k][2]]
        return ARRIVAL_SEMS[q][ARRIVALS[q].index((p, k, 5 if last_hop else b))]

    half = 2 * wrows

    def out_cols(bz, bx, by):
        block = (bz * 2 + bx) * 2 + by
        return pl.ds(pl.multiple_of(block * half, half), half)

    def relative(b):
        return (x + (b in (1, 2))) % 2, (y + (b in (2, 3))) % 2

    swaps = [
        pltpu.make_async_remote_copy(
            src_ref=src, dst_ref=dst, send_sem=part_send.at[i // 2], recv_sem=part_recv.at[i // 2],
            device_id=partner, device_id_type=MESH,
        )
        for i, (src, dst) in enumerate(weight_parts)
    ]

    def prune(i, state):
        if i == 0:
            for j, ref in enumerate((w.at[pl.ds(0, half)], masks.at[pl.ds(0, 2)])):
                for sem in (local_sem, part_send, part_recv):
                    pltpu.make_async_copy(ref, ref, sem.at[j]).wait()
            row = lax.broadcasted_iota(jnp.int32, (8, masks.shape[2]), 0)
            table = jnp.zeros((8, masks.shape[2]), jnp.float32)
            for r in range(4):
                table = jnp.where(row == r, masks[r].astype(jnp.float32), table)
            state["table"] = table.astype(jnp.bfloat16)
        step = width // PRUNES
        block = width // masks.shape[2]
        start = i * step
        where_ = lax.broadcasted_iota(jnp.int32, (masks.shape[2], step), 0)
        col = lax.broadcasted_iota(jnp.int32, (masks.shape[2], step), 1) + start
        first = where_ * block
        inside = jnp.logical_and(col >= first, col < first + block)
        select = jnp.where(inside, 1.0, 0.0).astype(jnp.bfloat16)
        wide[...] = jnp.dot(state["table"], select, preferred_element_type=jnp.float32)
        kept = []
        for r in range(4):
            keep = jnp.broadcast_to(wide[r:r + 1, :], (wrows, step))
            part = w[pl.ds(r * wrows, wrows), pl.ds(start, step)].astype(jnp.float32)
            kept.append((part * keep).astype(jnp.bfloat16))
        turned[pl.ds(start, step), :] = jnp.concatenate(kept, axis=0).T

    def program(q, table):
        links = (xdev, ydev, inward if q == 0 else outward, inward)
        sends, state = [], {}

        def finish(p, both):
            gate = both[:, :half]
            hid[slot(p, 4), :] = (gate / (1.0 + jnp.exp(-gate)) * both[:, half:]).astype(jnp.bfloat16)
            for b in (2, 1, 3, 0):
                if (p, b) == (q, 0):
                    state["kept_out"] = pltpu.make_async_copy(
                        hid.at[slot(p, 0)], out.at[:, out_cols(z, x, y)], out_local
                    )
                    state["kept_out"].start()
                    continue
                tx, ty = relative(b)
                pltpu.make_async_remote_copy(
                    src_ref=hid.at[slot(p, b)], dst_ref=out.at[:, out_cols(z, x, y)],
                    send_sem=out_send, recv_sem=out_recv,
                    device_id=device(plane_z(p), tx, ty), device_id_type=MESH,
                ).start()

        def multiply(p, k):
            at = slot(p, 4)
            both = jnp.dot(held[at, cols(k)], turned[cols(k), :], preferred_element_type=jnp.float32)
            done = state.get(p, 0)
            if done:
                both = both + total[at, :]
            state[p] = done + 1
            if done + 1 < len(PIECES):
                total[at, :] = both
            else:
                finish(p, both)

        for op in table:
            if op[0] == 0:
                _, link, p, k, src, p2, dst = op
                q2 = 1 - q if link == 2 else q
                source = held.at[slot(p, src), cols(k)]
                copy = pltpu.make_async_remote_copy(
                    src_ref=source, dst_ref=held.at[slot(p2, dst), cols(k)],
                    send_sem=send_sem.at[GROUPS[q][len(sends)]], recv_sem=recv_sem.at[arrival(q2, p2, k, dst)],
                    device_id=links[link], device_id_type=MESH,
                )
                copy.start()
                sends.append(op)
            elif op[0] == 1:
                _, p, k, b = op
                at = slot(p, b) if b < 5 else pl.ds((p * 4 + 1 + PIECES[k][2]) * rows, 2 * rows)
                ref = held.at[at, cols(k)]
                pltpu.make_async_copy(ref, ref, recv_sem.at[ARRIVAL_SEMS[q][ARRIVALS[q].index((p, k, b))]]).wait()
            elif op[0] == 2:
                multiply(op[1], op[2])
            elif op[0] == 3:
                prune(op[1], state)
            else:
                for copy in swaps:
                    copy.start()
                for i, (src, dst) in enumerate(weight_parts):
                    pltpu.make_async_copy(src, dst, local_sem.at[i // 2]).start()
        for group, (high, wide_) in enumerate(SHAPES[q]):
            ref = held.at[pl.ds(0, high * rows), pl.ds(0, wide_ * unit)]
            pltpu.make_async_copy(ref, ref, send_sem.at[group]).wait()
        others = 4 * NZ - 1
        ref = hid.at[pl.ds(0, others * rows)]
        pltpu.make_async_copy(ref, ref, out_send).wait()
        state["kept_out"].wait()
        ref = out.at[:, pl.ds(0, others * half)]
        pltpu.make_async_copy(ref, ref, out_recv).wait()

    for q in range(2):
        pl.when(when_q[q])(functools.partial(program, q, ORDERS[q]))


def shards(tokens, gate_weight, up_weight, gate_mask, up_mask):
    rows, width = tokens.shape
    wrows = gate_weight.shape[0]
    blocks = lax.axis_size("seq") * lax.axis_size("panel") // 2
    hidden = lax.axis_size("seq") * lax.axis_size("panel") * wrows
    dma = pltpu.SemaphoreType.DMA
    return pl.pallas_call(
        kernel,
        out_shape=pltpu.VMEM((rows, hidden), jnp.bfloat16),
        in_specs=[pl.BlockSpec(memory_space=pl.ANY)] * 5,
        out_specs=pl.BlockSpec(memory_space=pltpu.VMEM),
        scratch_shapes=[
            pltpu.VMEM((blocks * rows, width), jnp.bfloat16),
            pltpu.VMEM((4 * wrows, width), jnp.bfloat16),
            pltpu.VMEM((width, 4 * wrows), jnp.bfloat16),
            pltpu.VMEM((4, 1, gate_mask.shape[1]), jnp.int32),
            pltpu.VMEM((8, width // PRUNES), jnp.float32),
            pltpu.VMEM((blocks * rows, 2 * wrows), jnp.bfloat16),
            pltpu.VMEM((blocks * rows, 4 * wrows), jnp.float32),
            dma((1 + max(map(max, ARRIVAL_SEMS)),)), dma((max(map(len, SHAPES)),)),
            dma((2,)), dma((2,)), dma((3,)), dma, dma, dma,
        ],
        compiler_params=pltpu.CompilerParams(collective_id=0, has_side_effects=True),
    )(tokens, gate_weight, up_weight, gate_mask, up_mask)


def solution(mesh):
    spec = P(("seq", "panel"), None)
    fits = mesh.shape["seq"] == 2 * NZ and mesh.shape["panel"] == 4
    body = shards if fits else general_shards
    return jax.shard_map(
        body, mesh=mesh, in_specs=(spec,) * 5, out_specs=spec, check_vma=False
    )
```
